32 devices in a mesh: seq: 4 (over x, core), shard: 8 (over z, y).
Axes of the slice: x: 2, y: 2, z: 4, core: 2. Of those that a mesh axis runs over, the one named last changes fastest.
Arguments:
- inputs: bfloat16 [8, 2048, 1024], P('shard', 'seq'), may hold values from -6 to 6
- attn_gain: bfloat16 [1024], P('shard'), may hold values from 0.5 to 1.5
- qkv_weight: bfloat16 [3, 1024, 1024], P(None, 'shard'), may hold values from -0.1875 to 0.1875
- out_weight: bfloat16 [1024, 1024], P('shard'), may hold values from -6 to 6
- mlp_gain: bfloat16 [1024], P('shard'), may hold values from 0.5 to 1.5
- in_weight: bfloat16 [1024, 5248], P('shard'), may hold values from -0.1875 to 0.1875
- mlp_out: bfloat16 [2624, 1024], P(None, 'shard'), may hold values from -0.125 to 0.125
- cotangent: bfloat16 [8, 2048, 1024], P('shard', 'seq'), may hold values from -6 to 6
Outputs:
- result: bfloat16 [8, 2048, 1024], P('shard', 'seq')
- input_grad: float32 [8, 2048, 1024], P('shard', 'seq')
- attn_gain_grad: float32 [1024], P(('seq', 'shard'))
- qkv_grad: float32 [3, 1024, 1024], P(None, 'shard', 'seq')
- out_grad: float32 [1024, 1024], P('seq', 'shard')
- mlp_gain_grad: float32 [1024], P(('seq', 'shard'))
- in_grad: float32 [1024, 5248], P('shard', 'seq')
- mlp_out_grad: float32 [2624, 1024], P('seq', 'shard')
The draws below stay inside these ranges and needn't reach their ends.
All inputs are finite; a program needn't handle non-finite values.
Results may differ from the reference program's by a relative error of at most 0.017.
Values may be sent and summed in bfloat16 or wider, within the bound.
No kernel may reach another device: no remote copies, remote signals or barrier semaphores. Data moves between devices by JAX's collectives and lax.ppermute only.
A program may use at most 192 MiB of HBM per device.

```python
import math
import jax
import jax.numpy as jnp
from jax import lax

D = 1024
HEADS = 16
HD = 64
FF = 2624
SEQ_LEN = 2048
SEQS_ALL = 8


def spiked(array, key, source, target, shards_of, factor):
    owner, partner = [(jnp.arange(array.shape[dim]) // (array.shape[dim] // shards_of)).reshape([-1 if axis == dim else 1 for axis in range(array.ndim)]) for dim in (source, target)]
    chosen = jax.random.permutation(key, shards_of)[partner]
    strong = (owner == chosen) | (owner == (partner + shards_of // 2) % shards_of)
    return jnp.where(strong, factor * array, array)


def block_levels(own_key, shape, split, least, high):
    level, own = 1.0, jax.random.fold_in(own_key, 6)
    for position, shards_of in split:
        draws = jnp.exp(jax.random.uniform(jax.random.fold_in(own, position), (shards_of,), jnp.float32, least / len(split), high / len(split)))
        level = level * jnp.repeat(draws, shape[position] // shards_of).reshape([-1 if axis == position else 1 for axis in range(len(shape))])
    return level


def scatter_about(key, extent, deviation, bound, pieces=(), kind=jnp.bfloat16):
    array = jax.random.normal(key, extent, jnp.float32) * deviation
    if len(pieces) > 0:
        array = block_levels(key, extent, pieces, -0.22, 0.18) * array
    return jnp.clip(array, min=-bound, max=bound).astype(kind)


def gaussian_with(key, extent, deviation, reach, shards, heavy, held_as=jnp.bfloat16):
    array = deviation * jax.random.normal(key, extent, jnp.float32)
    if shards:
        array = array * block_levels(key, extent, shards, -0.22, 0.18)
    return jnp.clip(spiked(array, jax.random.fold_in(key, 3), *heavy), -reach, reach).astype(held_as)


def setup_inputs(seed: int = 0) -> dict:
    splits = jax.random.split(jax.random.key(seed), 9)
    inputs = gaussian_with(splits[0], (SEQS_ALL, SEQ_LEN, D), 1.0, 6.0, ((0, 8), (1, 4)), (0, 2, 8, 2.0))
    attn_gain = jnp.clip(1.0 + 0.1 * jax.random.normal(splits[1], (D,), jnp.float32), 0.5, 1.5).astype(jnp.bfloat16)
    qkv_weight = scatter_about(splits[2], (3, D, D), D ** -0.5, 0.1875, ((1, 8),))
    out_weight = scatter_about(splits[3], (D, D), (max(1, D * 8 // (3 * SEQ_LEN))) ** -0.5, 6.0, ((0, 8),))
    mlp_gain = jnp.clip(1.0 + 0.1 * jax.random.normal(splits[4], (D,), jnp.float32), 0.5, 1.5).astype(jnp.bfloat16)
    in_weight = scatter_about(splits[5], (D, 2 * FF), D ** -0.5, 0.1875, ((0, 8),))
    mlp_out = scatter_about(splits[6], (FF, D), FF ** -0.5, 0.125, ((1, 8),))
    cotangent = gaussian_with(splits[7], (SEQS_ALL, SEQ_LEN, D), 1.0, 6.0, ((0, 8), (1, 4)), (0, 2, 8, 2.0))
    return dict(inputs=inputs, attn_gain=attn_gain, qkv_weight=qkv_weight, out_weight=out_weight, mlp_gain=mlp_gain, in_weight=in_weight, mlp_out=mlp_out, cotangent=cotangent)


epsilon = 1e-05
rope_base = 160000.0
query_block = 512

@jax.custom_vjp
def low(v):
    return lax.optimization_barrier(v.astype(jnp.bfloat16)).astype(jnp.float32)

@jax.custom_vjp
def low_back(v):
    return v

def low_keep(v):
    return (low(v), None)

def low_pass(kept, grad):
    return (grad,)

def back_keep(v):
    return (v, None)

def back_low(kept, grad):
    return (low(grad),)
low.defvjp(low_keep, low_pass)
low_back.defvjp(back_keep, back_low)

def product(form, left, right):
    return jnp.einsum(form, left, right, precision=lax.Precision.HIGHEST)

def layer_norm(values, gain_vec):
    center = values - lax.optimization_barrier(jnp.mean(values, axis=-1, keepdims=True))
    inv_scale = lax.rsqrt(lax.optimization_barrier(jnp.mean(center * center, axis=-1, keepdims=True)) + epsilon)
    return center * inv_scale * gain_vec

def rope_tables(positions, head_size):
    frequency = 1.0 / rope_base ** (jnp.arange(0, head_size, 2, dtype=jnp.float32) / head_size)
    angles = positions.astype(jnp.float32)[:, None] * frequency[None, :]
    angles = jnp.concatenate([angles, angles], axis=-1)
    return (jnp.cos(angles)[:, None, :], jnp.sin(angles)[:, None, :])

def rotate(values, cosine_table, sine_table):
    half_size = values.shape[-1] // 2
    turned = jnp.concatenate([-values[..., half_size:], values[..., :half_size]], axis=-1)
    return values * cosine_table + turned * sine_table

def attend(queries, keys_all, values_all):
    group_size = queries.shape[0]
    length_all = queries.shape[1]
    query_rows = min(query_block, length_all)
    score_scale = 1.0 / math.sqrt(HD)
    query_parts = queries.reshape(group_size, length_all // query_rows, query_rows, HEADS, HD)
    query_parts = jnp.moveaxis(query_parts, 1, 0)

    @jax.checkpoint
    def one_block(query_part):
        scores = low_back(score_scale * product('gqhd,gkhd->ghqk', query_part, keys_all))
        row_max = lax.optimization_barrier(jnp.max(scores, axis=-1, keepdims=True))
        exponent = jnp.exp(scores - row_max)
        probs = exponent / lax.optimization_barrier(jnp.sum(exponent, axis=-1, keepdims=True))
        return product('ghqk,gkhd->gqhd', low(probs), values_all)
    context = lax.map(one_block, query_parts)
    return jnp.moveaxis(context, 0, 1).reshape(queries.shape)

def layer_forward(source, attn_scale, qkv_proj, out_proj, mlp_scale, wide_proj, down_proj):
    group_size, length_all, feature_count = source.shape
    first_norm = low(layer_norm(source, attn_scale))
    projected = low_back(product('gld,cde->cgle', first_norm, qkv_proj))
    cosine_table, sine_table = rope_tables(jnp.arange(length_all), HD)

    def split_heads(values):
        return values.reshape(group_size, length_all, HEADS, HD)
    queries = low_back(low(rotate(split_heads(projected[0]), cosine_table, sine_table)))
    keys_all = low_back(low(rotate(split_heads(projected[1]), cosine_table, sine_table)))
    values_all = low(split_heads(projected[2]))
    context = low_back(low(attend(queries, keys_all, values_all)))
    context = context.reshape(group_size, length_all, feature_count)
    after_attn = source + low_back(product('gli,ie->gle', context, out_proj))
    second_norm = low(layer_norm(after_attn, mlp_scale))
    gate_up = low_back(product('gld,df->glf', second_norm, wide_proj))
    hidden = low(jax.nn.gelu(gate_up[..., :FF], approximate=False) * gate_up[..., FF:])
    return after_attn + low_back(product('glf,fe->gle', hidden, down_proj))

def reference(inputs, attn_gain, qkv_weight, out_weight, mlp_gain, in_weight, mlp_out, cotangent):
    weight_set = (attn_gain.astype(jnp.float32), qkv_weight.astype(jnp.float32), out_weight.astype(jnp.float32), mlp_gain.astype(jnp.float32), in_weight.astype(jnp.float32), mlp_out.astype(jnp.float32))
    seq_total = inputs.shape[0]
    group_size = math.gcd(seq_total, max(1, 4096 // SEQ_LEN))
    step_count = seq_total // group_size
    sources = inputs.astype(jnp.float32).reshape(step_count, group_size, SEQ_LEN, D)
    outer_grads = cotangent.astype(jnp.float32).reshape(step_count, group_size, SEQ_LEN, D)

    def one_step(totals, members):
        source, outer_grad = members
        output_value, pull_back = jax.vjp(layer_forward, source, *weight_set)
        grad_list = pull_back(outer_grad)
        totals = tuple((total_item + grad_item for total_item, grad_item in zip(totals, grad_list[1:])))
        return (totals, (output_value.astype(jnp.bfloat16), grad_list[0]))
    empty_grads = tuple((jnp.zeros_like(weight_item) for weight_item in weight_set))
    totals, (outputs, input_grads) = lax.scan(one_step, empty_grads, (sources, outer_grads))
    return (outputs.reshape(inputs.shape), input_grads.reshape(inputs.shape), totals[0], totals[1], totals[2], totals[3], totals[4], totals[5])
```

```python
from functools import partial
import math

import jax
import jax.numpy as jnp
from jax import lax
from jax.experimental import pallas as pl
from jax.experimental.pallas import tpu as pltpu
from jax.sharding import PartitionSpec as P

HEADS = 16
HD = 64
FF = 2624

epsilon = 1e-05
rope_base = 160000.0

f32 = jnp.float32
bf16 = jnp.bfloat16

WIDTH = 1024
HALF = FF // 2
PADDED = 1408
BLOCK = FF // 4
COLS = 256
EXTRA = 16
ROWS_BY_COLS = (((0,), (0,)), ((), ()))
COLS_BY_COLS = (((1,), (1,)), ((), ()))
VMEM_LIMIT = 58 * 1024 * 1024

ANY = pl.BlockSpec(memory_space=pl.ANY)
SMEM = pl.BlockSpec(memory_space=pltpu.SMEM)


def params():
    return pltpu.CompilerParams(vmem_limit_bytes=VMEM_LIMIT)


def sds(shape, dtype=bf16):
    return jax.ShapeDtypeStruct(shape, dtype)


def aligned(index, size):
    return pl.ds(pl.multiple_of(index * size, size), size)


def normalize(values):
    center = values - jnp.mean(values, axis=-1, keepdims=True)
    inv_scale = lax.rsqrt(jnp.mean(center * center, axis=-1, keepdims=True) + epsilon)
    return center * inv_scale, inv_scale


def norm_back(grads, xhat, inv_scale):
    mean_grad = jnp.mean(grads, axis=-1, keepdims=True)
    mean_both = jnp.mean(grads * xhat, axis=-1, keepdims=True)
    return inv_scale * (grads - mean_grad - xhat * mean_both)


def turned(values):
    lane = lax.broadcasted_iota(jnp.int32, values.shape, 1)
    width = values.shape[1]
    return jnp.where(
        lane % HD < HD // 2, pltpu.roll(values, width - HD // 2, 1), pltpu.roll(values, HD // 2, 1)
    )


def twice(table):
    return jnp.concatenate([table, table], axis=1)


def qkv_kernel(count, idx, *refs):
    x_refs, refs = refs[:4], refs[4:]
    w_refs, refs = refs[:count], refs[count:]
    if count == 1:
        gain_ref, refs = refs[0], refs[1:]
    cos_ref, sin_ref, fn_o, q_o, k_o, v_o, w_o, g_o, xs, gs, semx, semw, semg = refs
    step = pl.program_id(0)
    shard = idx[0]
    size = WIDTH // count

    def x_copy(r):
        return pltpu.make_async_copy(x_refs[r], xs.at[r], semx.at[r])

    def w_copy(r):
        return pltpu.make_async_copy(
            w_refs[r].at[pl.ds(0, size)], w_o.at[aligned(jnp.bitwise_xor(shard, r), size)], semw.at[r]
        )

    def g_copy(r):
        return pltpu.make_async_copy(
            w_refs[r].at[pl.ds(size, EXTRA)], gs.at[jnp.bitwise_xor(shard, r)], semg.at[r]
        )

    @pl.when(step == 0)
    def _():
        if count == 1:
            w_all = pltpu.make_async_copy(w_refs[0], w_o, semw.at[0])
            w_all.start()
        else:
            for r in range(count):
                w_copy(r).start()
                g_copy(r).start()
        for r in range(4):
            x_copy(r).start()
        if count == 1:
            w_all.wait()
            g_o[0:1] = gain_ref[0:1].astype(f32)
            g_o[1:2] = gain_ref[1:2].astype(f32)
        else:
            for r in range(count):
                w_copy(r).wait()
                g_copy(r).wait()
            for r in range(count):
                part = gs[r].astype(f32)
                g_o[0:1, r * size : (r + 1) * size] = part[0:1, 0:size]
                g_o[1:2, r * size : (r + 1) * size] = part[0:1, size : 2 * size]

    for r in range(4):

        @pl.when(step == r)
        def _():
            x_copy(r).wait()

    xhat, _ = normalize(xs[step].astype(f32))
    first_low = (xhat * g_o[0:1]).astype(bf16)
    fn_o[...] = first_low
    cosine, sine = twice(cos_ref[...]), twice(sin_ref[...])
    outs = (q_o, k_o, v_o)
    for part in range(3):
        value = jnp.dot(first_low, w_o[:, part * COLS : (part + 1) * COLS], preferred_element_type=f32)
        if part < 2:
            value = value * cosine + turned(value) * sine
        value = value.astype(bf16)
        if part == 0:
            value = value * jnp.asarray(1.0 / math.sqrt(HD), bf16)
        outs[part][...] = value


def qkv_call(count, idx, chunks, pieces, gains, cosine, sine):
    rows = chunks[0].shape[0]
    by_step = lambda width: pl.BlockSpec((rows, width), lambda r: (r, 0))
    whole = lambda shape: pl.BlockSpec(shape, lambda r: (0, 0))
    extra = [] if count > 1 else [gains]
    return pl.pallas_call(
        partial(qkv_kernel, count),
        grid=(4,),
        in_specs=[SMEM]
        + [ANY] * (4 + count)
        + ([] if count > 1 else [whole((2, WIDTH))])
        + [by_step(128), by_step(128)],
        out_specs=[
            by_step(WIDTH),
            by_step(COLS),
            by_step(COLS),
            by_step(COLS),
            whole((WIDTH, 3 * COLS)),
            whole((8, WIDTH)),
        ],
        out_shape=[
            sds((4 * rows, WIDTH)),
            sds((4 * rows, COLS)),
            sds((4 * rows, COLS)),
            sds((4 * rows, COLS)),
            sds((WIDTH, 3 * COLS)),
            sds((8, WIDTH), f32),
        ],
        scratch_shapes=[
            pltpu.VMEM((4, rows, WIDTH), bf16),
            pltpu.VMEM((8, EXTRA, 3 * COLS), bf16),
            pltpu.SemaphoreType.DMA((4,)),
            pltpu.SemaphoreType.DMA((count,)),
            pltpu.SemaphoreType.DMA((count,)),
        ],
        compiler_params=params(),
        name="project",
    )(idx, *chunks, *pieces, *extra, cosine, sine)


def head_of(shape):
    return lax.broadcasted_iota(jnp.int32, shape, len(shape) - 1) // HD


def attend_kernel(q_ref, k_ref, v_ref, o_ref, lse_ref):
    q, k, v = q_ref[...], k_ref[...], v_ref[...]
    heads = head_of(q.shape)
    total = jnp.zeros(q.shape, f32)
    lses = jnp.zeros((q.shape[0], 128), f32)
    lane = lax.broadcasted_iota(jnp.int32, lses.shape, 1)
    for h in range(COLS // HD):
        q_h = jnp.where(heads == h, q, jnp.zeros_like(q))
        scores = lax.dot_general(q_h, k, COLS_BY_COLS, preferred_element_type=f32)
        row_max = jnp.max(scores, axis=1, keepdims=True)
        exponent = jnp.exp(scores - row_max)
        row_total = jnp.sum(exponent, axis=1, keepdims=True)
        context = jnp.dot(exponent.astype(bf16), v, preferred_element_type=f32)
        total = jnp.where(heads == h, context * (1.0 / row_total), total)
        lses = jnp.where(lane == h, row_max + jnp.log(row_total), lses)
    o_ref[...] = total.astype(bf16)
    lse_ref[...] = lses.T[:8]


def attend(q, k, v, part, tile=512):
    span = k.shape[0]
    rows = span // 2
    steps = rows // tile
    kept = pl.BlockSpec((span, COLS), lambda i: (0, 0))
    return pl.pallas_call(
        attend_kernel,
        grid=(steps,),
        in_specs=[pl.BlockSpec((tile, COLS), lambda i: (i + part * steps, 0)), kept, kept],
        out_specs=[
            pl.BlockSpec((tile, COLS), lambda i: (i, 0)),
            pl.BlockSpec((8, tile), lambda i: (0, i)),
        ],
        out_shape=[sds((rows, COLS)), sds((8, rows), f32)],
        compiler_params=params(),
        name="attend",
    )(q, k, v)


def attend_back_kernel(last, *refs):
    q_ref, do_ref, o_ref, lse_ref, k_ref, v_ref, qcos, qsin, refs = *refs[:8], refs[8:]
    if last:
        dk_i, dv_i, kcos, ksin, refs = *refs[:4], refs[4:]
    dq_ref, dk_ref, dv_ref, do_s, inner_s, dq_s = refs
    step = pl.program_id(0)
    n_heads = COLS // HD

    @pl.when(step == 0)
    def _():
        do = do_ref[...]
        product = do.astype(f32) * o_ref[...].astype(f32)
        high = product.astype(bf16)
        rest = (product - high.astype(f32)).astype(bf16)
        chosen = (
            head_of((8, COLS)) == lax.broadcasted_iota(jnp.int32, (8, COLS), 0)
        ).astype(bf16)
        inner_s[...] = lax.dot_general(
            chosen, high, COLS_BY_COLS, preferred_element_type=f32
        ) + lax.dot_general(chosen, rest, COLS_BY_COLS, preferred_element_type=f32)
        heads = head_of(do.shape)
        for h in range(n_heads):
            do_s[h] = jnp.where(heads == h, do, jnp.zeros_like(do))
        dq_s[...] = jnp.zeros_like(dq_s)

    q, k, v = q_ref[...], k_ref[...], v_ref[...]
    heads = head_of(k.shape)
    dk = jnp.zeros(k.shape, f32)
    dv = jnp.zeros(k.shape, f32)
    dq = dq_s[...]
    for h in range(n_heads):
        k_h = jnp.where(heads == h, k, jnp.zeros_like(k))
        scores = lax.dot_general(k_h, q, COLS_BY_COLS, preferred_element_type=f32)
        probs = jnp.exp(scores - lse_ref[h : h + 1, :])
        probs_grad = lax.dot_general(v, do_s[h], COLS_BY_COLS, preferred_element_type=f32)
        scores_grad = (probs * (probs_grad - inner_s[h : h + 1, :])).astype(bf16)
        dv = dv + jnp.dot(probs.astype(bf16), do_s[h], preferred_element_type=f32)
        dk = jnp.where(heads == h, jnp.dot(scores_grad, q, preferred_element_type=f32), dk)
        dq = dq + lax.dot_general(scores_grad, k_h, ROWS_BY_COLS, preferred_element_type=f32)
    dq_s[...] = dq
    if last:
        dk = dk + dk_i[...]
        dv = dv + dv_i[...]
        dk_ref[...] = (dk * twice(kcos[...]) - turned(dk) * twice(ksin[...])).astype(bf16)
        dv_ref[...] = dv.astype(bf16)
    else:
        dk_ref[...] = dk
        dv_ref[...] = dv

    @pl.when(step == pl.num_programs(0) - 1)
    def _():
        dq = dq_s[...] * (1.0 / math.sqrt(HD))
        dq_ref[...] = (dq * twice(qcos[...]) - turned(dq) * twice(qsin[...])).astype(bf16)


def attend_back(part, q, do, o, lse, k, v, cosine, sine, earlier=None, tile=512):
    span = k.shape[0]
    rows = do.shape[0]
    last = earlier is not None
    rows_at = lambda at, width: pl.BlockSpec((rows, width), lambda i: (at, 0))
    keys = lambda width: pl.BlockSpec((tile, width), lambda i: (i, 0))
    grads = bf16 if last else f32
    return pl.pallas_call(
        partial(attend_back_kernel, last),
        grid=(span // tile,),
        in_specs=[
            rows_at(part, COLS),
            rows_at(0, COLS),
            rows_at(0, COLS),
            pl.BlockSpec((8, rows), lambda i: (0, 0)),
            keys(COLS),
            keys(COLS),
            rows_at(part, 128),
            rows_at(part, 128),
        ]
        + ([keys(COLS), keys(COLS), keys(128), keys(128)] if last else []),
        out_specs=[rows_at(0, COLS), keys(COLS), keys(COLS)],
        out_shape=[sds((rows, COLS)), sds((span, COLS), grads), sds((span, COLS), grads)],
        scratch_shapes=[
            pltpu.VMEM((COLS // HD, rows, COLS), bf16),
            pltpu.VMEM((8, rows), f32),
            pltpu.VMEM((rows, COLS), f32),
        ],
        compiler_params=params(),
        name="attend_back",
    )(q, do, o, lse, k, v, cosine, sine, *((*earlier, cosine, sine) if last else ()))


def fetch_rows(count, shard, piece_refs, target, sem):
    size = target.shape[0] // count
    copies = []
    for r in range(count):
        place = aligned(jnp.bitwise_xor(shard, r), size) if count > 1 else pl.ds(0, size)
        copies.append(pltpu.make_async_copy(piece_refs[r], target.at[place], sem.at[r]))
    return copies


def out_kernel(count, idx, mine_ref, other_ref, *refs):
    w_refs, (o_ref, wsel_ref, w_s, sem) = refs[:count], refs[count:]
    copies = fetch_rows(count, idx[0], w_refs, w_s, sem)
    for copy in copies:
        copy.start()
    for copy in copies:
        copy.wait()
    seq = idx[1]
    wsel_ref[0:COLS] = w_s[aligned(seq, COLS)]
    wsel_ref[COLS:] = w_s[aligned(jnp.bitwise_xor(seq, 2), COLS)]
    value = jnp.dot(mine_ref[...], wsel_ref[0:COLS], preferred_element_type=f32)
    value = value + jnp.dot(other_ref[...], wsel_ref[COLS:], preferred_element_type=f32)
    o_ref[...] = value.astype(bf16)


def out_call(count, idx, mine, other, pieces):
    vmem = pl.BlockSpec(memory_space=pltpu.VMEM)
    return pl.pallas_call(
        partial(out_kernel, count),
        in_specs=[SMEM, vmem, vmem] + [ANY] * count,
        out_specs=[vmem, vmem],
        out_shape=[sds((mine.shape[0], WIDTH)), sds((2 * COLS, WIDTH))],
        scratch_shapes=[pltpu.VMEM((WIDTH, WIDTH), bf16), pltpu.SemaphoreType.DMA((count,))],
        compiler_params=params(),
        name="out_project",
    )(idx, mine, other, *pieces)


def mlp_kernel(count, idx, *refs):
    x0, x1, po, pr, c0, c1, g_ref, refs = *refs[:7], refs[7:]
    win_refs, wd_refs, refs = refs[:count], refs[count : 2 * count], refs[2 * count :]
    sn_o, hid_o, gug_o, sgp_o, wd_o, refs = *refs[:5], refs[5:]
    xs, pos, prs, cs, wi, wd, sn_s, hid_s, gug_s, sgp_s, sem_a, sem_i, sem_d, sem_o = refs
    shard = idx[0]
    rows = xs.shape[1]
    loads = [
        pltpu.make_async_copy(x0, xs.at[0], sem_a.at[0]),
        pltpu.make_async_copy(x1, xs.at[1], sem_a.at[1]),
        pltpu.make_async_copy(po, pos, sem_a.at[2]),
        pltpu.make_async_copy(pr, prs, sem_a.at[3]),
        pltpu.make_async_copy(c0, cs.at[pl.ds(0, rows)], sem_a.at[4]),
        pltpu.make_async_copy(c1, cs.at[pl.ds(rows, rows)], sem_a.at[5]),
    ]
    wi_loads = fetch_rows(count, shard, win_refs, wi, sem_i)
    wd_loads = []
    width = WIDTH // count
    for r in range(count):
        place = aligned(jnp.bitwise_xor(shard, r), width) if count > 1 else pl.ds(0, width)
        wd_loads.append(
            pltpu.make_async_copy(wd_refs[r], wd.at[pl.ds(0, HALF), place], sem_d.at[r])
        )
    for copy in loads[:4] + wi_loads + loads[4:] + wd_loads:
        copy.start()
    wd[HALF:] = jnp.zeros((PADDED - HALF, WIDTH), bf16)
    for copy in loads[:4]:
        copy.wait()
    for r in range(2):
        here, there = pl.ds(r * rows, rows), pl.ds((1 - r) * rows, rows)
        after = xs[r].astype(f32) + pos[here].astype(f32) + prs[there].astype(f32)
        xhat, _ = normalize(after)
        sn_s[here] = (xhat * g_ref[1:2]).astype(bf16)
    stores = []

    def store(source, target, k):
        copy = pltpu.make_async_copy(source, target, sem_o.at[k])
        copy.start()
        stores.append(copy)

    store(sn_s, sn_o, 0)
    for copy in wi_loads + loads[4:] + wd_loads:
        copy.wait()
    store(wd, wd_o, 1)
    start = 0
    while start < PADDED:
        size = min(256, PADDED - start)
        here = pl.ds(start, size)
        gate = jnp.dot(sn_s[...], wi[:, here], preferred_element_type=f32)
        up = jnp.dot(sn_s[...], wi[:, pl.ds(PADDED + start, size)], preferred_element_type=f32)
        back = lax.dot_general(cs[...], wd[here], COLS_BY_COLS, preferred_element_type=f32)
        below = 0.5 * (1.0 + lax.erf(gate * math.sqrt(0.5)))
        density = jnp.exp(-0.5 * gate * gate) * (1.0 / math.sqrt(2.0 * math.pi))
        unit = gate * below
        hid_s[:, here] = (unit * up).astype(bf16)
        gug_s[0, :, here] = (back * up * (below + gate * density)).astype(bf16)
        gug_s[1, :, here] = (back * unit).astype(bf16)
        start += size
    store(hid_s, hid_o, 2)
    store(gug_s, gug_o, 3)
    value = lax.dot_general(gug_s[0], wi[:, :PADDED], COLS_BY_COLS, preferred_element_type=f32)
    value = value + lax.dot_general(gug_s[1], wi[:, PADDED:], COLS_BY_COLS, preferred_element_type=f32)
    sgp_s[...] = value.astype(bf16)
    store(sgp_s, sgp_o, 4)
    for copy in stores:
        copy.wait()


def mlp_call(count, idx, x0, x1, po, pr, c0, c1, gains, win, wd):
    rows = x0.shape[0]
    return pl.pallas_call(
        partial(mlp_kernel, count),
        in_specs=[SMEM] + [ANY] * 6 + [pl.BlockSpec(memory_space=pltpu.VMEM)] + [ANY] * (2 * count),
        out_specs=[ANY] * 5,
        out_shape=[
            sds((2 * rows, WIDTH)),
            sds((2 * rows, PADDED)),
            sds((2, 2 * rows, PADDED)),
            sds((2 * rows, WIDTH)),
            sds((PADDED, WIDTH)),
        ],
        scratch_shapes=[
            pltpu.VMEM((2, rows, WIDTH), bf16),
            pltpu.VMEM((2 * rows, WIDTH), bf16),
            pltpu.VMEM((2 * rows, WIDTH), bf16),
            pltpu.VMEM((2 * rows, WIDTH), bf16),
            pltpu.VMEM((WIDTH, 2 * PADDED), bf16),
            pltpu.VMEM((PADDED, WIDTH), bf16),
            pltpu.VMEM((2 * rows, WIDTH), bf16),
            pltpu.VMEM((2 * rows, PADDED), bf16),
            pltpu.VMEM((2, 2 * rows, PADDED), bf16),
            pltpu.VMEM((2 * rows, WIDTH), bf16),
            pltpu.SemaphoreType.DMA((6,)),
            pltpu.SemaphoreType.DMA((count,)),
            pltpu.SemaphoreType.DMA((count,)),
            pltpu.SemaphoreType.DMA((5,)),
        ],
        compiler_params=params(),
        name="feed_forward",
    )(idx, x0, x1, po, pr, c0, c1, gains, *win, *wd)


def down_kernel(count, idx, hid_ref, wd_ref, c0, c1, other_o, mine_o, keep_o, send_o, acc):
    shard, x_place = idx[0], idx[2]
    rows = c0.shape[0]
    for r, target in ((1, other_o), (0, mine_o)):
        target[...] = jnp.dot(
            hid_ref[r * rows : (r + 1) * rows], wd_ref[...], preferred_element_type=f32
        ).astype(bf16)
    acc[...] = lax.dot_general(
        hid_ref[0:rows], c0[...], ROWS_BY_COLS, preferred_element_type=f32
    ) + lax.dot_general(hid_ref[rows:], c1[...], ROWS_BY_COLS, preferred_element_type=f32)
    width = WIDTH // count
    for part, target in ((1, send_o), (0, keep_o)):
        here = pl.ds(pl.multiple_of(jnp.bitwise_xor(x_place, part) * BLOCK, 8), BLOCK)
        for r in range(count):
            place = aligned(jnp.bitwise_xor(shard, r), width) if count > 1 else pl.ds(0, width)
            target[r] = acc[here, place].astype(bf16)


def down_call(count, idx, hidden, wd, c0, c1):
    rows = c0.shape[0]
    vmem = pl.BlockSpec(memory_space=pltpu.VMEM)
    return pl.pallas_call(
        partial(down_kernel, count),
        in_specs=[SMEM] + [vmem] * 4,
        out_specs=[vmem] * 4,
        out_shape=[
            sds((rows, WIDTH)),
            sds((rows, WIDTH)),
            sds((count, BLOCK, WIDTH // count)),
            sds((count, BLOCK, WIDTH // count)),
        ],
        scratch_shapes=[pltpu.VMEM((PADDED, WIDTH), f32)],
        compiler_params=params(),
        name="down_project",
    )(idx, hidden, wd, c0, c1)


def norm_two_kernel(x0, x1, po, pr, so, sr, c0, c1, g_ref, wsel, res_o, low_o, mine_o, other_o, gain_o):
    rows = x0.shape[0]
    gain = g_ref[1:2]
    for r, (x_ref, c_ref) in enumerate(((x0, c0), (x1, c1))):
        here, there = pl.ds(r * rows, rows), pl.ds((1 - r) * rows, rows)
        after = x_ref[...].astype(f32) + po[here].astype(f32) + pr[there].astype(f32)
        xhat, inv_scale = normalize(after)
        second = so[here].astype(f32) + sr[there].astype(f32)
        res = c_ref[...].astype(f32) + norm_back(second * gain, xhat, inv_scale)
        if r == 0:
            res_o[...] = res
            total = jnp.sum(second * xhat, axis=0, keepdims=True)
            gain_o[...] = jnp.broadcast_to(total, gain_o.shape)
        low = res.astype(bf16)
        low_o[here] = low
        value = lax.dot_general(low, wsel[...], COLS_BY_COLS, preferred_element_type=f32).astype(bf16)
        mine_o[here] = value[:, :COLS]
        other_o[here] = value[:, COLS:]


def norm_two_call(x0, x1, po, pr, so, sr, c0, c1, gains, wsel):
    rows = x0.shape[0]
    vmem = pl.BlockSpec(memory_space=pltpu.VMEM)
    return pl.pallas_call(
        norm_two_kernel,
        in_specs=[vmem] * 10,
        out_specs=[vmem] * 5,
        out_shape=[
            sds((rows, WIDTH), f32),
            sds((2 * rows, WIDTH)),
            sds((2 * rows, COLS)),
            sds((2 * rows, COLS)),
            sds((8, WIDTH), f32),
        ],
        compiler_params=params(),
        name="norm_two_back",
    )(x0, x1, po, pr, so, sr, c0, c1, gains, wsel)


def wide_kernel(count, idx, sn_ref, gug_ref, *refs):
    outs, acc = refs[:-1], refs[-1]
    part = pl.program_id(0)
    shard = idx[0]
    acc[...] = lax.dot_general(sn_ref[...], gug_ref[0], ROWS_BY_COLS, preferred_element_type=f32)
    size = WIDTH // count
    for r in range(count):
        place = aligned(jnp.bitwise_xor(shard, r), size) if count > 1 else pl.ds(0, size)
        outs[r % len(outs)][0, r // len(outs)] = acc[place].astype(bf16)


def wide_call(count, idx, sn, gug):
    tokens = sn.shape[0]
    split = 2 if count > 1 else 1
    size = WIDTH // count
    spec = lambda shape, at: pl.BlockSpec(shape, at)
    grid_spec = pltpu.PrefetchScalarGridSpec(
        num_scalar_prefetch=1,
        grid=(2,),
        in_specs=[
            spec((tokens, WIDTH), lambda p, s: (0, 0)),
            spec((1, tokens, PADDED), lambda p, s: (jnp.bitwise_xor(p, s[2]), 0, 0)),
        ],
        out_specs=[spec((1, count // split, size, PADDED), lambda p, s: (p, 0, 0, 0))] * split,
        scratch_shapes=[pltpu.VMEM((WIDTH, PADDED), f32)],
    )
    return pl.pallas_call(
        partial(wide_kernel, count),
        grid_spec=grid_spec,
        out_shape=[sds((2, count // split, size, PADDED))] * split,
        compiler_params=params(),
        name="wide_grad",
    )(idx, sn, gug)


def out_grad_kernel(count, idx, mine, other, low, keep_o, send_o, acc):
    shard = idx[0]
    width = WIDTH // count
    for source, target in ((other, send_o), (mine, keep_o)):
        acc[...] = lax.dot_general(source[...], low[...], ROWS_BY_COLS, preferred_element_type=f32)
        for r in range(count):
            place = aligned(jnp.bitwise_xor(shard, r), width) if count > 1 else pl.ds(0, width)
            target[r] = acc[:, place].astype(bf16)


def out_grad_call(count, idx, mine, other, low):
    vmem = pl.BlockSpec(memory_space=pltpu.VMEM)
    return pl.pallas_call(
        partial(out_grad_kernel, count),
        in_specs=[SMEM] + [vmem] * 3,
        out_specs=[vmem] * 2,
        out_shape=[sds((count, COLS, WIDTH // count))] * 2,
        scratch_shapes=[pltpu.VMEM((COLS, WIDTH), f32)],
        compiler_params=params(),
        name="out_grad",
    )(idx, mine, other, low)


def first_kernel(q_ref, k0, v0, k1, v1, w_ref, far_o, near_o):
    pass


def back_project_kernel(q_ref, k_ref, v_ref, w_ref, o_ref):
    value = lax.dot_general(q_ref[...], w_ref[:, :COLS], COLS_BY_COLS, preferred_element_type=f32)
    value += lax.dot_general(k_ref[...], w_ref[:, COLS : 2 * COLS], COLS_BY_COLS, preferred_element_type=f32)
    value += lax.dot_general(v_ref[...], w_ref[:, 2 * COLS :], COLS_BY_COLS, preferred_element_type=f32)
    o_ref[0] = value.astype(bf16)


def back_project(q_near, q_far, k, v, w, chunk):
    rows = q_near.shape[0] // 2
    outs = []
    at = lambda where: pl.BlockSpec((rows, COLS), lambda i: (where, 0))
    for half, q in ((1, q_far), (0, q_near)):
        where = 2 * half + chunk
        outs.append(
            pl.pallas_call(
                back_project_kernel,
                grid=(1,),
                in_specs=[at(chunk), at(where), at(where), pl.BlockSpec((WIDTH, 3 * COLS), lambda i: (0, 0))],
                out_specs=pl.BlockSpec((1, rows, WIDTH), lambda i: (0, 0, 0)),
                out_shape=sds((1, rows, WIDTH)),
                compiler_params=params(),
                name="back_project",
            )(q, k, v, w)
        )
    return outs


def qkv_grad_kernel(count, idx, fn_ref, qn, qf, k_ref, v_ref, w_ref, g_ref, keep_o, *refs):
    if count > 1:
        send_o, gain_o, acc = refs
    else:
        gain_o, acc = refs
    rows = qn.shape[0]
    near, far = fn_ref[:rows], fn_ref[rows:]
    acc[:, :COLS] = lax.dot_general(
        near, qn[...], ROWS_BY_COLS, preferred_element_type=f32
    ) + lax.dot_general(far, qf[...], ROWS_BY_COLS, preferred_element_type=f32)
    acc[:, COLS : 2 * COLS] = lax.dot_general(
        fn_ref[...], k_ref[...], ROWS_BY_COLS, preferred_element_type=f32
    )
    acc[:, 2 * COLS :] = lax.dot_general(
        fn_ref[...], v_ref[...], ROWS_BY_COLS, preferred_element_type=f32
    )
    shard = idx[0]
    size = WIDTH // count
    for r in range(count):
        place = aligned(jnp.bitwise_xor(shard, r), size) if count > 1 else pl.ds(0, size)
        target = (keep_o, send_o)[r % 2] if count > 1 else keep_o
        target[r // 2 if count > 1 else r] = acc[place].astype(bf16)
    both = acc[...] * w_ref[...].astype(f32)
    high = both.astype(bf16)
    rest = (both - high.astype(f32)).astype(bf16)
    ones = jnp.ones((8, 3 * COLS), bf16)
    total = lax.dot_general(ones, high, COLS_BY_COLS, preferred_element_type=f32)
    total += lax.dot_general(ones, rest, COLS_BY_COLS, preferred_element_type=f32)
    gain_o[...] = total / g_ref[0:1]


def qkv_grad_call(count, idx, first_low, q_near, q_far, k, v, w, gains):
    vmem = pl.BlockSpec(memory_space=pltpu.VMEM)
    split = 2 if count > 1 else 1
    size = WIDTH // count
    return pl.pallas_call(
        partial(qkv_grad_kernel, count),
        in_specs=[SMEM] + [vmem] * 7,
        out_specs=[vmem] * (split + 1),
        out_shape=[sds((count // split, size, 3 * COLS))] * split + [sds((8, WIDTH), f32)],
        scratch_shapes=[pltpu.VMEM((WIDTH, 3 * COLS), f32)],
        compiler_params=params(),
        name="project_grad",
    )(idx, first_low, q_near, q_far, k, v, w, gains)


def norm_one_kernel(x_ref, res_ref, own, core, far, g_ref, o_ref):
    xhat, inv_scale = normalize(x_ref[...].astype(f32))
    first = own[0].astype(f32) + core[0].astype(f32) + far[0].astype(f32)
    o_ref[...] = res_ref[...] + norm_back(first * g_ref[0:1], xhat, inv_scale)


def norm_one_call(x, res, own, core, far, gains):
    vmem = pl.BlockSpec(memory_space=pltpu.VMEM)
    return pl.pallas_call(
        norm_one_kernel,
        in_specs=[vmem] * 6,
        out_specs=vmem,
        out_shape=sds(res.shape, f32),
        compiler_params=params(),
        name="norm_one_back",
    )(x, res, own, core, far, gains)


def swap(value, axis, bits):
    size = lax.axis_size(axis)
    return lax.ppermute(value, axis, [(place, place ^ bits) for place in range(size)])


def gather_eight(value):
    p = [value] + [None] * 7
    p[4] = swap(value, "shard", 4)
    p[2] = swap(value, "shard", 2)
    p[1] = swap(value, "shard", 1)
    p[6] = swap(p[4], "shard", 2)
    p[3] = swap(p[2], "shard", 1)
    p[5] = swap(p[4], "shard", 1)
    p[7] = swap(p[6], "shard", 1)
    return p


def plus(left, right):
    return (left.astype(f32) + right.astype(f32)).astype(bf16)


def reduce_z(parts):
    there = plus(parts[2], swap(parts[3], "shard", 2))
    near = swap(parts[1], "shard", 2)
    far = swap(there, "shard", 4)
    return parts[0].astype(f32) + near.astype(f32) + far.astype(f32)


def tie(values, after):
    values, _ = lax.optimization_barrier((values, after))
    return values


def per_device(inputs, attn_gain, qkv_weight, out_weight, mlp_gain, in_weight, mlp_out, cotangent):
    _, rows, width = inputs.shape
    shards = lax.axis_size("shard")
    eight = shards == 8
    count = 8 if eight else 1
    piece = width // shards
    seq, shard = lax.axis_index("seq"), lax.axis_index("shard")
    x_place, core = seq // 2, seq % 2
    idx = jnp.stack([shard, seq, x_place, core]).astype(jnp.int32)

    order = jnp.bitwise_xor(seq, jnp.arange(4))
    places = (order[:, None] * rows + jnp.arange(rows)[None, :]).reshape(-1)
    frequency = 1.0 / rope_base ** (jnp.arange(0, HD, 2, dtype=f32) / HD)
    angles = places.astype(f32)[:, None] * jnp.tile(frequency, 4)[None, :]
    sign = jnp.where(jnp.arange(128) % HD < HD // 2, -1.0, 1.0)
    cosine, sine = jnp.cos(angles), jnp.sin(angles) * sign

    x0 = inputs[0]
    c0 = cotangent[0]
    w_qkv = lax.dynamic_slice_in_dim(qkv_weight, seq * COLS, COLS, 2)
    w_qkv = jnp.transpose(w_qkv, (1, 0, 2)).reshape(piece, 3 * COLS)
    w_in = in_weight.reshape(piece, 2, 2, HALF)
    w_in = lax.dynamic_index_in_dim(w_in, core, 2, keepdims=False)
    w_in = jnp.pad(w_in, ((0, 0), (0, 0), (0, PADDED - HALF))).reshape(piece, 2 * PADDED)
    w_down = lax.dynamic_slice_in_dim(mlp_out, core * HALF, HALF, 0)

    x2 = swap(x0, "seq", 2)
    x1 = swap(x0, "seq", 1)
    x3 = swap(x2, "seq", 1)
    if eight:
        gain_rows = jnp.concatenate([attn_gain, mlp_gain, jnp.zeros(3 * COLS - 2 * piece, bf16)])[None]
        w_qkv = jnp.concatenate([w_qkv, jnp.pad(gain_rows, ((0, EXTRA - 1), (0, 0)))], axis=0)
        qkv_pieces = gather_eight(w_qkv)
        both_gains = None
        later = tie((out_weight, w_in, w_down), (qkv_pieces[7], x2))
        out_pieces = gather_eight(later[0])
        later = tie(later[1:], (out_pieces[7],))
        in_pieces = gather_eight(later[0])
        later = tie(later[1:], (in_pieces[7],))
        down_pieces = gather_eight(later[0])
    else:
        both_gains = jnp.stack(
            [
                lax.all_gather(attn_gain, "shard", axis=0, tiled=True),
                lax.all_gather(mlp_gain, "shard", axis=0, tiled=True),
            ]
        )
        qkv_pieces = [lax.all_gather(w_qkv, "shard", axis=0, tiled=True)]
        out_pieces = [lax.all_gather(out_weight, "shard", axis=0, tiled=True)]
        in_pieces = [lax.all_gather(w_in, "shard", axis=0, tiled=True)]
        down_pieces = [lax.all_gather(w_down, "shard", axis=1, tiled=True)]
    c1 = swap(c0, "seq", 1)

    first_low, q, k, v, w_full, gains = qkv_call(
        count, idx, (x0, x1, x2, x3), qkv_pieces, both_gains, cosine, sine
    )
    ctx_far, lse_far = attend(q, k, v, 1)
    ctx_other = swap(ctx_far, "seq", 2)
    ctx_near, lse_near = attend(tie(q, ctx_far), k, v, 0)
    out_own, w_sel = out_call(count, idx, ctx_near, ctx_other, out_pieces)
    out_core = swap(out_own, "seq", 1)
    second_low, hidden, gate_up_grad, second_own, w_down_full = mlp_call(
        count, idx, x0, x1, out_own, out_core, c0, c1, gains, in_pieces, down_pieces
    )
    second_core = swap(second_own, "seq", 1)
    down_other, down_mine, down_keep, down_send = down_call(
        count, idx, hidden, w_down_full, c0, c1
    )
    down_core = swap(down_other, "seq", 1)
    res, res_low, grad_near, grad_other, gain_two = norm_two_call(
        x0, x1, out_own, out_core, second_own, second_core, c0, c1, gains, w_sel
    )
    grad_far = swap(grad_other, "seq", 2)
    result = (
        x0.astype(f32)
        + out_own[:rows].astype(f32)
        + out_core[rows:].astype(f32)
        + down_mine.astype(f32)
        + down_core.astype(f32)
    ).astype(bf16)[None]
    wide = wide_call(count, idx, second_low, gate_up_grad)
    out_keep, out_send = out_grad_call(count, idx, ctx_near, ctx_other, res_low)

    raw_q_near, dk, dv = attend_back(0, q, grad_near, ctx_near, lse_near, k, v, cosine, sine)
    raw_q_far, raw_k, raw_v = attend_back(
        1, q, grad_far, ctx_far, lse_far, k, v, cosine, sine, (dk, dv)
    )

    far_core, near_core = back_project(raw_q_near, raw_q_far, raw_k, raw_v, w_full, 1)
    far_got, near_got = swap(far_core, "seq", 1), swap(near_core, "seq", 1)
    far_own, near_own = back_project(raw_q_near, raw_q_far, raw_k, raw_v, w_full, 0)
    first_far = swap(plus(far_own, far_got), "seq", 2)
    *qkv_terms, gain_one = qkv_grad_call(
        count, idx, first_low, raw_q_near, raw_q_far, raw_k, raw_v, w_full, gains
    )
    input_grad = norm_one_call(x0, res, near_own, near_got, first_far, gains)[None]

    down_sum = plus(down_keep, swap(down_send, "seq", 2))
    out_sum = plus(out_keep, swap(out_send, "seq", 2))
    gain_terms = jnp.concatenate([gain_one[:1], gain_two[:1]], axis=0)
    if eight:
        wide_keep, wide_send = wide
        wide_sum = plus(wide_keep, swap(wide_send, "shard", 1))
        wide_sum = plus(wide_sum[0], swap(wide_sum[1], "seq", 2))
        wide_total = reduce_z([wide_sum[r] for r in range(4)])
        down_sum, out_sum = (
            plus(t[0::2], swap(t[1::2], "shard", 1)) for t in (down_sum, out_sum)
        )
        down_total = reduce_z([down_sum[r] for r in range(4)])
        out_total = reduce_z([out_sum[r] for r in range(4)])
        qkv_keep, qkv_send = qkv_terms
        qkv_sum = plus(qkv_keep, swap(qkv_send, "shard", 1))
        qkv_total = reduce_z([qkv_sum[r] for r in range(4)])
        for axis, bits in (("seq", 1), ("shard", 1), ("shard", 2), ("seq", 2), ("shard", 4)):
            gain_terms = gain_terms + swap(gain_terms, axis, bits)
    else:
        wide_sum = plus(wide[0][0, 0], swap(wide[0][1, 0], "seq", 2))
        scatter = lambda value, dim: lax.psum_scatter(
            value, "shard", scatter_dimension=dim, tiled=True
        ).astype(f32)
        wide_total = scatter(wide_sum, 0)
        down_total = scatter(down_sum[0], 1)
        out_total = scatter(out_sum[0], 1)
        qkv_total = scatter(qkv_terms[0][0], 0)
        gain_terms = lax.psum(gain_terms, ("seq", "shard"))
    moved = lax.ppermute(down_total.astype(bf16), "seq", [(1, 2), (2, 1)]).astype(f32)
    down_total = jnp.where((seq == 1) | (seq == 2), moved, down_total)
    take = width // (4 * shards)
    gain_out = lax.dynamic_slice_in_dim(gain_terms, (seq * shards + shard) * take, take, 1)
    qkv_out = jnp.transpose(qkv_total.reshape(piece, 3, COLS), (1, 0, 2))
    return (
        result,
        input_grad,
        gain_out[0],
        qkv_out,
        out_total,
        gain_out[1],
        wide_total[:, :HALF],
        down_total,
    )


def solution(mesh):
    placed = (
        P("shard", "seq", None),
        P("shard"),
        P(None, "shard", None),
        P("shard", None),
        P("shard"),
        P("shard", None),
        P(None, "shard"),
        P("shard", "seq", None),
    )
    return jax.shard_map(
        per_device,
        mesh=mesh,
        in_specs=placed,
        out_specs=(
            P("shard", "seq", None),
            P("shard", "seq", None),
            P(("seq", "shard")),
            P(None, "shard", "seq"),
            P("seq", "shard"),
            P(("seq", "shard")),
            P("shard", "seq"),
            P("seq", "shard"),
        ),
        check_vma=False,
    )
```

```python
from functools import partial
import math

import jax
import jax.numpy as jnp
from jax import lax
from jax.experimental import pallas as pl
from jax.experimental.pallas import tpu as pltpu
from jax.sharding import PartitionSpec as P

HEADS = 16
HD = 64
FF = 2624

epsilon = 1e-05
rope_base = 160000.0

f32 = jnp.float32
bf16 = jnp.bfloat16

WIDTH = 1024
HALF = FF // 2
PADDED = 1408
BLOCK = FF // 4
COLS = 256
CHUNKS = (0, 4, 2, 6, 1, 5, 3, 7)
EXTRA = 16
ROWS_BY_COLS = (((0,), (0,)), ((), ()))
COLS_BY_COLS = (((1,), (1,)), ((), ()))
VMEM_LIMIT = 58 * 1024 * 1024

ANY = pl.BlockSpec(memory_space=pl.ANY)
SMEM = pl.BlockSpec(memory_space=pltpu.SMEM)


def cost(micros):
    return pl.CostEstimate(flops=int(micros), transcendentals=0, bytes_accessed=int(micros))


def params():
    return pltpu.CompilerParams(vmem_limit_bytes=VMEM_LIMIT)


def sds(shape, dtype=bf16):
    return jax.ShapeDtypeStruct(shape, dtype)


def aligned(index, size):
    return pl.ds(pl.multiple_of(index * size, size), size)


def normalize(values):
    center = values - jnp.mean(values, axis=-1, keepdims=True)
    inv_scale = lax.rsqrt(jnp.mean(center * center, axis=-1, keepdims=True) + epsilon)
    return center * inv_scale, inv_scale


def norm_back(grads, xhat, inv_scale):
    mean_grad = jnp.mean(grads, axis=-1, keepdims=True)
    mean_both = jnp.mean(grads * xhat, axis=-1, keepdims=True)
    return inv_scale * (grads - mean_grad - xhat * mean_both)


def turned(values):
    lane = lax.broadcasted_iota(jnp.int32, values.shape, 1)
    width = values.shape[1]
    return jnp.where(
        lane % HD < HD // 2, pltpu.roll(values, width - HD // 2, 1), pltpu.roll(values, HD // 2, 1)
    )


def twice(table):
    return jnp.concatenate([table, table], axis=1)


def piece_of(refs, place, rows=None, width=None):
    array, lead, column = place
    index = () if lead is None else (lead,)
    rows = slice(None) if rows is None else rows
    cols = slice(None) if width is None else pl.ds(column, width)
    return refs[array].at[(*index, rows, cols)]


def fetch_rows(count, shard, refs, places, width, target, sem):
    size = target.shape[0] // count
    copies = []
    for r in range(count):
        rows = aligned(jnp.bitwise_xor(shard, r), size) if count > 1 else pl.ds(0, size)
        copies.append(
            pltpu.make_async_copy(piece_of(refs, places[r], width=width), target.at[rows], sem.at[r])
        )
    return copies


def qkv_kernel(count, places, idx, *refs):
    x_refs, refs = refs[:4], refs[4:]
    n_arrays = 1 + max(array for array, _, _ in places)
    w_refs, refs = refs[:n_arrays], refs[n_arrays:]
    if count == 1:
        gain_ref, refs = refs[0], refs[1:]
    cos_ref, sin_ref, fn_o, q_o, k_o, v_o, w_o, g_o, xs, gs, semx, semw, semg = refs
    step = pl.program_id(0)
    shard = idx[0]
    size = WIDTH // count

    def x_copy(r):
        return pltpu.make_async_copy(x_refs[r], xs.at[r], semx.at[r])

    def w_copy(r):
        return pltpu.make_async_copy(
            piece_of(w_refs, places[r], rows=pl.ds(0, size)), w_o.at[aligned(jnp.bitwise_xor(shard, r), size)], semw.at[r]
        )

    def g_copy(r):
        return pltpu.make_async_copy(
            piece_of(w_refs, places[r], rows=pl.ds(size, EXTRA)), gs.at[jnp.bitwise_xor(shard, r)], semg.at[r]
        )

    @pl.when(step == 0)
    def _():
        if count == 1:
            w_all = pltpu.make_async_copy(w_refs[0], w_o, semw.at[0])
            w_all.start()
        else:
            for r in range(count):
                w_copy(r).start()
                g_copy(r).start()
        for r in range(4):
            x_copy(r).start()
        if count == 1:
            w_all.wait()
            g_o[0:1] = gain_ref[0:1].astype(f32)
            g_o[1:2] = gain_ref[1:2].astype(f32)
        else:
            for r in range(count):
                w_copy(r).wait()
                g_copy(r).wait()
            for r in range(count):
                part = gs[r].astype(f32)
                g_o[0:1, r * size : (r + 1) * size] = part[0:1, 0:size]
                g_o[1:2, r * size : (r + 1) * size] = part[0:1, size : 2 * size]

    for r in range(4):

        @pl.when(step == r)
        def _():
            x_copy(r).wait()

    xhat, _ = normalize(xs[step].astype(f32))
    first_low = (xhat * g_o[0:1]).astype(bf16)
    fn_o[...] = first_low
    cosine, sine = twice(cos_ref[...]), twice(sin_ref[...])
    outs = (q_o, k_o, v_o)
    for part in range(3):
        value = jnp.dot(first_low, w_o[:, part * COLS : (part + 1) * COLS], preferred_element_type=f32)
        if part < 2:
            value = value * cosine + turned(value) * sine
        value = value.astype(bf16)
        if part == 0:
            value = value * jnp.asarray(1.0 / math.sqrt(HD), bf16)
        outs[part][...] = value


def qkv_call(count, idx, chunks, pieces, gains, cosine, sine):
    arrays, where = pieces
    rows = chunks[0].shape[0]
    by_step = lambda width: pl.BlockSpec((rows, width), lambda r: (r, 0))
    whole = lambda shape: pl.BlockSpec(shape, lambda r: (0, 0))
    extra = [] if count > 1 else [gains]
    return pl.pallas_call(
        partial(qkv_kernel, count, where),
        grid=(4,),
        in_specs=[SMEM]
        + [ANY] * (4 + len(arrays))
        + ([] if count > 1 else [whole((2, WIDTH))])
        + [by_step(128), by_step(128)],
        out_specs=[
            by_step(WIDTH),
            by_step(COLS),
            by_step(COLS),
            by_step(COLS),
            whole((WIDTH, 3 * COLS)),
            whole((8, WIDTH)),
        ],
        out_shape=[
            sds((4 * rows, WIDTH)),
            sds((4 * rows, COLS)),
            sds((4 * rows, COLS)),
            sds((4 * rows, COLS)),
            sds((WIDTH, 3 * COLS)),
            sds((8, WIDTH), f32),
        ],
        scratch_shapes=[
            pltpu.VMEM((4, rows, WIDTH), bf16),
            pltpu.VMEM((8, EXTRA, 3 * COLS), bf16),
            pltpu.SemaphoreType.DMA((4,)),
            pltpu.SemaphoreType.DMA((count,)),
            pltpu.SemaphoreType.DMA((count,)),
        ],
        compiler_params=params(),
        cost_estimate=cost(11),
        name="project",
    )(idx, *chunks, *arrays, *extra, cosine, sine)


def head_of(shape):
    return lax.broadcasted_iota(jnp.int32, shape, len(shape) - 1) // HD


def attend_kernel(q_ref, k_ref, v_ref, o_ref, lse_ref):
    q, k, v = q_ref[...], k_ref[...], v_ref[...]
    heads = head_of(q.shape)
    total = jnp.zeros(q.shape, f32)
    lses = jnp.zeros((q.shape[0], 128), f32)
    lane = lax.broadcasted_iota(jnp.int32, lses.shape, 1)
    for h in range(COLS // HD):
        q_h = jnp.where(heads == h, q, jnp.zeros_like(q))
        scores = lax.dot_general(q_h, k, COLS_BY_COLS, preferred_element_type=f32)
        row_max = jnp.max(scores, axis=1, keepdims=True)
        exponent = jnp.exp(scores - row_max)
        row_total = jnp.sum(exponent, axis=1, keepdims=True)
        context = jnp.dot(exponent.astype(bf16), v, preferred_element_type=f32)
        total = jnp.where(heads == h, context * (1.0 / row_total), total)
        lses = jnp.where(lane == h, row_max + jnp.log(row_total), lses)
    o_ref[...] = total.astype(bf16)
    lse_ref[...] = lses.T[:8]


def attend(q, k, v, chunk, after=()):
    span = k.shape[0]
    rows = span // 4
    kept = pl.BlockSpec((span, COLS), lambda i: (0, 0))
    return pl.pallas_call(
        lambda *refs: attend_kernel(*refs[:3], *refs[3 + len(after) :]),
        grid=(1,),
        in_specs=[pl.BlockSpec((rows, COLS), lambda i: (chunk, 0)), kept, kept] + [ANY] * len(after),
        out_specs=[
            pl.BlockSpec((rows, COLS), lambda i: (0, 0)),
            pl.BlockSpec((8, rows), lambda i: (0, 0)),
        ],
        out_shape=[sds((rows, COLS)), sds((8, rows), f32)],
        compiler_params=params(),
        cost_estimate=cost(8),
        name="attend",
    )(q, k, v, *after)


def attend_back_kernel(last, pair, *refs):
    q_ref, do_ref, oa_ref, ob_ref, la_ref, lb_ref, k_ref, v_ref, qcos, qsin, refs = *refs[:10], refs[10:]
    if last:
        dk_i, dv_i, kcos, ksin, refs = *refs[:4], refs[4:]
    dq_ref, dk_ref, dv_ref, do_s, inner_s, lse_s, dq_s = refs
    step = pl.program_id(0)
    width = q_ref.shape[1]
    n_heads = width // HD

    @pl.when(step == 0)
    def _():
        do = do_ref[...]
        context = jnp.concatenate([oa_ref[...], ob_ref[...]], axis=0)
        product = do.astype(f32) * context.astype(f32)
        high = product.astype(bf16)
        rest = (product - high.astype(f32)).astype(bf16)
        chosen = (
            head_of((8, width)) == lax.broadcasted_iota(jnp.int32, (8, width), 0)
        ).astype(bf16)
        inner_s[...] = lax.dot_general(
            chosen, high, COLS_BY_COLS, preferred_element_type=f32
        ) + lax.dot_general(chosen, rest, COLS_BY_COLS, preferred_element_type=f32)
        lse_s[...] = jnp.concatenate([la_ref[...], lb_ref[...]], axis=1)
        heads = head_of(do.shape)
        for h in range(n_heads):
            do_s[h] = jnp.where(heads == h, do, jnp.zeros_like(do))
        dq_s[...] = jnp.zeros_like(dq_s)

    q, k, v = q_ref[...], k_ref[...], v_ref[...]
    heads = head_of(k.shape)
    dk = jnp.zeros(k.shape, f32)
    dv = jnp.zeros(k.shape, f32)
    dq = dq_s[...]
    for h in range(n_heads):
        at = n_heads * pair + h
        k_h = jnp.where(heads == h, k, jnp.zeros_like(k))
        scores = lax.dot_general(k_h, q, COLS_BY_COLS, preferred_element_type=f32)
        probs = jnp.exp(scores - lse_s[at : at + 1, :])
        probs_grad = lax.dot_general(v, do_s[h], COLS_BY_COLS, preferred_element_type=f32)
        scores_grad = (probs * (probs_grad - inner_s[h : h + 1, :])).astype(bf16)
        dv = dv + jnp.dot(probs.astype(bf16), do_s[h], preferred_element_type=f32)
        dk = jnp.where(heads == h, jnp.dot(scores_grad, q, preferred_element_type=f32), dk)
        dq = dq + lax.dot_general(scores_grad, k_h, ROWS_BY_COLS, preferred_element_type=f32)
    dq_s[...] = dq
    if last:
        dk = dk + dk_i[...]
        dv = dv + dv_i[...]
        dk_ref[...] = (dk * kcos[...] - turned(dk) * ksin[...]).astype(bf16)
        dv_ref[...] = dv.astype(bf16)
    else:
        dk_ref[...] = dk
        dv_ref[...] = dv

    @pl.when(step == pl.num_programs(0) - 1)
    def _():
        dq = dq_s[...] * (1.0 / math.sqrt(HD))
        dq_ref[...] = (dq * qcos[...] - turned(dq) * qsin[...]).astype(bf16)


def attend_back(part, pair, q, do, contexts, lses, k, v, cosine, sine, earlier=None, after=(), tile=512):
    span = k.shape[0]
    rows = do.shape[0]
    last = earlier is not None
    rows_at = lambda at, col, count=rows, width=128: pl.BlockSpec((count, width), lambda i: (at, col))
    keys = lambda col: pl.BlockSpec((tile, 128), lambda i: (i, col))
    grads = bf16 if last else f32
    n_in = 10 + (4 if last else 0)
    return pl.pallas_call(
        lambda *refs: attend_back_kernel(last, pair, *refs[:n_in], *refs[n_in + len(after) :]),
        grid=(span // tile,),
        in_specs=[
            rows_at(part, pair),
            rows_at(0, pair),
            rows_at(0, pair, rows // 2),
            rows_at(0, pair, rows // 2),
            rows_at(0, 0, 8, rows // 2),
            rows_at(0, 0, 8, rows // 2),
            keys(pair),
            keys(pair),
            rows_at(part, 0),
            rows_at(part, 0),
        ]
        + ([keys(0), keys(0), keys(0), keys(0)] if last else [])
        + [ANY] * len(after),
        out_specs=[rows_at(0, 0), keys(0), keys(0)],
        out_shape=[sds((rows, 128)), sds((span, 128), grads), sds((span, 128), grads)],
        scratch_shapes=[
            pltpu.VMEM((128 // HD, rows, 128), bf16),
            pltpu.VMEM((8, rows), f32),
            pltpu.VMEM((8, rows), f32),
            pltpu.VMEM((rows, 128), f32),
        ],
        compiler_params=params(),
        cost_estimate=cost(15),
        name="attend_back",
    )(q, do, *contexts, *lses, k, v, cosine, sine, *((*earlier, cosine, sine) if last else ()), *after)


def out_kernel(count, places, idx, ma_ref, mb_ref, other_ref, *refs):
    w_refs, (o_ref, wsel_ref, w_s, sem) = refs[:-4], refs[-4:]
    copies = fetch_rows(count, idx[0], w_refs, places, WIDTH, w_s, sem)
    for copy in copies:
        copy.start()
    for copy in copies:
        copy.wait()
    seq = idx[1]
    wsel_ref[0:COLS] = w_s[aligned(seq, COLS)]
    wsel_ref[COLS:] = w_s[aligned(jnp.bitwise_xor(seq, 2), COLS)]
    rows = ma_ref.shape[0]
    for r, mine in enumerate((ma_ref, mb_ref)):
        both = jnp.concatenate([mine[...], other_ref[r * rows : (r + 1) * rows]], axis=1)
        value = jnp.dot(both, wsel_ref[...], preferred_element_type=f32)
        o_ref[r * rows : (r + 1) * rows] = value.astype(bf16)


def out_call(count, idx, mine, other, pieces):
    vmem = pl.BlockSpec(memory_space=pltpu.VMEM)
    arrays, where = pieces
    return pl.pallas_call(
        partial(out_kernel, count, where),
        in_specs=[SMEM] + [vmem] * 3 + [ANY] * len(arrays),
        out_specs=[vmem, vmem],
        out_shape=[sds((2 * mine[0].shape[0], WIDTH)), sds((2 * COLS, WIDTH))],
        scratch_shapes=[pltpu.VMEM((WIDTH, WIDTH), bf16), pltpu.SemaphoreType.DMA((count,))],
        compiler_params=params(),
        cost_estimate=cost(5),
        name="out_project",
    )(idx, *mine, other, *arrays)


def mlp_kernel(count, n_arrays, mine, other, down, idx, *refs):
    x0, x1, po, pr, c0, c1, g_ref, refs = *refs[:7], refs[7:]
    w_refs, refs = refs[:n_arrays], refs[n_arrays:]
    sn_o, hid_o, gug_o, sgp_o, wd_o, refs = *refs[:5], refs[5:]
    xs, pos, prs, cs, wi, wd, sn_s, hid_s, gug_s, sgp_s, sem_a, sem_m, sem_i, sem_d, sem_o = refs
    shard, x_place = idx[0], idx[2]
    rows = xs.shape[1]
    loads = [
        pltpu.make_async_copy(x0, xs.at[0], sem_a.at[0]),
        pltpu.make_async_copy(x1, xs.at[1], sem_a.at[1]),
        pltpu.make_async_copy(po, pos, sem_a.at[2]),
        pltpu.make_async_copy(pr, prs, sem_a.at[3]),
        pltpu.make_async_copy(c0, cs.at[pl.ds(0, rows)], sem_a.at[4]),
        pltpu.make_async_copy(c1, cs.at[pl.ds(rows, rows)], sem_a.at[5]),
    ]
    here = wi.at[:, aligned(x_place, PADDED)]
    there = wi.at[:, aligned(1 - x_place, PADDED)]
    wi_loads = fetch_rows(count, shard, w_refs, mine, PADDED, here, sem_m)
    wi_loads += fetch_rows(count, shard, w_refs, other, PADDED, there, sem_i)
    wd_loads = fetch_rows(count, shard, w_refs, down, PADDED, wd, sem_d)
    for copy in loads[:4] + wi_loads + loads[4:] + wd_loads:
        copy.start()
    for copy in loads[:4]:
        copy.wait()
    for r in range(2):
        here, there = pl.ds(r * rows, rows), pl.ds((1 - r) * rows, rows)
        after = xs[r].astype(f32) + pos[here].astype(f32) + prs[there].astype(f32)
        xhat, _ = normalize(after)
        sn_s[here] = (xhat * g_ref[1:2]).astype(bf16)
    stores = []

    def store(source, target, k):
        copy = pltpu.make_async_copy(source, target, sem_o.at[k])
        copy.start()
        stores.append(copy)

    store(sn_s, sn_o, 0)
    for copy in wi_loads + loads[4:] + wd_loads:
        copy.wait()
    store(wd, wd_o, 1)
    start = 0
    while start < PADDED:
        size = min(256, PADDED - start)
        here = pl.ds(start, size)
        gate = jnp.dot(sn_s[...], wi[:, here], preferred_element_type=f32)
        up = jnp.dot(sn_s[...], wi[:, pl.ds(PADDED + start, size)], preferred_element_type=f32)
        back = jnp.dot(cs[...], wd[:, here], preferred_element_type=f32)
        below = 0.5 * (1.0 + lax.erf(gate * math.sqrt(0.5)))
        density = jnp.exp(-0.5 * gate * gate) * (1.0 / math.sqrt(2.0 * math.pi))
        unit = gate * below
        hid_s[:, here] = (unit * up).astype(bf16)
        gug_s[0, :, here] = (back * up * (below + gate * density)).astype(bf16)
        gug_s[1, :, here] = (back * unit).astype(bf16)
        start += size
    store(hid_s, hid_o, 2)
    store(gug_s, gug_o, 3)
    value = lax.dot_general(gug_s[0], wi[:, :PADDED], COLS_BY_COLS, preferred_element_type=f32)
    value = value + lax.dot_general(gug_s[1], wi[:, PADDED:], COLS_BY_COLS, preferred_element_type=f32)
    sgp_s[...] = value.astype(bf16)
    store(sgp_s, sgp_o, 4)
    for copy in stores:
        copy.wait()


def mlp_call(count, idx, x0, x1, po, pr, c0, c1, gains, arrays, mine, other, down):
    rows = x0.shape[0]
    return pl.pallas_call(
        partial(mlp_kernel, count, len(arrays), mine, other, down),
        in_specs=[SMEM] + [ANY] * 6 + [pl.BlockSpec(memory_space=pltpu.VMEM)] + [ANY] * len(arrays),
        out_specs=[ANY] * 5,
        out_shape=[
            sds((2 * rows, WIDTH)),
            sds((2 * rows, PADDED)),
            sds((2, 2 * rows, PADDED)),
            sds((2 * rows, WIDTH)),
            sds((WIDTH, PADDED)),
        ],
        scratch_shapes=[
            pltpu.VMEM((2, rows, WIDTH), bf16),
            pltpu.VMEM((2 * rows, WIDTH), bf16),
            pltpu.VMEM((2 * rows, WIDTH), bf16),
            pltpu.VMEM((2 * rows, WIDTH), bf16),
            pltpu.VMEM((WIDTH, 2 * PADDED), bf16),
            pltpu.VMEM((WIDTH, PADDED), bf16),
            pltpu.VMEM((2 * rows, WIDTH), bf16),
            pltpu.VMEM((2 * rows, PADDED), bf16),
            pltpu.VMEM((2, 2 * rows, PADDED), bf16),
            pltpu.VMEM((2 * rows, WIDTH), bf16),
            pltpu.SemaphoreType.DMA((6,)),
            pltpu.SemaphoreType.DMA((count,)),
            pltpu.SemaphoreType.DMA((count,)),
            pltpu.SemaphoreType.DMA((count,)),
            pltpu.SemaphoreType.DMA((5,)),
        ],
        compiler_params=params(),
        cost_estimate=cost(25),
        name="feed_forward",
    )(idx, x0, x1, po, pr, c0, c1, gains, *arrays)


def down_kernel(count, idx, hid_ref, wd_ref, c0, c1, ma, mb, other, low, res_other, res_mine, keep_o, send_o, acc):
    shard, x_place = idx[0], idx[2]
    rows = c0.shape[0]
    width = WIDTH // count
    places = [
        aligned(jnp.bitwise_xor(shard, r), width) if count > 1 else pl.ds(0, width) for r in CHUNKS[:count]
    ]
    acc[...] = lax.dot_general(
        hid_ref[0:rows], c0[...], ROWS_BY_COLS, preferred_element_type=f32
    ) + lax.dot_general(hid_ref[rows:], c1[...], ROWS_BY_COLS, preferred_element_type=f32)
    for part, target in ((1, send_o), (0, keep_o)):
        here = pl.ds(pl.multiple_of(jnp.bitwise_xor(x_place, part) * BLOCK, 8), BLOCK)
        for r in range(count):
            target[r, 0:BLOCK] = acc[here, places[r]].astype(bf16)
    mine = jnp.concatenate([ma[...], mb[...]], axis=0)
    for context, target in ((other[...], send_o), (mine, keep_o)):
        acc[0:COLS] = lax.dot_general(context, low[...], ROWS_BY_COLS, preferred_element_type=f32)
        for r in range(count):
            target[r, BLOCK:] = acc[0:COLS, places[r]].astype(bf16)
    for r, target in ((1, res_other), (0, res_mine)):
        target[...] = lax.dot_general(
            hid_ref[r * rows : (r + 1) * rows], wd_ref[...], COLS_BY_COLS, preferred_element_type=f32
        ).astype(bf16)


def down_call(count, idx, hidden, wd, c0, c1, mine, other, low):
    rows = c0.shape[0]
    vmem = pl.BlockSpec(memory_space=pltpu.VMEM)
    return pl.pallas_call(
        partial(down_kernel, count),
        in_specs=[SMEM] + [vmem] * 8,
        out_specs=[vmem] * 4,
        out_shape=[
            sds((rows, WIDTH)),
            sds((rows, WIDTH)),
            sds((count, BLOCK + COLS, WIDTH // count)),
            sds((count, BLOCK + COLS, WIDTH // count)),
        ],
        scratch_shapes=[pltpu.VMEM((PADDED, WIDTH), f32)],
        compiler_params=params(),
        cost_estimate=cost(15),
        name="down_project",
    )(idx, hidden, wd, c0, c1, *mine, other, low)


def norm_two_kernel(x0, x1, po, pr, so, sr, c0, c1, g_ref, wsel, res_o, low_o, mine_o, other_o, gain_o):
    step = pl.program_id(0)
    half = pl.num_programs(0) // 2
    first = step < half
    gain = g_ref[1:2]
    x = jnp.where(first, x0[...], x1[...])
    c = jnp.where(first, c0[...], c1[...])
    after = x.astype(f32) + po[...].astype(f32) + pr[...].astype(f32)
    xhat, inv_scale = normalize(after)
    second = so[...].astype(f32) + sr[...].astype(f32)
    res = c.astype(f32) + norm_back(second * gain, xhat, inv_scale)

    @pl.when(step == 0)
    def _():
        gain_o[...] = jnp.zeros_like(gain_o)

    @pl.when(first)
    def _():
        res_o[...] = res
        gain_o[...] += jnp.sum(second * xhat, axis=0, keepdims=True)

    low = res.astype(bf16)
    low_o[...] = low
    value = lax.dot_general(low, wsel[...], COLS_BY_COLS, preferred_element_type=f32).astype(bf16)
    mine_o[...] = value[:, :COLS]
    other_o[...] = value[:, COLS:]


def norm_two_call(x0, x1, po, pr, so, sr, c0, c1, gains, wsel, half=2):
    rows = x0.shape[0]
    size = rows // half
    spec = lambda width, at: pl.BlockSpec((size, width), lambda s: (at(s), 0))
    lower = lambda s: jnp.minimum(s, half - 1)
    upper = lambda s: jnp.maximum(s - half, 0)
    same = lambda s: s
    other = lambda s: lax.rem(s + half, 2 * half)
    whole = lambda shape: pl.BlockSpec(shape, lambda s: (0, 0))
    return pl.pallas_call(
        norm_two_kernel,
        grid=(2 * half,),
        in_specs=[
            spec(WIDTH, lower),
            spec(WIDTH, upper),
            spec(WIDTH, same),
            spec(WIDTH, other),
            spec(WIDTH, same),
            spec(WIDTH, other),
            spec(WIDTH, lower),
            spec(WIDTH, upper),
            whole((8, WIDTH)),
            whole((2 * COLS, WIDTH)),
        ],
        out_specs=[
            spec(WIDTH, lower),
            spec(WIDTH, same),
            spec(COLS, same),
            spec(COLS, same),
            whole((8, WIDTH)),
        ],
        out_shape=[
            sds((rows, WIDTH), f32),
            sds((2 * rows, WIDTH)),
            sds((2 * rows, COLS)),
            sds((2 * rows, COLS)),
            sds((8, WIDTH), f32),
        ],
        compiler_params=params(),
        cost_estimate=cost(8),
        name="norm_two_back",
    )(x0, x1, po, pr, so, sr, c0, c1, gains, wsel)


def wide_kernel(count, idx, sn_ref, gug_ref, *refs):
    outs, acc = refs[:-1], refs[-1]
    part = pl.program_id(0)
    shard = idx[0]
    acc[...] = lax.dot_general(sn_ref[...], gug_ref[0], ROWS_BY_COLS, preferred_element_type=f32)
    size = WIDTH // count
    per_array = count // len(outs)
    for k, r in enumerate(CHUNKS[:count]):
        place = aligned(jnp.bitwise_xor(shard, r), size) if count > 1 else pl.ds(0, size)
        outs[k // per_array][0, k % per_array] = acc[place].astype(bf16)


def wide_call(count, idx, sn, gug):
    tokens = sn.shape[0]
    split = 2 if count > 1 else 1
    size = WIDTH // count
    spec = lambda shape, at: pl.BlockSpec(shape, at)
    grid_spec = pltpu.PrefetchScalarGridSpec(
        num_scalar_prefetch=1,
        grid=(2,),
        in_specs=[
            spec((tokens, WIDTH), lambda p, s: (0, 0)),
            spec((1, tokens, PADDED), lambda p, s: (jnp.bitwise_xor(p, s[2]), 0, 0)),
        ],
        out_specs=[spec((1, count // split, size, PADDED), lambda p, s: (p, 0, 0, 0))] * split,
        scratch_shapes=[pltpu.VMEM((WIDTH, PADDED), f32)],
    )
    return pl.pallas_call(
        partial(wide_kernel, count),
        grid_spec=grid_spec,
        out_shape=[sds((2, count // split, size, PADDED))] * split,
        compiler_params=params(),
        cost_estimate=cost(12),
        name="wide_grad",
    )(idx, sn, gug)


def back_project_kernel(q0, q1, f0, f1, k0n, k1n, k0f, k1f, v0n, v1n, v0f, v1f, w_ref, both_o):
    for half, parts in (
        (1, (f0, f1, k0f, k1f, v0f, v1f)),
        (0, (q0, q1, k0n, k1n, v0n, v1n)),
    ):
        raw = jnp.concatenate([part[...] for part in parts], axis=1)
        both_o[half] = lax.dot_general(
            raw, w_ref[...], COLS_BY_COLS, preferred_element_type=f32
        ).astype(bf16)


def back_project(raw_pairs, w, chunk):
    rows = raw_pairs[0][0].shape[0] // 2
    at = lambda where: pl.BlockSpec((rows, 128), lambda i: (where, 0))
    q0, f0, k0, v0 = raw_pairs[0]
    q1, f1, k1, v1 = raw_pairs[1]
    return pl.pallas_call(
        back_project_kernel,
        grid=(1,),
        in_specs=[at(chunk)] * 6
        + [at(chunk + 2)] * 2
        + [at(chunk)] * 2
        + [at(chunk + 2)] * 2
        + [pl.BlockSpec((WIDTH, 3 * COLS), lambda i: (0, 0))],
        out_specs=pl.BlockSpec((2, rows, WIDTH), lambda i: (0, 0, 0)),
        out_shape=sds((2, rows, WIDTH)),
        compiler_params=params(),
        cost_estimate=cost(5),
        name="back_project",
    )(q0, q1, f0, f1, k0, k1, k0, k1, v0, v1, v0, v1, w)


def qkv_grad_kernel(count, idx, fn_ref, qn, qf, k_ref, v_ref, wq, wk, wv, g_ref, keep_o, *refs):
    if count > 1:
        send_o, gain_o, acc = refs
    else:
        gain_o, acc = refs
    rows = qn.shape[0]
    q = jnp.concatenate([qn[...], qf[...]], axis=0)
    raw = jnp.concatenate([q, k_ref[...], v_ref[...]], axis=1)
    acc[...] = lax.dot_general(fn_ref[...], raw, ROWS_BY_COLS, preferred_element_type=f32)
    shard = idx[0]
    size = WIDTH // count
    for k, r in enumerate(CHUNKS[:count]):
        place = aligned(jnp.bitwise_xor(shard, r), size) if count > 1 else pl.ds(0, size)
        target = (keep_o, send_o)[k // 4] if count > 1 else keep_o
        target[k % 4] = acc[place].astype(bf16)
    w = jnp.concatenate([wq[...], wk[...], wv[...]], axis=1)
    both = acc[...] * w.astype(f32)
    high = both.astype(bf16)
    rest = (both - high.astype(f32)).astype(bf16)
    ones = jnp.ones((8, w.shape[1]), bf16)
    total = lax.dot_general(ones, high, COLS_BY_COLS, preferred_element_type=f32)
    total += lax.dot_general(ones, rest, COLS_BY_COLS, preferred_element_type=f32)
    gain_o[...] = total / g_ref[0:1]


def qkv_grad_call(count, idx, first_low, raw, w, gains, pair):
    vmem = pl.BlockSpec(memory_space=pltpu.VMEM)
    split = 2 if count > 1 else 1
    size = WIDTH // count
    width = 3 * 128
    whole = lambda shape: pl.BlockSpec(shape, lambda i: (0,) * len(shape))
    weight = lambda part: pl.BlockSpec((WIDTH, 128), lambda i: (0, 2 * part + pair))
    grads = [(count // split, size, width)] * split + [(8, WIDTH)]
    return pl.pallas_call(
        partial(qkv_grad_kernel, count),
        grid=(1,),
        in_specs=[SMEM, whole(first_low.shape)]
        + [whole(value.shape) for value in raw]
        + [weight(0), weight(1), weight(2), whole(gains.shape)],
        out_specs=[whole(shape) for shape in grads],
        out_shape=[sds(shape) for shape in grads[:-1]] + [sds(grads[-1], f32)],
        scratch_shapes=[pltpu.VMEM((WIDTH, width), f32)],
        compiler_params=params(),
        cost_estimate=cost(6),
        name="project_grad",
    )(idx, first_low, *raw, w, w, w, gains)


def norm_one_kernel(x_ref, res_ref, own, core, far, g_ref, o_ref):
    xhat, inv_scale = normalize(x_ref[...].astype(f32))
    first = own[0].astype(f32) + core[0].astype(f32) + far[...].astype(f32)
    o_ref[...] = res_ref[...] + norm_back(first * g_ref[0:1], xhat, inv_scale)


def norm_one_call(x, res, own, core, far, gains, steps=4):
    rows = x.shape[0]
    block = pl.BlockSpec((rows // steps, WIDTH), lambda i: (i, 0))
    return pl.pallas_call(
        norm_one_kernel,
        grid=(steps,),
        in_specs=[
            block,
            block,
            pl.BlockSpec((1, rows // steps, WIDTH), lambda i: (0, i, 0)),
            pl.BlockSpec((1, rows // steps, WIDTH), lambda i: (0, i, 0)),
            block,
            pl.BlockSpec((8, WIDTH), lambda i: (0, 0)),
        ],
        out_specs=block,
        out_shape=sds(res.shape, f32),
        compiler_params=params(),
        cost_estimate=cost(3),
        name="norm_one_back",
    )(x, res, own, core, far, gains)


def swap(value, axis, bits):
    size = lax.axis_size(axis)
    return lax.ppermute(value, axis, [(place, place ^ bits) for place in range(size)])


def plus(left, right):
    return (left.astype(f32) + right.astype(f32)).astype(bf16)


def together(*values):
    return lax.optimization_barrier(values)


def per_device(inputs, attn_gain, qkv_weight, out_weight, mlp_gain, in_weight, mlp_out, cotangent):
    _, rows, width = inputs.shape
    shards = lax.axis_size("shard")
    eight = shards == 8
    count = 8 if eight else 1
    piece = width // shards
    seq, shard = lax.axis_index("seq"), lax.axis_index("shard")
    x_place, core = seq // 2, seq % 2
    idx = jnp.stack([shard, seq, x_place, core]).astype(jnp.int32)

    order = jnp.bitwise_xor(seq, jnp.arange(4))
    places = (order[:, None] * rows + jnp.arange(rows)[None, :]).reshape(-1)
    frequency = 1.0 / rope_base ** (jnp.arange(0, HD, 2, dtype=f32) / HD)
    angles = places.astype(f32)[:, None] * jnp.tile(frequency, 4)[None, :]
    sign = jnp.where(jnp.arange(128) % HD < HD // 2, -1.0, 1.0)
    cosine, sine = jnp.cos(angles), jnp.sin(angles) * sign

    x0 = inputs[0]
    c0 = cotangent[0]
    w_qkv = lax.dynamic_slice_in_dim(qkv_weight, seq * COLS, COLS, 2)
    w_qkv = jnp.transpose(w_qkv, (1, 0, 2)).reshape(piece, 3 * COLS)
    w_in = in_weight.reshape(piece, 2, 2, HALF)
    w_in = lax.dynamic_index_in_dim(w_in, core, 2, keepdims=False)
    w_in = jnp.pad(w_in, ((0, 0), (0, 0), (0, PADDED - HALF)))
    w_mine = lax.dynamic_index_in_dim(w_in, x_place, 1, keepdims=False)
    w_other = lax.dynamic_index_in_dim(w_in, 1 - x_place, 1, keepdims=False)
    w_down = lax.dynamic_slice_in_dim(mlp_out, core * HALF, HALF, 0).T
    w_down = jnp.pad(w_down, ((0, 0), (0, PADDED - HALF)))

    x2 = swap(x0, "seq", 2)
    by_y = lambda value: swap(value, "shard", 1)
    by_z = lambda value: swap(value, "shard", 2)
    by_zz = lambda value: swap(value, "shard", 4)
    by_x = lambda value: swap(value, "seq", 2)
    by_core = lambda value: swap(value, "seq", 1)
    if eight:
        gain_rows = jnp.concatenate([attn_gain, mlp_gain, jnp.zeros(3 * COLS - 2 * piece, bf16)])[None]
        a0 = jnp.concatenate([w_qkv, jnp.pad(gain_rows, ((0, EXTRA - 1), (0, 0)))], axis=0)
        f0 = jnp.concatenate([w_mine, out_weight, w_down], axis=1)
        a4, a2, a1, f1 = by_zz(a0), by_z(a0), by_y(a0), by_y(f0)
        a4, a2, a1, x0, cosine, sine, idx = together(a4, a2, a1, x0, cosine, sine, idx)
        a6, a35 = by_z(a4), by_y(jnp.stack([a2, a4]))
        x1 = by_core(x0)
        a6, a35, x2, f1 = together(a6, a35, x2, f1)
        a7 = by_y(a6)
        x3 = by_core(x2)
        g0, h0 = f0[:, : PADDED + WIDTH], f0[:, PADDED + WIDTH :]
        g0, h0, a6 = together(g0, h0, a6)
        g4, g2 = by_zz(g0), by_z(g0)
        first_low, q, k, v, w_full, gains = qkv_call(
            count,
            idx,
            (x0, x1, x2, x3),
            (
                (a0, a1, a2, a4, a35, a6, a7),
                tuple((array, lead, 0) for array, lead in
                    ((0, None), (1, None), (2, None), (4, 0), (3, None), (4, 1), (5, None), (6, None))),
            ),
            None,
            cosine,
            sine,
        )
        q, g4, g2, h0, x1 = together(q, g4, g2, h0, x1)
        g6, g35 = by_z(g4), by_y(jnp.stack([g2, g4]))
        e124 = by_x(jnp.stack([f1[:, :PADDED], g2[:, :PADDED], g4[:, :PADDED]]))
        ctx_fa, lse_fa = attend(q, k, v, 2)
        ctx_fa, q, h0 = together(ctx_fa, q, h0)
        h4, h2 = by_zz(h0), by_z(h0)
        ctx_fb, lse_fb = attend(q, k, v, 3)
        ctx_fa, ctx_fb, q, g6 = together(ctx_fa, ctx_fb, q, g6)
        other = by_x(jnp.concatenate([ctx_fa, ctx_fb], axis=0))
        ctx_na, lse_na = attend(q, k, v, 0)
        ctx_na, q, e124, g6 = together(ctx_na, q, e124, g6)
        g7 = by_y(g6)
        ctx_nb, lse_nb = attend(q, k, v, 1)
        ctx_nb, g35, h4, h2, other = together(ctx_nb, g35, h4, h2, other)
        h6, h35 = by_z(h4), by_y(jnp.stack([h2, h4]))
        e356 = by_x(jnp.concatenate([g35[:, :, :PADDED], g6[None, :, :PADDED]], axis=0))
        ctx_nb, g7, h6 = together(ctx_nb, g7, h6)
        e7 = by_x(g7[:, :PADDED])
        h6, h35, e356, ctx_nb = together(h6, h35, e356, ctx_nb)
        h7 = by_y(h6)
        arrays = (f0, f1, g2, g4, g35, g6, g7, h2, h4, h35, h6, h7, w_other, e124, e356, e7)
        wide_at = ((0, None), (1, None), (2, None), (4, 0), (3, None), (4, 1), (5, None), (6, None))
        mine_at = tuple((array, lead, 0) for array, lead in wide_at)
        out_pieces = (arrays[:7], tuple((array, lead, PADDED) for array, lead in wide_at))
        down_at = ((0, None, PADDED + WIDTH), (1, None, PADDED + WIDTH)) + tuple(
            (array, lead, 0) for array, lead in ((7, None), (9, 0), (8, None), (9, 1), (10, None), (11, None))
        )
        other_at = tuple(
            (array, lead, 0)
            for array, lead in
            ((12, None), (13, 0), (13, 1), (14, 0), (13, 2), (14, 1), (14, 2), (15, None))
        )
    else:
        x1, x3 = by_core(x0), by_core(x2)
        gather = lambda value: lax.all_gather(value, "shard", axis=0, tiled=True)
        alone = ((0, None, 0),)
        first_low, q, k, v, w_full, gains = qkv_call(
            count,
            idx,
            (x0, x1, x2, x3),
            ((gather(w_qkv),), alone),
            jnp.stack([gather(attn_gain), gather(mlp_gain)]),
            cosine,
            sine,
        )
        arrays = (gather(w_mine), gather(w_down))
        arrays += (by_x(arrays[0]),)
        out_pieces = ((gather(out_weight),), alone)
        mine_at, down_at, other_at = alone, ((1, None, 0),), ((2, None, 0),)
        (ctx_fa, lse_fa), (ctx_fb, lse_fb) = attend(q, k, v, 2), attend(q, k, v, 3)
        other = by_x(jnp.concatenate([ctx_fa, ctx_fb], axis=0))
        (ctx_na, lse_na), (ctx_nb, lse_nb) = attend(q, k, v, 0), attend(q, k, v, 1)
    c1 = by_core(c0)

    near, far = (ctx_na, ctx_nb), (ctx_fa, ctx_fb)
    lse_near, lse_far = (lse_na, lse_nb), (lse_fa, lse_fb)
    out_own, w_sel = out_call(count, idx, near, other, out_pieces)
    out_core = by_core(out_own)
    second_low, hidden, gate_up_grad, second_own, w_down_full = mlp_call(
        count, idx, x0, x1, out_own, out_core, c0, c1, gains, arrays, mine_at, other_at, down_at
    )
    second_core = by_core(second_own)
    wide = list(wide_call(count, idx, second_low, gate_up_grad))
    wide[-1], second_core = together(wide[-1], second_core)
    res, res_low, grad_near, grad_other, gain_two = norm_two_call(
        x0, x1, out_own, out_core, second_own, second_core, c0, c1, gains, w_sel
    )
    grad_far = by_x(grad_other)
    down_other, down_mine, late_keep, late_send = down_call(
        count, idx, hidden, w_down_full, c0, c1, near, other, res_low
    )
    if eight:
        wide_keep, wide_send = wide
        wide_got = by_y(wide_send)
    part = lambda half, pair, grads, earlier=None: attend_back(
        half, pair, q, grads, (near, far)[half], (lse_near, lse_far)[half], k, v, cosine, sine, earlier
    )
    late_send, down_mine, grad_near, grad_far = together(late_send, down_mine, grad_near, grad_far)
    down_core = by_core(down_other)
    late_got = by_x(late_send)
    q_n0, dk0, dv0 = part(0, 0, grad_near)
    q_n0, grad_near, down_core = together(q_n0, grad_near, down_core)
    q_n1, dk1, dv1 = part(0, 1, grad_near)
    q_n1, grad_far = together(q_n1, grad_far)
    q_f0, k0, v0 = part(1, 0, grad_far, (dk0, dv0))
    if eight:
        q_f0, late_got, wide_got, grad_far = together(q_f0, late_got, wide_got, grad_far)
        late_mine = plus(late_keep[:4], late_got[:4])
        late_got = by_y(plus(late_keep[4:], late_got[4:]))
        wide_mine = plus(wide_keep[0], wide_got[0])
        wide_got = by_x(plus(wide_keep[1], wide_got[1]))
    raw0 = (q_n0, q_f0, k0, v0)
    *terms0, gain_a = qkv_grad_call(count, idx, first_low, raw0, w_full, gains, 0)
    if eight:
        terms0[0], terms0[1], grad_far = together(terms0[0], terms0[1], grad_far)
        terms0_got = by_y(terms0[1])
    q_f1, k1, v1 = part(1, 1, grad_far, (dk1, dv1))
    raw1 = (q_n1, q_f1, k1, v1)
    first_core = back_project((raw0, raw1), w_full, 1)
    if eight:
        first_core, q_f1, late_got, terms0_got, wide_got = together(
            first_core, q_f1, late_got, terms0_got, wide_got
        )
        first_got = by_core(first_core)
        late_next = by_z(plus(late_mine[2:], late_got[2:]))
        terms0_next = by_z(plus(terms0[0][2:], terms0_got[2:]))
        wide_next = by_z(plus(wide_mine[2:], wide_got[2:]))
    else:
        first_got = by_core(first_core)
    raw1 = (q_n1, q_f1, k1, v1)
    *terms1, gain_b = qkv_grad_call(count, idx, first_low, raw1, w_full, gains, 1)
    if eight:
        terms1[0], terms1[1], first_got, q_f1 = together(terms1[0], terms1[1], first_got, q_f1)
        terms1_got = by_y(terms1[1])
        raw1 = (q_n1, q_f1, k1, v1)
    first_own = back_project((raw0, raw1), w_full, 0)
    gain_terms = jnp.concatenate([gain_a[:1] + gain_b[:1], gain_two[:1]], axis=0)
    final = lambda mine, got: mine.astype(f32) + got.astype(f32)
    if eight:
        first_own, late_next, terms0_next, gain_terms = together(
            first_own, late_next, terms0_next, gain_terms
        )
        first_far = by_x(plus(first_own[1], first_got[1]))
        late_mine = plus(late_mine[:2], late_got[:2])
        terms0_mine = plus(terms0[0][:2], terms0_got[:2])
        late_last = by_zz(plus(late_mine[1], late_next[1]))
        terms0_last = by_zz(plus(terms0_mine[1], terms0_next[1]))
        gain_terms = gain_terms + by_core(gain_terms)
        terms1_got, wide_next, gain_terms = together(terms1_got, wide_next, gain_terms)
        terms1_next = by_z(plus(terms1[0][2:], terms1_got[2:]))
        terms1_mine = plus(terms1[0][:2], terms1_got[:2])
        wide_mine = plus(wide_mine[:2], wide_got[:2])
        wide_last = by_zz(plus(wide_mine[1], wide_next[1]))
        gain_terms = gain_terms + by_y(gain_terms)
        late_total = final(plus(late_mine[0], late_next[0]), late_last)
        terms1_next, late_total, terms0_last, gain_terms, down_core = together(
            terms1_next, late_total, terms0_last, gain_terms, down_core
        )
        gain_terms = gain_terms + by_z(gain_terms)
        terms1_last = by_zz(plus(terms1_mine[1], terms1_next[1]))
        gain_terms, first_far = together(gain_terms, first_far)
        gain_terms = gain_terms + by_x(gain_terms)
        gain_terms = gain_terms + by_zz(gain_terms)
        wide_total = final(plus(wide_mine[0], wide_next[0]), wide_last)
        totals = [
            final(plus(terms0_mine[0], terms0_next[0]), terms0_last),
            final(plus(terms1_mine[0], terms1_next[0]), terms1_last),
        ]
    else:
        first_far = by_x(plus(first_own[1], first_got[1]))
        wide_sum = plus(wide[0][0, 0], by_x(wide[0][1, 0]))
        scatter = lambda value, dim: lax.psum_scatter(
            value, "shard", scatter_dimension=dim, tiled=True
        ).astype(f32)
        wide_total = scatter(wide_sum, 0)
        late_total = scatter(plus(late_keep, late_got)[0], 1)
        totals = [scatter(terms[0][0], 0) for terms in (terms0, terms1)]
        gain_terms = lax.psum(gain_terms, ("seq", "shard"))
    result = (
        x0.astype(f32)
        + out_own[:rows].astype(f32)
        + out_core[rows:].astype(f32)
        + down_mine.astype(f32)
        + down_core.astype(f32)
    ).astype(bf16)[None]
    input_grad = norm_one_call(x0, res, first_own, first_got, first_far, gains)[None]
    down_total, out_total = late_total[:BLOCK], late_total[BLOCK:]
    moved = lax.ppermute(down_total.astype(bf16), "seq", [(1, 2), (2, 1)]).astype(f32)
    down_total = jnp.where((seq == 1) | (seq == 2), moved, down_total)
    take = width // (4 * shards)
    gain_out = lax.dynamic_slice_in_dim(gain_terms, (seq * shards + shard) * take, take, 1)
    qkv_out = jnp.stack(
        [
            jnp.concatenate([total[:, at * 128 : (at + 1) * 128] for total in totals], axis=1)
            for at in range(3)
        ]
    )
    return (
        result,
        input_grad,
        gain_out[0],
        qkv_out,
        out_total,
        gain_out[1],
        wide_total[:, :HALF],
        down_total,
    )


def solution(mesh):
    placed = (
        P("shard", "seq", None),
        P("shard"),
        P(None, "shard", None),
        P("shard", None),
        P("shard"),
        P("shard", None),
        P(None, "shard"),
        P("shard", "seq", None),
    )
    return jax.shard_map(
        per_device,
        mesh=mesh,
        in_specs=placed,
        out_specs=(
            P("shard", "seq", None),
            P("shard", "seq", None),
            P(("seq", "shard")),
            P(None, "shard", "seq"),
            P("seq", "shard"),
            P(("seq", "shard")),
            P("shard", "seq"),
            P("seq", "shard"),
        ),
        check_vma=False,
    )
```

```python
from functools import partial
import math

import jax
import jax.numpy as jnp
from jax import lax
from jax.experimental import pallas as pl
from jax.experimental.pallas import tpu as pltpu
from jax.sharding import PartitionSpec as P

HEADS = 16
HD = 64
FF = 2624

epsilon = 1e-05
rope_base = 160000.0

f32 = jnp.float32
bf16 = jnp.bfloat16

WIDTH = 1024
HALF = FF // 2
PADDED = 1408
BLOCK = FF // 4
COLS = 256
CHUNKS = (0, 4, 2, 6, 1, 5, 3, 7)
SPLIT = 768
EXTRA = 16
ROWS_BY_COLS = (((0,), (0,)), ((), ()))
COLS_BY_COLS = (((1,), (1,)), ((), ()))
VMEM_LIMIT = 58 * 1024 * 1024

ANY = pl.BlockSpec(memory_space=pl.ANY)
SMEM = pl.BlockSpec(memory_space=pltpu.SMEM)


def cost(micros):
    return pl.CostEstimate(flops=int(micros), transcendentals=0, bytes_accessed=int(micros))


def params():
    return pltpu.CompilerParams(vmem_limit_bytes=VMEM_LIMIT)


def sds(shape, dtype=bf16):
    return jax.ShapeDtypeStruct(shape, dtype)


def aligned(index, size):
    return pl.ds(pl.multiple_of(index * size, size), size)


def normalize(values):
    center = values - jnp.mean(values, axis=-1, keepdims=True)
    inv_scale = lax.rsqrt(jnp.mean(center * center, axis=-1, keepdims=True) + epsilon)
    return center * inv_scale, inv_scale


def norm_back(grads, xhat, inv_scale):
    mean_grad = jnp.mean(grads, axis=-1, keepdims=True)
    mean_both = jnp.mean(grads * xhat, axis=-1, keepdims=True)
    return inv_scale * (grads - mean_grad - xhat * mean_both)


def turned(values):
    lane = lax.broadcasted_iota(jnp.int32, values.shape, 1)
    width = values.shape[1]
    return jnp.where(
        lane % HD < HD // 2, pltpu.roll(values, width - HD // 2, 1), pltpu.roll(values, HD // 2, 1)
    )


def twice(table):
    return jnp.concatenate([table, table], axis=1)


def piece_of(refs, place, rows=None, width=None):
    array, lead, column = place
    index = () if lead is None else (lead,)
    rows = slice(None) if rows is None else rows
    cols = slice(None) if width is None else pl.ds(column, width)
    return refs[array].at[(*index, rows, cols)]


def fetch_rows(count, idx, refs, places, width, target, sem):
    size = target.shape[0] // count
    copies = []
    for r in range(count):
        rows = aligned(idx[4 + r], size) if count > 1 else pl.ds(0, size)
        copies.append(
            pltpu.make_async_copy(piece_of(refs, places[r], width=width), target.at[rows], sem.at[r])
        )
    return copies


def qkv_kernel(count, places, idx, *refs):
    x_refs, refs = refs[:4], refs[4:]
    n_arrays = 1 + max(array for array, _, _ in places)
    w_refs, refs = refs[:n_arrays], refs[n_arrays:]
    if count == 1:
        gain_ref, refs = refs[0], refs[1:]
    cos_ref, sin_ref, fn_o, q_o, k_o, v_o, w_o, g_o, xs, gs, semx, semw, semg = refs
    step = pl.program_id(0)
    shard = idx[0]
    size = WIDTH // count

    def x_copy(r):
        return pltpu.make_async_copy(x_refs[r], xs.at[r], semx.at[r])

    def w_copy(r):
        return pltpu.make_async_copy(
            piece_of(w_refs, places[r], rows=pl.ds(0, size)), w_o.at[aligned(jnp.bitwise_xor(shard, r), size)], semw.at[r]
        )

    def g_copy(r):
        return pltpu.make_async_copy(
            piece_of(w_refs, places[r], rows=pl.ds(size, EXTRA)), gs.at[jnp.bitwise_xor(shard, r)], semg.at[r]
        )

    @pl.when(step == 0)
    def _():
        if count == 1:
            w_all = pltpu.make_async_copy(w_refs[0], w_o, semw.at[0])
            w_all.start()
        else:
            for r in range(count):
                w_copy(r).start()
                g_copy(r).start()
        for r in range(4):
            x_copy(r).start()
        if count == 1:
            w_all.wait()
            g_o[0:1] = gain_ref[0:1].astype(f32)
            g_o[1:2] = gain_ref[1:2].astype(f32)
        else:
            for r in range(count):
                w_copy(r).wait()
                g_copy(r).wait()
            for r in range(count):
                part = gs[r].astype(f32)
                g_o[0:1, r * size : (r + 1) * size] = part[0:1, 0:size]
                g_o[1:2, r * size : (r + 1) * size] = part[0:1, size : 2 * size]

    for r in range(4):

        @pl.when(step == r)
        def _():
            x_copy(r).wait()

    xhat, _ = normalize(xs[step].astype(f32))
    first_low = (xhat * g_o[0:1]).astype(bf16)
    fn_o[...] = first_low
    cosine, sine = twice(cos_ref[...]), twice(sin_ref[...])
    outs = (q_o, k_o, v_o)
    for part in range(3):
        value = jnp.dot(first_low, w_o[:, part * COLS : (part + 1) * COLS], preferred_element_type=f32)
        if part < 2:
            value = value * cosine + turned(value) * sine
        value = value.astype(bf16)
        if part == 0:
            value = value * jnp.asarray(1.0 / math.sqrt(HD), bf16)
        outs[part][...] = value


def qkv_call(count, idx, chunks, pieces, gains, cosine, sine):
    arrays, where = pieces
    rows = chunks[0].shape[0]
    by_step = lambda width: pl.BlockSpec((rows, width), lambda r: (r, 0))
    whole = lambda shape: pl.BlockSpec(shape, lambda r: (0, 0))
    extra = [] if count > 1 else [gains]
    return pl.pallas_call(
        partial(qkv_kernel, count, where),
        grid=(4,),
        in_specs=[SMEM]
        + [ANY] * (4 + len(arrays))
        + ([] if count > 1 else [whole((2, WIDTH))])
        + [by_step(128), by_step(128)],
        out_specs=[
            by_step(WIDTH),
            by_step(COLS),
            by_step(COLS),
            by_step(COLS),
            whole((WIDTH, 3 * COLS)),
            whole((8, WIDTH)),
        ],
        out_shape=[
            sds((4 * rows, WIDTH)),
            sds((4 * rows, COLS)),
            sds((4 * rows, COLS)),
            sds((4 * rows, COLS)),
            sds((WIDTH, 3 * COLS)),
            sds((8, WIDTH), f32),
        ],
        scratch_shapes=[
            pltpu.VMEM((4, rows, WIDTH), bf16),
            pltpu.VMEM((8, EXTRA, 3 * COLS), bf16),
            pltpu.SemaphoreType.DMA((4,)),
            pltpu.SemaphoreType.DMA((count,)),
            pltpu.SemaphoreType.DMA((count,)),
        ],
        compiler_params=params(),
        cost_estimate=cost(11),
        name="project",
    )(idx, *chunks, *arrays, *extra, cosine, sine)


def head_of(shape):
    return lax.broadcasted_iota(jnp.int32, shape, len(shape) - 1) // HD


def attend_kernel(q_ref, k_ref, v_ref, o_ref, lse_ref):
    q, k, v = q_ref[...], k_ref[...], v_ref[...]
    heads = head_of(q.shape)
    total = jnp.zeros(q.shape, f32)
    lses = jnp.zeros((q.shape[0], 128), f32)
    lane = lax.broadcasted_iota(jnp.int32, lses.shape, 1)
    for h in range(COLS // HD):
        q_h = jnp.where(heads == h, q, jnp.zeros_like(q))
        scores = lax.dot_general(q_h, k, COLS_BY_COLS, preferred_element_type=f32)
        row_max = jnp.max(scores, axis=1, keepdims=True)
        exponent = jnp.exp(scores - row_max)
        row_total = jnp.sum(exponent, axis=1, keepdims=True)
        context = jnp.dot(exponent.astype(bf16), v, preferred_element_type=f32)
        total = jnp.where(heads == h, context * (1.0 / row_total), total)
        lses = jnp.where(lane == h, row_max + jnp.log(row_total), lses)
    o_ref[...] = total.astype(bf16)
    lse_ref[...] = lses.T[:8]


def attend(q, k, v, chunk, after=()):
    span = k.shape[0]
    rows = span // 4
    kept = pl.BlockSpec((span, COLS), lambda i: (0, 0))
    return pl.pallas_call(
        lambda *refs: attend_kernel(*refs[:3], *refs[3 + len(after) :]),
        grid=(1,),
        in_specs=[pl.BlockSpec((rows, COLS), lambda i: (chunk, 0)), kept, kept] + [ANY] * len(after),
        out_specs=[
            pl.BlockSpec((rows, COLS), lambda i: (0, 0)),
            pl.BlockSpec((8, rows), lambda i: (0, 0)),
        ],
        out_shape=[sds((rows, COLS)), sds((8, rows), f32)],
        compiler_params=params(),
        cost_estimate=cost(8),
        name="attend",
    )(q, k, v, *after)


def attend_back_kernel(last, pair, *refs):
    q_ref, do_ref, oa_ref, ob_ref, la_ref, lb_ref, k_ref, v_ref, qcos, qsin, refs = *refs[:10], refs[10:]
    if last:
        dk_i, dv_i, kcos, ksin, refs = *refs[:4], refs[4:]
    dq_ref, dk_ref, dv_ref, do_s, inner_s, lse_s, dq_s = refs
    step = pl.program_id(0)
    width = q_ref.shape[1]
    n_heads = width // HD

    @pl.when(step == 0)
    def _():
        do = do_ref[...]
        context = jnp.concatenate([oa_ref[...], ob_ref[...]], axis=0)
        product = do.astype(f32) * context.astype(f32)
        high = product.astype(bf16)
        rest = (product - high.astype(f32)).astype(bf16)
        chosen = (
            head_of((8, width)) == lax.broadcasted_iota(jnp.int32, (8, width), 0)
        ).astype(bf16)
        inner_s[...] = lax.dot_general(
            chosen, high, COLS_BY_COLS, preferred_element_type=f32
        ) + lax.dot_general(chosen, rest, COLS_BY_COLS, preferred_element_type=f32)
        lse_s[...] = jnp.concatenate([la_ref[...], lb_ref[...]], axis=1)
        heads = head_of(do.shape)
        for h in range(n_heads):
            do_s[h] = jnp.where(heads == h, do, jnp.zeros_like(do))
        dq_s[...] = jnp.zeros_like(dq_s)

    q, k, v = q_ref[...], k_ref[...], v_ref[...]
    heads = head_of(k.shape)
    dk = jnp.zeros(k.shape, f32)
    dv = jnp.zeros(k.shape, f32)
    dq = dq_s[...]
    for h in range(n_heads):
        at = n_heads * pair + h
        k_h = jnp.where(heads == h, k, jnp.zeros_like(k))
        scores = lax.dot_general(k_h, q, COLS_BY_COLS, preferred_element_type=f32)
        probs = jnp.exp(scores - lse_s[at : at + 1, :])
        probs_grad = lax.dot_general(v, do_s[h], COLS_BY_COLS, preferred_element_type=f32)
        scores_grad = (probs * (probs_grad - inner_s[h : h + 1, :])).astype(bf16)
        dv = dv + jnp.dot(probs.astype(bf16), do_s[h], preferred_element_type=f32)
        dk = jnp.where(heads == h, jnp.dot(scores_grad, q, preferred_element_type=f32), dk)
        dq = dq + lax.dot_general(scores_grad, k_h, ROWS_BY_COLS, preferred_element_type=f32)
    dq_s[...] = dq
    if last:
        dk = dk + dk_i[...]
        dv = dv + dv_i[...]
        dk_ref[...] = (dk * kcos[...] - turned(dk) * ksin[...]).astype(bf16)
        dv_ref[...] = dv.astype(bf16)
    else:
        dk_ref[...] = dk
        dv_ref[...] = dv

    @pl.when(step == pl.num_programs(0) - 1)
    def _():
        dq = dq_s[...] * (1.0 / math.sqrt(HD))
        dq_ref[...] = (dq * qcos[...] - turned(dq) * qsin[...]).astype(bf16)


def attend_back(part, pair, q, do, contexts, lses, k, v, cosine, sine, earlier=None, after=(), tile=512):
    span = k.shape[0]
    rows = do.shape[0]
    last = earlier is not None
    rows_at = lambda at, col, count=rows, width=128: pl.BlockSpec((count, width), lambda i: (at, col))
    keys = lambda col: pl.BlockSpec((tile, 128), lambda i: (i, col))
    grads = bf16 if last else f32
    n_in = 10 + (4 if last else 0)
    return pl.pallas_call(
        lambda *refs: attend_back_kernel(last, pair, *refs[:n_in], *refs[n_in + len(after) :]),
        grid=(span // tile,),
        in_specs=[
            rows_at(part, pair),
            rows_at(0, pair),
            rows_at(0, pair, rows // 2),
            rows_at(0, pair, rows // 2),
            rows_at(0, 0, 8, rows // 2),
            rows_at(0, 0, 8, rows // 2),
            keys(pair),
            keys(pair),
            rows_at(part, 0),
            rows_at(part, 0),
        ]
        + ([keys(0), keys(0), keys(0), keys(0)] if last else [])
        + [ANY] * len(after),
        out_specs=[rows_at(0, 0), keys(0), keys(0)],
        out_shape=[sds((rows, 128)), sds((span, 128), grads), sds((span, 128), grads)],
        scratch_shapes=[
            pltpu.VMEM((128 // HD, rows, 128), bf16),
            pltpu.VMEM((8, rows), f32),
            pltpu.VMEM((8, rows), f32),
            pltpu.VMEM((rows, 128), f32),
        ],
        compiler_params=params(),
        cost_estimate=cost(15),
        name="attend_back",
    )(q, do, *contexts, *lses, k, v, cosine, sine, *((*earlier, cosine, sine) if last else ()), *after)


def out_kernel(count, places, idx, ma_ref, mb_ref, other_ref, *refs):
    w_refs, (o_ref, wsel_ref, w_s, sem) = refs[:-4], refs[-4:]
    copies = fetch_rows(count, idx, w_refs, places, WIDTH, w_s, sem)
    for copy in copies:
        copy.start()
    for copy in copies:
        copy.wait()
    seq = idx[1]
    wsel_ref[0:COLS] = w_s[aligned(seq, COLS)]
    wsel_ref[COLS:] = w_s[aligned(jnp.bitwise_xor(seq, 2), COLS)]
    rows = ma_ref.shape[0]
    for r, mine in enumerate((ma_ref, mb_ref)):
        both = jnp.concatenate([mine[...], other_ref[r * rows : (r + 1) * rows]], axis=1)
        value = jnp.dot(both, wsel_ref[...], preferred_element_type=f32)
        o_ref[r * rows : (r + 1) * rows] = value.astype(bf16)


def out_call(count, idx, mine, other, pieces):
    vmem = pl.BlockSpec(memory_space=pltpu.VMEM)
    arrays, where = pieces
    return pl.pallas_call(
        partial(out_kernel, count, where),
        in_specs=[SMEM] + [vmem] * 3 + [ANY] * len(arrays),
        out_specs=[vmem, vmem],
        out_shape=[sds((2 * mine[0].shape[0], WIDTH)), sds((2 * COLS, WIDTH))],
        scratch_shapes=[pltpu.VMEM((WIDTH, WIDTH), bf16), pltpu.SemaphoreType.DMA((count,))],
        compiler_params=params(),
        cost_estimate=cost(5),
        name="out_project",
    )(idx, *mine, other, *arrays)


def mlp_kernel(count, n_arrays, mine, other, down, idx, *refs):
    x0, x1, po, pr, c0, c1, g_ref, refs = *refs[:7], refs[7:]
    w_refs, refs = refs[:n_arrays], refs[n_arrays:]
    sn_o, hid_o, gug_o, sgp_o, wd_o, refs = *refs[:5], refs[5:]
    xs, pos, prs, cs, wi, wd, sn_s, hid_s, gug_s, sgp_s, sem_a, sem_m, sem_i, sem_d, sem_o = refs
    x_place = idx[2]
    rows = xs.shape[1]
    loads = [
        pltpu.make_async_copy(x0, xs.at[0], sem_a.at[0]),
        pltpu.make_async_copy(x1, xs.at[1], sem_a.at[1]),
        pltpu.make_async_copy(po, pos, sem_a.at[2]),
        pltpu.make_async_copy(pr, prs, sem_a.at[3]),
        pltpu.make_async_copy(c0, cs.at[pl.ds(0, rows)], sem_a.at[4]),
        pltpu.make_async_copy(c1, cs.at[pl.ds(rows, rows)], sem_a.at[5]),
    ]
    here = wi.at[:, aligned(x_place, PADDED)]
    there = wi.at[:, aligned(1 - x_place, PADDED)]
    wi_loads = fetch_rows(count, idx, w_refs, mine, PADDED, here, sem_m)
    wi_loads += fetch_rows(count, idx, w_refs, other, PADDED, there, sem_i)
    wd_loads = fetch_rows(count, idx, w_refs, down, PADDED, wd, sem_d)
    for copy in loads[:4] + wi_loads + loads[4:] + wd_loads:
        copy.start()
    for copy in loads[:4]:
        copy.wait()
    for r in range(2):
        here, there = pl.ds(r * rows, rows), pl.ds((1 - r) * rows, rows)
        after = xs[r].astype(f32) + pos[here].astype(f32) + prs[there].astype(f32)
        xhat, _ = normalize(after)
        sn_s[here] = (xhat * g_ref[1:2]).astype(bf16)
    stores = []

    def store(source, target, k):
        copy = pltpu.make_async_copy(source, target, sem_o.at[k])
        copy.start()
        stores.append(copy)

    store(sn_s, sn_o, 0)
    for copy in wi_loads + loads[4:] + wd_loads:
        copy.wait()
    store(wd, wd_o, 1)
    start = 0
    while start < PADDED:
        size = min(256, PADDED - start)
        here = pl.ds(start, size)
        gate = jnp.dot(sn_s[...], wi[:, here], preferred_element_type=f32)
        up = jnp.dot(sn_s[...], wi[:, pl.ds(PADDED + start, size)], preferred_element_type=f32)
        back = jnp.dot(cs[...], wd[:, here], preferred_element_type=f32)
        below = 0.5 * (1.0 + lax.erf(gate * math.sqrt(0.5)))
        density = jnp.exp(-0.5 * gate * gate) * (1.0 / math.sqrt(2.0 * math.pi))
        unit = gate * below
        hid_s[:, here] = (unit * up).astype(bf16)
        gug_s[0, :, here] = (back * up * (below + gate * density)).astype(bf16)
        gug_s[1, :, here] = (back * unit).astype(bf16)
        start += size
    store(hid_s, hid_o, 2)
    store(gug_s, gug_o, 3)
    value = lax.dot_general(gug_s[0], wi[:, :PADDED], COLS_BY_COLS, preferred_element_type=f32)
    value = value + lax.dot_general(gug_s[1], wi[:, PADDED:], COLS_BY_COLS, preferred_element_type=f32)
    sgp_s[...] = value.astype(bf16)
    store(sgp_s, sgp_o, 4)
    for copy in stores:
        copy.wait()


def mlp_call(count, idx, x0, x1, po, pr, c0, c1, gains, arrays, mine, other, down):
    rows = x0.shape[0]
    return pl.pallas_call(
        partial(mlp_kernel, count, len(arrays), mine, other, down),
        in_specs=[SMEM] + [ANY] * 6 + [pl.BlockSpec(memory_space=pltpu.VMEM)] + [ANY] * len(arrays),
        out_specs=[ANY] * 5,
        out_shape=[
            sds((2 * rows, WIDTH)),
            sds((2 * rows, PADDED)),
            sds((2, 2 * rows, PADDED)),
            sds((2 * rows, WIDTH)),
            sds((WIDTH, PADDED)),
        ],
        scratch_shapes=[
            pltpu.VMEM((2, rows, WIDTH), bf16),
            pltpu.VMEM((2 * rows, WIDTH), bf16),
            pltpu.VMEM((2 * rows, WIDTH), bf16),
            pltpu.VMEM((2 * rows, WIDTH), bf16),
            pltpu.VMEM((WIDTH, 2 * PADDED), bf16),
            pltpu.VMEM((WIDTH, PADDED), bf16),
            pltpu.VMEM((2 * rows, WIDTH), bf16),
            pltpu.VMEM((2 * rows, PADDED), bf16),
            pltpu.VMEM((2, 2 * rows, PADDED), bf16),
            pltpu.VMEM((2 * rows, WIDTH), bf16),
            pltpu.SemaphoreType.DMA((6,)),
            pltpu.SemaphoreType.DMA((count,)),
            pltpu.SemaphoreType.DMA((count,)),
            pltpu.SemaphoreType.DMA((count,)),
            pltpu.SemaphoreType.DMA((5,)),
        ],
        compiler_params=params(),
        cost_estimate=cost(25),
        name="feed_forward",
    )(idx, x0, x1, po, pr, c0, c1, gains, *arrays)


def down_kernel(count, idx, hid_ref, wd_ref, c0, c1, ma, mb, other, low, res_other, res_mine, *refs):
    outs, downs, acc = refs[:2], refs[2:-1], refs[-1]
    shard, x_place = idx[0], idx[2]
    rows = c0.shape[0]
    width = WIDTH // count
    places = [
        aligned(jnp.bitwise_xor(shard, r), width) if count > 1 else pl.ds(0, width) for r in CHUNKS[:count]
    ]
    acc[...] = lax.dot_general(
        hid_ref[0:rows], c0[...], ROWS_BY_COLS, preferred_element_type=f32
    ) + lax.dot_general(hid_ref[rows:], c1[...], ROWS_BY_COLS, preferred_element_type=f32)
    for part in range(2):
        here = pl.ds(pl.multiple_of(jnp.bitwise_xor(x_place, part) * BLOCK, 8), BLOCK)
        for r in range(count):
            downs[r // 4][part, r % 4] = acc[here, places[r]].astype(bf16)
    mine = jnp.concatenate([ma[...], mb[...]], axis=0)
    for part, context in enumerate((mine, other[...])):
        acc[0:COLS] = lax.dot_general(context, low[...], ROWS_BY_COLS, preferred_element_type=f32)
        for r in range(count):
            outs[part][r] = acc[0:COLS, places[r]].astype(bf16)
    for r, target in ((1, res_other), (0, res_mine)):
        target[...] = lax.dot_general(
            hid_ref[r * rows : (r + 1) * rows], wd_ref[...], COLS_BY_COLS, preferred_element_type=f32
        ).astype(bf16)


def down_call(count, idx, hidden, wd, c0, c1, mine, other, low):
    rows = c0.shape[0]
    split = 2 if count > 1 else 1
    vmem = pl.BlockSpec(memory_space=pltpu.VMEM)
    return pl.pallas_call(
        partial(down_kernel, count),
        in_specs=[SMEM] + [vmem] * 8,
        out_specs=[vmem] * (4 + split),
        out_shape=[sds((rows, WIDTH))] * 2
        + [sds((count, COLS, WIDTH // count))] * 2
        + [sds((2, count // split, BLOCK, WIDTH // count))] * split,
        scratch_shapes=[pltpu.VMEM((PADDED, WIDTH), f32)],
        compiler_params=params(),
        cost_estimate=cost(15),
        name="down_project",
    )(idx, hidden, wd, c0, c1, *mine, other, low)


def norm_two_kernel(x0, x1, po, pr, so, sr, c0, c1, g_ref, wsel, res_o, low_o, mine_o, other_o, gain_o):
    step = pl.program_id(0)
    half = pl.num_programs(0) // 2
    first = step < half
    gain = g_ref[1:2]
    x = jnp.where(first, x0[...], x1[...])
    c = jnp.where(first, c0[...], c1[...])
    after = x.astype(f32) + po[...].astype(f32) + pr[...].astype(f32)
    xhat, inv_scale = normalize(after)
    second = so[...].astype(f32) + sr[...].astype(f32)
    res = c.astype(f32) + norm_back(second * gain, xhat, inv_scale)

    @pl.when(step == 0)
    def _():
        gain_o[...] = jnp.zeros_like(gain_o)

    @pl.when(first)
    def _():
        res_o[...] = res
        gain_o[...] += jnp.sum(second * xhat, axis=0, keepdims=True)

    low = res.astype(bf16)
    low_o[...] = low
    value = lax.dot_general(low, wsel[...], COLS_BY_COLS, preferred_element_type=f32).astype(bf16)
    mine_o[...] = value[:, :COLS]
    other_o[...] = value[:, COLS:]


def norm_two_call(x0, x1, po, pr, so, sr, c0, c1, gains, wsel, half=2):
    rows = x0.shape[0]
    size = rows // half
    spec = lambda width, at: pl.BlockSpec((size, width), lambda s: (at(s), 0))
    lower = lambda s: jnp.minimum(s, half - 1)
    upper = lambda s: jnp.maximum(s - half, 0)
    same = lambda s: s
    other = lambda s: lax.rem(s + half, 2 * half)
    whole = lambda shape: pl.BlockSpec(shape, lambda s: (0, 0))
    return pl.pallas_call(
        norm_two_kernel,
        grid=(2 * half,),
        in_specs=[
            spec(WIDTH, lower),
            spec(WIDTH, upper),
            spec(WIDTH, same),
            spec(WIDTH, other),
            spec(WIDTH, same),
            spec(WIDTH, other),
            spec(WIDTH, lower),
            spec(WIDTH, upper),
            whole((8, WIDTH)),
            whole((2 * COLS, WIDTH)),
        ],
        out_specs=[
            spec(WIDTH, lower),
            spec(WIDTH, same),
            spec(COLS, same),
            spec(COLS, same),
            whole((8, WIDTH)),
        ],
        out_shape=[
            sds((rows, WIDTH), f32),
            sds((2 * rows, WIDTH)),
            sds((2 * rows, COLS)),
            sds((2 * rows, COLS)),
            sds((8, WIDTH), f32),
        ],
        compiler_params=params(),
        cost_estimate=cost(8),
        name="norm_two_back",
    )(x0, x1, po, pr, so, sr, c0, c1, gains, wsel)


def wide_kernel(count, idx, sn_ref, gug_ref, *refs):
    shard = idx[0]
    part = pl.program_id(0)
    size = WIDTH // count
    if count == 1:
        out, acc = refs
        acc[...] = lax.dot_general(sn_ref[...], gug_ref[0], ROWS_BY_COLS, preferred_element_type=f32)
        out[0, 0] = acc[...].astype(bf16)
        return
    keep_a, send_a, keep_b, send_b, acc = refs
    acc[...] = lax.dot_general(sn_ref[...], gug_ref[0], ROWS_BY_COLS, preferred_element_type=f32)
    for k, r in enumerate(CHUNKS):
        place = aligned(jnp.bitwise_xor(shard, r), size)
        (keep_a, send_a)[k // 4][0, k % 4] = acc[place, :SPLIT].astype(bf16)

    def store(target):
        for k, r in enumerate(CHUNKS):
            place = aligned(jnp.bitwise_xor(shard, r), size)
            target[k] = acc[place, SPLIT:].astype(bf16)

    @pl.when(part == 0)
    def _():
        store(keep_b)

    @pl.when(part == 1)
    def _():
        store(send_b)


def wide_call(count, idx, sn, gug):
    tokens = sn.shape[0]
    size = WIDTH // count
    spec = lambda shape, at: pl.BlockSpec(shape, at)
    whole = lambda shape: pl.BlockSpec(shape, lambda p, s: (0,) * len(shape))
    by_part = lambda shape: pl.BlockSpec((1, *shape[1:]), lambda p, s: (p, 0, 0, 0))
    first, second = (2, 4, size, SPLIT), (8, size, PADDED - SPLIT)
    alone = (2, 1, WIDTH, PADDED)
    grid_spec = pltpu.PrefetchScalarGridSpec(
        num_scalar_prefetch=1,
        grid=(2,),
        in_specs=[
            spec((tokens, WIDTH), lambda p, s: (0, 0)),
            spec((1, tokens, PADDED), lambda p, s: (jnp.bitwise_xor(p, s[2]), 0, 0)),
        ],
        out_specs=[by_part(first)] * 2 + [whole(second)] * 2 if count > 1 else [by_part(alone)],
        scratch_shapes=[pltpu.VMEM((WIDTH, PADDED), f32)],
    )
    return pl.pallas_call(
        partial(wide_kernel, count),
        grid_spec=grid_spec,
        out_shape=[sds(first)] * 2 + [sds(second)] * 2 if count > 1 else [sds(alone)],
        compiler_params=params(),
        cost_estimate=cost(12),
        name="wide_grad",
    )(idx, sn, gug)


def back_project_kernel(q0, q1, f0, f1, k0n, k1n, k0f, k1f, v0n, v1n, v0f, v1f, w_ref, both_o):
    for half, parts in (
        (1, (f0, f1, k0f, k1f, v0f, v1f)),
        (0, (q0, q1, k0n, k1n, v0n, v1n)),
    ):
        raw = jnp.concatenate([part[...] for part in parts], axis=1)
        both_o[half] = lax.dot_general(
            raw, w_ref[...], COLS_BY_COLS, preferred_element_type=f32
        ).astype(bf16)


def back_project(raw_pairs, w, chunk):
    rows = raw_pairs[0][0].shape[0] // 2
    at = lambda where: pl.BlockSpec((rows, 128), lambda i: (where, 0))
    q0, f0, k0, v0 = raw_pairs[0]
    q1, f1, k1, v1 = raw_pairs[1]
    return pl.pallas_call(
        back_project_kernel,
        grid=(1,),
        in_specs=[at(chunk)] * 6
        + [at(chunk + 2)] * 2
        + [at(chunk)] * 2
        + [at(chunk + 2)] * 2
        + [pl.BlockSpec((WIDTH, 3 * COLS), lambda i: (0, 0))],
        out_specs=pl.BlockSpec((2, rows, WIDTH), lambda i: (0, 0, 0)),
        out_shape=sds((2, rows, WIDTH)),
        compiler_params=params(),
        cost_estimate=cost(5),
        name="back_project",
    )(q0, q1, f0, f1, k0, k1, k0, k1, v0, v1, v0, v1, w)


def qkv_grad_kernel(count, idx, fn_ref, qn, qf, k_ref, v_ref, wq, wk, wv, g_ref, keep_o, *refs):
    if count > 1:
        send_o, gain_o, acc = refs
    else:
        gain_o, acc = refs
    rows = qn.shape[0]
    q = jnp.concatenate([qn[...], qf[...]], axis=0)
    raw = jnp.concatenate([q, k_ref[...], v_ref[...]], axis=1)
    acc[...] = lax.dot_general(fn_ref[...], raw, ROWS_BY_COLS, preferred_element_type=f32)
    shard = idx[0]
    size = WIDTH // count
    for k, r in enumerate(CHUNKS[:count]):
        place = aligned(jnp.bitwise_xor(shard, r), size) if count > 1 else pl.ds(0, size)
        target = (keep_o, send_o)[k // 4] if count > 1 else keep_o
        for part in range(3):
            value = acc[place, part * 128 : (part + 1) * 128]
            target[k % 4, part * size : (part + 1) * size] = value.astype(bf16)
    w = jnp.concatenate([wq[...], wk[...], wv[...]], axis=1)
    both = acc[...] * w.astype(f32)
    high = both.astype(bf16)
    rest = (both - high.astype(f32)).astype(bf16)
    ones = jnp.ones((8, w.shape[1]), bf16)
    total = lax.dot_general(ones, high, COLS_BY_COLS, preferred_element_type=f32)
    total += lax.dot_general(ones, rest, COLS_BY_COLS, preferred_element_type=f32)
    gain_o[...] = total / g_ref[0:1]


def qkv_grad_call(count, idx, first_low, raw, w, gains, pair):
    vmem = pl.BlockSpec(memory_space=pltpu.VMEM)
    split = 2 if count > 1 else 1
    size = WIDTH // count
    width = 3 * 128
    whole = lambda shape: pl.BlockSpec(shape, lambda i: (0,) * len(shape))
    weight = lambda part: pl.BlockSpec((WIDTH, 128), lambda i: (0, 2 * part + pair))
    grads = [(count // split, 3 * size, 128)] * split + [(8, WIDTH)]
    return pl.pallas_call(
        partial(qkv_grad_kernel, count),
        grid=(1,),
        in_specs=[SMEM, whole(first_low.shape)]
        + [whole(value.shape) for value in raw]
        + [weight(0), weight(1), weight(2), whole(gains.shape)],
        out_specs=[whole(shape) for shape in grads],
        out_shape=[sds(shape) for shape in grads[:-1]] + [sds(grads[-1], f32)],
        scratch_shapes=[pltpu.VMEM((WIDTH, width), f32)],
        compiler_params=params(),
        cost_estimate=cost(6),
        name="project_grad",
    )(idx, first_low, *raw, w, w, w, gains)


def norm_one_kernel(x_ref, res_ref, own, core, far, g_ref, o_ref):
    xhat, inv_scale = normalize(x_ref[...].astype(f32))
    first = own[0].astype(f32) + core[0].astype(f32) + far[...].astype(f32)
    o_ref[...] = res_ref[...] + norm_back(first * g_ref[0:1], xhat, inv_scale)


def norm_one_call(x, res, own, core, far, gains, steps=4):
    rows = x.shape[0]
    block = pl.BlockSpec((rows // steps, WIDTH), lambda i: (i, 0))
    return pl.pallas_call(
        norm_one_kernel,
        grid=(steps,),
        in_specs=[
            block,
            block,
            pl.BlockSpec((1, rows // steps, WIDTH), lambda i: (0, i, 0)),
            pl.BlockSpec((1, rows // steps, WIDTH), lambda i: (0, i, 0)),
            block,
            pl.BlockSpec((8, WIDTH), lambda i: (0, 0)),
        ],
        out_specs=block,
        out_shape=sds(res.shape, f32),
        compiler_params=params(),
        cost_estimate=cost(3),
        name="norm_one_back",
    )(x, res, own, core, far, gains)


def swap(value, axis, bits):
    size = lax.axis_size(axis)
    return lax.ppermute(value, axis, [(place, place ^ bits) for place in range(size)])


def plus(left, right):
    return (left.astype(f32) + right.astype(f32)).astype(bf16)


def together(*values):
    return lax.optimization_barrier(values)


def per_device(inputs, attn_gain, qkv_weight, out_weight, mlp_gain, in_weight, mlp_out, cotangent):
    _, rows, width = inputs.shape
    shards = lax.axis_size("shard")
    eight = shards == 8
    count = 8 if eight else 1
    piece = width // shards
    seq, shard = lax.axis_index("seq"), lax.axis_index("shard")
    x_place, core = seq // 2, seq % 2
    owners = [jnp.bitwise_xor(lax.rem(shard + 8 - 2 * (r % 4), 8), r // 4) for r in range(8)]
    idx = jnp.stack([shard, seq, x_place, core, *owners]).astype(jnp.int32)

    order = jnp.bitwise_xor(seq, jnp.arange(4))
    places = (order[:, None] * rows + jnp.arange(rows)[None, :]).reshape(-1)
    frequency = 1.0 / rope_base ** (jnp.arange(0, HD, 2, dtype=f32) / HD)
    angles = places.astype(f32)[:, None] * jnp.tile(frequency, 4)[None, :]
    sign = jnp.where(jnp.arange(128) % HD < HD // 2, -1.0, 1.0)
    cosine, sine = jnp.cos(angles), jnp.sin(angles) * sign

    x0 = inputs[0]
    c0 = cotangent[0]
    w_qkv = lax.dynamic_slice_in_dim(qkv_weight, seq * COLS, COLS, 2)
    w_qkv = jnp.transpose(w_qkv, (1, 0, 2)).reshape(piece, 3 * COLS)
    w_in = in_weight.reshape(piece, 2, 2, HALF)
    w_in = lax.dynamic_index_in_dim(w_in, core, 2, keepdims=False)
    w_in = jnp.pad(w_in, ((0, 0), (0, 0), (0, PADDED - HALF)))
    w_mine = lax.dynamic_index_in_dim(w_in, x_place, 1, keepdims=False)
    w_other = lax.dynamic_index_in_dim(w_in, 1 - x_place, 1, keepdims=False)
    w_down = lax.dynamic_slice_in_dim(mlp_out, core * HALF, HALF, 0).T
    w_down = jnp.pad(w_down, ((0, 0), (0, PADDED - HALF)))

    x2 = swap(x0, "seq", 2)
    by_y = lambda value: swap(value, "shard", 1)
    by_z = lambda value: swap(value, "shard", 2)
    by_zz = lambda value: swap(value, "shard", 4)
    by_x = lambda value: swap(value, "seq", 2)
    by_core = lambda value: swap(value, "seq", 1)
    if eight:
        gain_rows = jnp.concatenate([attn_gain, mlp_gain, jnp.zeros(3 * COLS - 2 * piece, bf16)])[None]
        a0 = jnp.concatenate([w_qkv, jnp.pad(gain_rows, ((0, EXTRA - 1), (0, 0)))], axis=0)
        f0 = jnp.concatenate([w_mine, out_weight, w_down], axis=1)
        g0, h0 = f0[:, : PADDED + WIDTH], f0[:, PADDED + WIDTH :]
        narrow = lambda value: value[..., :PADDED]
        ring = lambda value: lax.ppermute(
            value, "shard", [(place, (place + 2) % 8) for place in range(8)]
        )
        a4, a2, a1 = by_zz(a0), by_z(a0), by_y(a0)
        a4, a2, a1, x0, cosine, sine, idx, f0, g0, h0, w_other = together(
            a4, a2, a1, x0, cosine, sine, idx, f0, g0, h0, w_other
        )
        a6, a35 = by_z(a4), by_y(jnp.stack([a2, a4]))
        x1 = by_core(x0)
        a6, a35, x2 = together(a6, a35, x2)
        a7 = by_y(a6)
        x3 = by_core(x2)
        x3, x1, a7, f0, g0, h0 = together(x3, x1, a7, f0, g0, h0)
        g1, h1, f4 = ring(g0), ring(h0), by_y(f0)
        first_low, q, k, v, w_full, gains = qkv_call(
            count,
            idx,
            (x0, x1, x2, x3),
            (
                (a0, a1, a2, a4, a35, a6, a7),
                tuple((array, lead, 0) for array, lead in
                    ((0, None), (1, None), (2, None), (4, 0), (3, None), (4, 1), (5, None), (6, None))),
            ),
            None,
            cosine,
            sine,
        )
        q, g1, h1, f4 = together(q, g1, h1, f4)
        g2, g5, h2, h5 = ring(g1), by_y(g1), ring(h1), by_y(h1)
        e14 = by_x(jnp.stack([narrow(g1), narrow(f4)]))
        ctx_fa, lse_fa = attend(q, k, v, 2)
        ctx_fa, q = together(ctx_fa, q)
        ctx_fb, lse_fb = attend(q, k, v, 3)
        ctx_fa, ctx_fb, q, g2, g5, h2, h5, e14 = together(ctx_fa, ctx_fb, q, g2, g5, h2, h5, e14)
        other = by_x(jnp.concatenate([ctx_fa, ctx_fb], axis=0))
        g3, g6 = ring(g2), by_y(g2)
        e25 = by_x(jnp.stack([narrow(g2), narrow(g5)]))
        ctx_na, lse_na = attend(q, k, v, 0)
        ctx_na, q = together(ctx_na, q)
        ctx_nb, lse_nb = attend(q, k, v, 1)
        ctx_nb, g3, g6, e25, h2, h5 = together(ctx_nb, g3, g6, e25, h2, h5)
        g7 = by_y(g3)
        h3 = ring(h2)
        e36 = by_x(jnp.stack([narrow(g3), narrow(g6)]))
        ctx_nb, h3, g7, other = together(ctx_nb, h3, g7, other)
        h67 = by_y(jnp.stack([h2, h3]))
        e7 = by_x(narrow(g7))
        arrays = (f0, g1, g2, g3, f4, g5, g6, g7, h1, h2, h3, h5, h67, w_other, e14, e25, e36, e7)
        wide_at = tuple((array, None) for array in range(8))
        mine_at = tuple((array, lead, 0) for array, lead in wide_at)
        out_pieces = (arrays[:8], tuple((array, lead, PADDED) for array, lead in wide_at))
        late = PADDED + WIDTH
        down_at = tuple(
            (array, lead, column)
            for array, lead, column in
            ((0, None, late), (8, None, 0), (9, None, 0), (10, None, 0))
            + ((4, None, late), (11, None, 0), (12, 0, 0), (12, 1, 0))
        )
        other_at = tuple(
            (array, lead, 0)
            for array, lead in
            ((13, None), (14, 0), (15, 0), (16, 0), (14, 1), (15, 1), (16, 1), (17, None))
        )
    else:
        x1, x3 = by_core(x0), by_core(x2)
        gather = lambda value: lax.all_gather(value, "shard", axis=0, tiled=True)
        alone = ((0, None, 0),)
        first_low, q, k, v, w_full, gains = qkv_call(
            count,
            idx,
            (x0, x1, x2, x3),
            ((gather(w_qkv),), alone),
            jnp.stack([gather(attn_gain), gather(mlp_gain)]),
            cosine,
            sine,
        )
        arrays = (gather(w_mine), gather(w_down))
        arrays += (by_x(arrays[0]),)
        out_pieces = ((gather(out_weight),), alone)
        mine_at, down_at, other_at = alone, ((1, None, 0),), ((2, None, 0),)
        (ctx_fa, lse_fa), (ctx_fb, lse_fb) = attend(q, k, v, 2), attend(q, k, v, 3)
        other = by_x(jnp.concatenate([ctx_fa, ctx_fb], axis=0))
        (ctx_na, lse_na), (ctx_nb, lse_nb) = attend(q, k, v, 0), attend(q, k, v, 1)
    c1 = by_core(c0)

    near, far = (ctx_na, ctx_nb), (ctx_fa, ctx_fb)
    lse_near, lse_far = (lse_na, lse_nb), (lse_fa, lse_fb)
    out_own, w_sel = out_call(count, idx, near, other, out_pieces)
    if eight:
        out_own, *last = together(out_own, *arrays)
        arrays = tuple(last)
    out_core = by_core(out_own)
    second_low, hidden, gate_up_grad, second_own, w_down_full = mlp_call(
        count, idx, x0, x1, out_own, out_core, c0, c1, gains, arrays, mine_at, other_at, down_at
    )
    second_core = by_core(second_own)
    wide = list(wide_call(count, idx, second_low, gate_up_grad))
    wide[-1], second_core = together(wide[-1], second_core)
    res, res_low, grad_near, grad_other, gain_two = norm_two_call(
        x0, x1, out_own, out_core, second_own, second_core, c0, c1, gains, w_sel
    )
    grad_far = by_x(grad_other)
    down_other, down_mine, out_keep, out_send, *down = down_call(
        count, idx, hidden, w_down_full, c0, c1, near, other, res_low
    )
    part = lambda half, pair, grads, earlier=None: attend_back(
        half, pair, q, grads, (near, far)[half], (lse_near, lse_far)[half], k, v, cosine, sine, earlier
    )
    if eight:
        a_keep, a_send, b_keep, b_send = wide
        a_got, b_got = by_y(a_send), by_x(b_send)
        out_send, grad_near, down[1] = together(out_send, grad_near, down[1])
        out_got, down_got = by_x(out_send), by_y(down[1])
        down_core = by_core(down_other)
    else:
        down_core = by_core(down_other)
    q_n0, dk0, dv0 = part(0, 0, grad_near)
    if eight:
        q_n0, grad_near, grad_far, down_core, a_got, b_got = together(
            q_n0, grad_near, grad_far, down_core, a_got, b_got
        )
        a_keep, a_got = plus(a_keep[0], a_got[0]), by_x(plus(a_keep[1], a_got[1]))
        b_keep, b_got = plus(b_keep[:4], b_got[:4]), by_y(plus(b_keep[4:], b_got[4:]))
    q_n1, dk1, dv1 = part(0, 1, grad_near)
    q_n1, grad_far = together(q_n1, grad_far)
    q_f0, k0, v0 = part(1, 0, grad_far, (dk0, dv0))
    if eight:
        q_f0, out_got, down_got, grad_far = together(q_f0, out_got, down_got, grad_far)
        down_keep, down_got = plus(down[0][0], down_got[0]), by_x(plus(down[0][1], down_got[1]))
    raw0 = (q_n0, q_f0, k0, v0)
    *terms0, gain_a = qkv_grad_call(count, idx, first_low, raw0, w_full, gains, 0)
    if eight:
        terms0[0], terms0[1], a_got, b_got, grad_far = together(
            terms0[0], terms0[1], a_got, b_got, grad_far
        )
        both = lambda lo, hi: jnp.concatenate(
            [plus(a_keep[lo:hi], a_got[lo:hi]), plus(b_keep[lo:hi], b_got[lo:hi])], axis=-1
        )
        wide_next, wide_keep = by_z(both(2, 4)), both(0, 2)
        out_next = by_y(jnp.concatenate([plus(out_keep[4:], out_got[4:]), terms0[1]], axis=1))
        out_keep = plus(out_keep[:4], out_got[:4])
    q_f1, k1, v1 = part(1, 1, grad_far, (dk1, dv1))
    raw1 = (q_n1, q_f1, k1, v1)
    first_core = back_project((raw0, raw1), w_full, 1)
    first_got = by_core(first_core)
    if eight:
        first_core, q_f1, wide_next, out_next, down_got = together(
            first_core, q_f1, wide_next, out_next, down_got
        )
        wide_last, wide_keep = by_zz(plus(wide_keep[1], wide_next[1])), plus(wide_keep[0], wide_next[0])
        rest = lambda lo, hi: jnp.concatenate(
            [
                plus(down_keep[lo:hi], down_got[lo:hi]),
                plus(out_keep[lo:hi], out_next[lo:hi, :COLS]),
                plus(terms0[0][lo:hi], out_next[lo:hi, COLS:]),
            ],
            axis=1,
        )
        rest_next, rest_keep = by_z(rest(2, 4)), rest(0, 2)
    raw1 = (q_n1, q_f1, k1, v1)
    *terms1, gain_b = qkv_grad_call(count, idx, first_low, raw1, w_full, gains, 1)
    gain_terms = jnp.concatenate([gain_a[:1] + gain_b[:1], gain_two[:1]], axis=0)
    if eight:
        terms1[0], terms1[1], gain_terms, first_got, q_f1 = together(
            terms1[0], terms1[1], gain_terms, first_got, q_f1
        )
        terms1_got = by_y(terms1[1])
        gain_got = by_core(gain_terms)
        raw1 = (q_n1, q_f1, k1, v1)
    first_own = back_project((raw0, raw1), w_full, 0)
    final = lambda mine, got: mine.astype(f32) + got.astype(f32)
    if eight:
        first_own, first_got, gain_got = together(first_own, first_got, gain_got)
        first_far = by_x(plus(first_own[1], first_got[1]))
        gain_terms = gain_terms + gain_got
        gain_got = by_y(gain_terms)
        first_own, terms1_got, wide_last = together(first_own, terms1_got, wide_last)
        terms1_next = by_z(plus(terms1[0][2:], terms1_got[2:]))
        terms1_keep = plus(terms1[0][:2], terms1_got[:2])
        first_own, rest_next, gain_got = together(first_own, rest_next, gain_got)
        rest_last, rest_keep = by_zz(plus(rest_keep[1], rest_next[1])), plus(rest_keep[0], rest_next[0])
        gain_terms = gain_terms + gain_got
        gain_got = by_z(gain_terms)
        terms1_next, gain_got = together(terms1_next, gain_got)
        terms1_last = by_zz(plus(terms1_keep[1], terms1_next[1]))
        terms1_keep = plus(terms1_keep[0], terms1_next[0])
        gain_terms = gain_terms + gain_got
        gain_got = by_zz(gain_terms)
        first_far, gain_got = together(first_far, gain_got)
        gain_terms = gain_terms + gain_got
        gain_terms = gain_terms + by_x(gain_terms)
        wide_total = final(wide_keep, wide_last)
        rest_total = final(rest_keep, rest_last)
        down_total, out_total = rest_total[:BLOCK], rest_total[BLOCK : BLOCK + COLS]
        totals = [rest_total[BLOCK + COLS :], final(terms1_keep, terms1_last)]
    else:
        first_far = by_x(plus(first_own[1], first_got[1]))
        wide_sum = plus(wide[0][0, 0], by_x(wide[0][1, 0]))
        scatter = lambda value, dim: lax.psum_scatter(
            value, "shard", scatter_dimension=dim, tiled=True
        ).astype(f32)
        wide_total = scatter(wide_sum, 0)
        down_total = scatter(plus(down[0][0, 0], by_x(down[0][1, 0])), 1)
        out_total = scatter(plus(out_keep, by_x(out_send))[0], 1)
        totals = [scatter(terms[0].reshape(3, width, 128), 1) for terms in (terms0, terms1)]
        gain_terms = lax.psum(gain_terms, ("seq", "shard"))
    result = (
        x0.astype(f32)
        + out_own[:rows].astype(f32)
        + out_core[rows:].astype(f32)
        + down_mine.astype(f32)
        + down_core.astype(f32)
    ).astype(bf16)[None]
    input_grad = norm_one_call(x0, res, first_own, first_got, first_far, gains)[None]
    if eight:
        down_total, first_own = together(down_total, first_own)
    moved = lax.ppermute(down_total.astype(bf16), "seq", [(1, 2), (2, 1)]).astype(f32)
    down_total = jnp.where((seq == 1) | (seq == 2), moved, down_total)
    take = width // (4 * shards)
    gain_out = lax.dynamic_slice_in_dim(gain_terms, (seq * shards + shard) * take, take, 1)
    qkv_out = jnp.concatenate([total.reshape(3, piece, 128) for total in totals], axis=2)
    return (
        result,
        input_grad,
        gain_out[0],
        qkv_out,
        out_total,
        gain_out[1],
        wide_total[:, :HALF],
        down_total,
    )


def solution(mesh):
    placed = (
        P("shard", "seq", None),
        P("shard"),
        P(None, "shard", None),
        P("shard", None),
        P("shard"),
        P("shard", None),
        P(None, "shard"),
        P("shard", "seq", None),
    )
    return jax.shard_map(
        per_device,
        mesh=mesh,
        in_specs=placed,
        out_specs=(
            P("shard", "seq", None),
            P("shard", "seq", None),
            P(("seq", "shard")),
            P(None, "shard", "seq"),
            P("seq", "shard"),
            P(("seq", "shard")),
            P("shard", "seq"),
            P("seq", "shard"),
        ),
        check_vma=False,
    )
```

```python
from functools import partial
import math

import jax
import jax.numpy as jnp
from jax import lax
from jax.experimental import pallas as pl
from jax.experimental.pallas import tpu as pltpu
from jax.sharding import PartitionSpec as P

HEADS = 16
HD = 64
FF = 2624

epsilon = 1e-05
rope_base = 160000.0

f32 = jnp.float32
bf16 = jnp.bfloat16

WIDTH = 1024
HALF = FF // 2
PADDED = 1408
BLOCK = FF // 4
COLS = 256
CHUNKS = (0, 4, 2, 6, 1, 5, 3, 7)
SPLIT = 768
EXTRA = 16
ROWS_BY_COLS = (((0,), (0,)), ((), ()))
COLS_BY_COLS = (((1,), (1,)), ((), ()))
VMEM_LIMIT = 58 * 1024 * 1024

ANY = pl.BlockSpec(memory_space=pl.ANY)
SMEM = pl.BlockSpec(memory_space=pltpu.SMEM)


def cost(micros):
    return pl.CostEstimate(flops=int(micros), transcendentals=0, bytes_accessed=int(micros))


def params():
    return pltpu.CompilerParams(vmem_limit_bytes=VMEM_LIMIT)


def sds(shape, dtype=bf16):
    return jax.ShapeDtypeStruct(shape, dtype)


def aligned(index, size):
    return pl.ds(pl.multiple_of(index * size, size), size)


def normalize(values):
    center = values - jnp.mean(values, axis=-1, keepdims=True)
    inv_scale = lax.rsqrt(jnp.mean(center * center, axis=-1, keepdims=True) + epsilon)
    return center * inv_scale, inv_scale


def norm_back(grads, xhat, inv_scale):
    mean_grad = jnp.mean(grads, axis=-1, keepdims=True)
    mean_both = jnp.mean(grads * xhat, axis=-1, keepdims=True)
    return inv_scale * (grads - mean_grad - xhat * mean_both)


def turned(values):
    lane = lax.broadcasted_iota(jnp.int32, values.shape, 1)
    width = values.shape[1]
    return jnp.where(
        lane % HD < HD // 2, pltpu.roll(values, width - HD // 2, 1), pltpu.roll(values, HD // 2, 1)
    )


def twice(table):
    return jnp.concatenate([table, table], axis=1)


def piece_of(refs, place, rows=None, width=None):
    array, lead, column = place
    index = () if lead is None else (lead,)
    rows = slice(None) if rows is None else rows
    cols = slice(None) if width is None else pl.ds(column, width)
    return refs[array].at[(*index, rows, cols)]


def fetch_rows(count, idx, refs, places, width, target, sem):
    size = target.shape[0] // count
    copies = []
    for r in range(count):
        rows = aligned(idx[4 + r], size) if count > 1 else pl.ds(0, size)
        copies.append(
            pltpu.make_async_copy(piece_of(refs, places[r], width=width), target.at[rows], sem.at[r])
        )
    return copies


def qkv_kernel(count, places, idx, *refs):
    x_refs, refs = refs[:4], refs[4:]
    n_arrays = 1 + max(array for array, _, _ in places)
    w_refs, refs = refs[:n_arrays], refs[n_arrays:]
    if count == 1:
        gain_ref, refs = refs[0], refs[1:]
    cos_ref, sin_ref, fn_o, q_o, k_o, v_o, w_o, g_o, xs, gs, semx, semw, semg = refs
    step = pl.program_id(0)
    shard = idx[0]
    size = WIDTH // count

    def x_copy(r):
        return pltpu.make_async_copy(x_refs[r], xs.at[r], semx.at[r])

    def w_copy(r):
        return pltpu.make_async_copy(
            piece_of(w_refs, places[r], rows=pl.ds(0, size)), w_o.at[aligned(jnp.bitwise_xor(shard, r), size)], semw.at[r]
        )

    def g_copy(r):
        return pltpu.make_async_copy(
            piece_of(w_refs, places[r], rows=pl.ds(size, EXTRA)), gs.at[jnp.bitwise_xor(shard, r)], semg.at[r]
        )

    @pl.when(step == 0)
    def _():
        if count == 1:
            w_all = pltpu.make_async_copy(w_refs[0], w_o, semw.at[0])
            w_all.start()
        else:
            for r in range(count):
                w_copy(r).start()
                g_copy(r).start()
        for r in range(4):
            x_copy(r).start()
        if count == 1:
            w_all.wait()
            g_o[0:1] = gain_ref[0:1].astype(f32)
            g_o[1:2] = gain_ref[1:2].astype(f32)
        else:
            for r in range(count):
                w_copy(r).wait()
                g_copy(r).wait()
            for r in range(count):
                part = gs[r].astype(f32)
                g_o[0:1, r * size : (r + 1) * size] = part[0:1, 0:size]
                g_o[1:2, r * size : (r + 1) * size] = part[0:1, size : 2 * size]

    for r in range(4):

        @pl.when(step == r)
        def _():
            x_copy(r).wait()

    xhat, _ = normalize(xs[step].astype(f32))
    first_low = (xhat * g_o[0:1]).astype(bf16)
    fn_o[...] = first_low
    cosine, sine = twice(cos_ref[...]), twice(sin_ref[...])
    outs = (q_o, k_o, v_o)
    for part in range(3):
        value = jnp.dot(first_low, w_o[:, part * COLS : (part + 1) * COLS], preferred_element_type=f32)
        if part < 2:
            value = value * cosine + turned(value) * sine
        value = value.astype(bf16)
        if part == 0:
            value = value * jnp.asarray(1.0 / math.sqrt(HD), bf16)
        outs[part][...] = value


def qkv_call(count, idx, chunks, pieces, gains, cosine, sine):
    arrays, where = pieces
    rows = chunks[0].shape[0]
    by_step = lambda width: pl.BlockSpec((rows, width), lambda r: (r, 0))
    whole = lambda shape: pl.BlockSpec(shape, lambda r: (0, 0))
    extra = [] if count > 1 else [gains]
    return pl.pallas_call(
        partial(qkv_kernel, count, where),
        grid=(4,),
        in_specs=[SMEM]
        + [ANY] * (4 + len(arrays))
        + ([] if count > 1 else [whole((2, WIDTH))])
        + [by_step(128), by_step(128)],
        out_specs=[
            by_step(WIDTH),
            by_step(COLS),
            by_step(COLS),
            by_step(COLS),
            whole((WIDTH, 3 * COLS)),
            whole((8, WIDTH)),
        ],
        out_shape=[
            sds((4 * rows, WIDTH)),
            sds((4 * rows, COLS)),
            sds((4 * rows, COLS)),
            sds((4 * rows, COLS)),
            sds((WIDTH, 3 * COLS)),
            sds((8, WIDTH), f32),
        ],
        scratch_shapes=[
            pltpu.VMEM((4, rows, WIDTH), bf16),
            pltpu.VMEM((8, EXTRA, 3 * COLS), bf16),
            pltpu.SemaphoreType.DMA((4,)),
            pltpu.SemaphoreType.DMA((count,)),
            pltpu.SemaphoreType.DMA((count,)),
        ],
        compiler_params=params(),
        cost_estimate=cost(11),
        name="project",
    )(idx, *chunks, *arrays, *extra, cosine, sine)


def head_of(shape):
    return lax.broadcasted_iota(jnp.int32, shape, len(shape) - 1) // HD


def attend_kernel(q_ref, k_ref, v_ref, o_ref, lse_ref):
    q, k, v = q_ref[...], k_ref[...], v_ref[...]
    heads = head_of(q.shape)
    total = jnp.zeros(q.shape, f32)
    lses = jnp.zeros((q.shape[0], 128), f32)
    lane = lax.broadcasted_iota(jnp.int32, lses.shape, 1)
    for h in range(COLS // HD):
        q_h = jnp.where(heads == h, q, jnp.zeros_like(q))
        scores = lax.dot_general(q_h, k, COLS_BY_COLS, preferred_element_type=f32)
        row_max = jnp.max(scores, axis=1, keepdims=True)
        exponent = jnp.exp(scores - row_max)
        row_total = jnp.sum(exponent, axis=1, keepdims=True)
        context = jnp.dot(exponent.astype(bf16), v, preferred_element_type=f32)
        total = jnp.where(heads == h, context * (1.0 / row_total), total)
        lses = jnp.where(lane == h, row_max + jnp.log(row_total), lses)
    o_ref[...] = total.astype(bf16)
    lse_ref[...] = lses.T[:8]


def attend(q, k, v, chunk, after=()):
    span = k.shape[0]
    rows = span // 4
    kept = pl.BlockSpec((span, COLS), lambda i: (0, 0))
    return pl.pallas_call(
        lambda *refs: attend_kernel(*refs[:3], *refs[3 + len(after) :]),
        grid=(1,),
        in_specs=[pl.BlockSpec((rows, COLS), lambda i: (chunk, 0)), kept, kept] + [ANY] * len(after),
        out_specs=[
            pl.BlockSpec((rows, COLS), lambda i: (0, 0)),
            pl.BlockSpec((8, rows), lambda i: (0, 0)),
        ],
        out_shape=[sds((rows, COLS)), sds((8, rows), f32)],
        compiler_params=params(),
        cost_estimate=cost(8),
        name="attend",
    )(q, k, v, *after)


def attend_back_kernel(last, pair, *refs):
    q_ref, do_ref, oa_ref, ob_ref, la_ref, lb_ref, k_ref, v_ref, qcos, qsin, refs = *refs[:10], refs[10:]
    if last:
        dk_i, dv_i, kcos, ksin, refs = *refs[:4], refs[4:]
    dq_ref, dk_ref, dv_ref, do_s, inner_s, lse_s, dq_s = refs
    step = pl.program_id(0)
    width = q_ref.shape[1]
    n_heads = width // HD

    @pl.when(step == 0)
    def _():
        do = do_ref[...]
        context = jnp.concatenate([oa_ref[...], ob_ref[...]], axis=0)
        product = do.astype(f32) * context.astype(f32)
        high = product.astype(bf16)
        rest = (product - high.astype(f32)).astype(bf16)
        chosen = (
            head_of((8, width)) == lax.broadcasted_iota(jnp.int32, (8, width), 0)
        ).astype(bf16)
        inner_s[...] = lax.dot_general(
            chosen, high, COLS_BY_COLS, preferred_element_type=f32
        ) + lax.dot_general(chosen, rest, COLS_BY_COLS, preferred_element_type=f32)
        lse_s[...] = jnp.concatenate([la_ref[...], lb_ref[...]], axis=1)
        heads = head_of(do.shape)
        for h in range(n_heads):
            do_s[h] = jnp.where(heads == h, do, jnp.zeros_like(do))
        dq_s[...] = jnp.zeros_like(dq_s)

    q, k, v = q_ref[...], k_ref[...], v_ref[...]
    heads = head_of(k.shape)
    dk = jnp.zeros(k.shape, f32)
    dv = jnp.zeros(k.shape, f32)
    dq = dq_s[...]
    for h in range(n_heads):
        at = n_heads * pair + h
        k_h = jnp.where(heads == h, k, jnp.zeros_like(k))
        scores = lax.dot_general(k_h, q, COLS_BY_COLS, preferred_element_type=f32)
        probs = jnp.exp(scores - lse_s[at : at + 1, :])
        probs_grad = lax.dot_general(v, do_s[h], COLS_BY_COLS, preferred_element_type=f32)
        scores_grad = (probs * (probs_grad - inner_s[h : h + 1, :])).astype(bf16)
        dv = dv + jnp.dot(probs.astype(bf16), do_s[h], preferred_element_type=f32)
        dk = jnp.where(heads == h, jnp.dot(scores_grad, q, preferred_element_type=f32), dk)
        dq = dq + lax.dot_general(scores_grad, k_h, ROWS_BY_COLS, preferred_element_type=f32)
    dq_s[...] = dq
    if last:
        dk = dk + dk_i[...]
        dv = dv + dv_i[...]
        dk_ref[...] = (dk * kcos[...] - turned(dk) * ksin[...]).astype(bf16)
        dv_ref[...] = dv.astype(bf16)
    else:
        dk_ref[...] = dk
        dv_ref[...] = dv

    @pl.when(step == pl.num_programs(0) - 1)
    def _():
        dq = dq_s[...] * (1.0 / math.sqrt(HD))
        dq_ref[...] = (dq * qcos[...] - turned(dq) * qsin[...]).astype(bf16)


def attend_back(part, pair, q, do, contexts, lses, k, v, cosine, sine, earlier=None, after=(), tile=512):
    span = k.shape[0]
    rows = do.shape[0]
    last = earlier is not None
    rows_at = lambda at, col, count=rows, width=128: pl.BlockSpec((count, width), lambda i: (at, col))
    keys = lambda col: pl.BlockSpec((tile, 128), lambda i: (i, col))
    grads = bf16 if last else f32
    n_in = 10 + (4 if last else 0)
    return pl.pallas_call(
        lambda *refs: attend_back_kernel(last, pair, *refs[:n_in], *refs[n_in + len(after) :]),
        grid=(span // tile,),
        in_specs=[
            rows_at(part, pair),
            rows_at(0, pair),
            rows_at(0, pair, rows // 2),
            rows_at(0, pair, rows // 2),
            rows_at(0, 0, 8, rows // 2),
            rows_at(0, 0, 8, rows // 2),
            keys(pair),
            keys(pair),
            rows_at(part, 0),
            rows_at(part, 0),
        ]
        + ([keys(0), keys(0), keys(0), keys(0)] if last else [])
        + [ANY] * len(after),
        out_specs=[rows_at(0, 0), keys(0), keys(0)],
        out_shape=[sds((rows, 128)), sds((span, 128), grads), sds((span, 128), grads)],
        scratch_shapes=[
            pltpu.VMEM((128 // HD, rows, 128), bf16),
            pltpu.VMEM((8, rows), f32),
            pltpu.VMEM((8, rows), f32),
            pltpu.VMEM((rows, 128), f32),
        ],
        compiler_params=params(),
        cost_estimate=cost(15),
        name="attend_back",
    )(q, do, *contexts, *lses, k, v, cosine, sine, *((*earlier, cosine, sine) if last else ()), *after)


def out_kernel(count, places, idx, ma_ref, mb_ref, oa_ref, ob_ref, *refs):
    w_refs, (o_ref, wsel_ref, w_s, sem) = refs[:-4], refs[-4:]
    copies = fetch_rows(count, idx, w_refs, places, WIDTH, w_s, sem)
    for copy in copies:
        copy.start()
    for copy in copies:
        copy.wait()
    seq = idx[1]
    wsel_ref[0:COLS] = w_s[aligned(seq, COLS)]
    wsel_ref[COLS:] = w_s[aligned(jnp.bitwise_xor(seq, 2), COLS)]
    rows = ma_ref.shape[0]
    for r, (mine, other) in enumerate(((ma_ref, oa_ref), (mb_ref, ob_ref))):
        both = jnp.concatenate([mine[...], other[...]], axis=1)
        value = jnp.dot(both, wsel_ref[...], preferred_element_type=f32)
        o_ref[r * rows : (r + 1) * rows] = value.astype(bf16)


def out_call(count, idx, mine, other, pieces):
    vmem = pl.BlockSpec(memory_space=pltpu.VMEM)
    arrays, where = pieces
    return pl.pallas_call(
        partial(out_kernel, count, where),
        in_specs=[SMEM] + [vmem] * 4 + [ANY] * len(arrays),
        out_specs=[vmem, vmem],
        out_shape=[sds((2 * mine[0].shape[0], WIDTH)), sds((2 * COLS, WIDTH))],
        scratch_shapes=[pltpu.VMEM((WIDTH, WIDTH), bf16), pltpu.SemaphoreType.DMA((count,))],
        compiler_params=params(),
        cost_estimate=cost(5),
        name="out_project",
    )(idx, *mine, *other, *arrays)


def mlp_kernel(count, n_arrays, mine, other, down, idx, *refs):
    x0, x1, po, pr, c0, c1, g_ref, refs = *refs[:7], refs[7:]
    w_refs, refs = refs[:n_arrays], refs[n_arrays:]
    sn_o, hid_o, gug_o, sgp_o, wd_o, refs = *refs[:5], refs[5:]
    xs, pos, prs, cs, wi, wd, sn_s, hid_s, gug_s, sgp_s, sem_a, sem_m, sem_i, sem_d, sem_o = refs
    x_place = idx[2]
    rows = xs.shape[1]
    loads = [
        pltpu.make_async_copy(x0, xs.at[0], sem_a.at[0]),
        pltpu.make_async_copy(x1, xs.at[1], sem_a.at[1]),
        pltpu.make_async_copy(po, pos, sem_a.at[2]),
        pltpu.make_async_copy(pr, prs, sem_a.at[3]),
        pltpu.make_async_copy(c0, cs.at[pl.ds(0, rows)], sem_a.at[4]),
        pltpu.make_async_copy(c1, cs.at[pl.ds(rows, rows)], sem_a.at[5]),
    ]
    here = wi.at[:, aligned(x_place, PADDED)]
    there = wi.at[:, aligned(1 - x_place, PADDED)]
    wi_loads = fetch_rows(count, idx, w_refs, mine, PADDED, here, sem_m)
    wi_loads += fetch_rows(count, idx, w_refs, other, PADDED, there, sem_i)
    wd_loads = fetch_rows(count, idx, w_refs, down, PADDED, wd, sem_d)
    for copy in loads[:4] + wi_loads + loads[4:] + wd_loads:
        copy.start()
    for copy in loads[:4]:
        copy.wait()
    for r in range(2):
        here, there = pl.ds(r * rows, rows), pl.ds((1 - r) * rows, rows)
        after = xs[r].astype(f32) + pos[here].astype(f32) + prs[there].astype(f32)
        xhat, _ = normalize(after)
        sn_s[here] = (xhat * g_ref[1:2]).astype(bf16)
    stores = []

    def store(source, target, k):
        copy = pltpu.make_async_copy(source, target, sem_o.at[k])
        copy.start()
        stores.append(copy)

    store(sn_s, sn_o, 0)
    for copy in wi_loads + loads[4:] + wd_loads:
        copy.wait()
    store(wd, wd_o, 1)
    start = 0
    while start < PADDED:
        size = min(256, PADDED - start)
        here = pl.ds(start, size)
        gate = jnp.dot(sn_s[...], wi[:, here], preferred_element_type=f32)
        up = jnp.dot(sn_s[...], wi[:, pl.ds(PADDED + start, size)], preferred_element_type=f32)
        back = jnp.dot(cs[...], wd[:, here], preferred_element_type=f32)
        below = 0.5 * (1.0 + lax.erf(gate * math.sqrt(0.5)))
        density = jnp.exp(-0.5 * gate * gate) * (1.0 / math.sqrt(2.0 * math.pi))
        unit = gate * below
        hid_s[:, here] = (unit * up).astype(bf16)
        gug_s[0, :, here] = (back * up * (below + gate * density)).astype(bf16)
        gug_s[1, :, here] = (back * unit).astype(bf16)
        start += size
    store(hid_s, hid_o, 2)
    store(gug_s, gug_o, 3)
    value = lax.dot_general(gug_s[0], wi[:, :PADDED], COLS_BY_COLS, preferred_element_type=f32)
    value = value + lax.dot_general(gug_s[1], wi[:, PADDED:], COLS_BY_COLS, preferred_element_type=f32)
    sgp_s[...] = value.astype(bf16)
    store(sgp_s, sgp_o, 4)
    for copy in stores:
        copy.wait()


def mlp_call(count, idx, x0, x1, po, pr, c0, c1, gains, arrays, mine, other, down):
    rows = x0.shape[0]
    return pl.pallas_call(
        partial(mlp_kernel, count, len(arrays), mine, other, down),
        in_specs=[SMEM] + [ANY] * 6 + [pl.BlockSpec(memory_space=pltpu.VMEM)] + [ANY] * len(arrays),
        out_specs=[ANY] * 5,
        out_shape=[
            sds((2 * rows, WIDTH)),
            sds((2 * rows, PADDED)),
            sds((2, 2 * rows, PADDED)),
            sds((2 * rows, WIDTH)),
            sds((WIDTH, PADDED)),
        ],
        scratch_shapes=[
            pltpu.VMEM((2, rows, WIDTH), bf16),
            pltpu.VMEM((2 * rows, WIDTH), bf16),
            pltpu.VMEM((2 * rows, WIDTH), bf16),
            pltpu.VMEM((2 * rows, WIDTH), bf16),
            pltpu.VMEM((WIDTH, 2 * PADDED), bf16),
            pltpu.VMEM((WIDTH, PADDED), bf16),
            pltpu.VMEM((2 * rows, WIDTH), bf16),
            pltpu.VMEM((2 * rows, PADDED), bf16),
            pltpu.VMEM((2, 2 * rows, PADDED), bf16),
            pltpu.VMEM((2 * rows, WIDTH), bf16),
            pltpu.SemaphoreType.DMA((6,)),
            pltpu.SemaphoreType.DMA((count,)),
            pltpu.SemaphoreType.DMA((count,)),
            pltpu.SemaphoreType.DMA((count,)),
            pltpu.SemaphoreType.DMA((5,)),
        ],
        compiler_params=params(),
        cost_estimate=cost(25),
        name="feed_forward",
    )(idx, x0, x1, po, pr, c0, c1, gains, *arrays)


def down_kernel(count, idx, hid_ref, wd_ref, c0, c1, ma, mb, oa, ob, low, res_other, res_mine, *refs):
    outs, downs, acc = refs[:2], refs[2:-1], refs[-1]
    shard, x_place = idx[0], idx[2]
    rows = c0.shape[0]
    width = WIDTH // count
    places = [
        aligned(jnp.bitwise_xor(shard, r), width) if count > 1 else pl.ds(0, width) for r in CHUNKS[:count]
    ]
    acc[...] = lax.dot_general(
        hid_ref[0:rows], c0[...], ROWS_BY_COLS, preferred_element_type=f32
    ) + lax.dot_general(hid_ref[rows:], c1[...], ROWS_BY_COLS, preferred_element_type=f32)
    for part in range(2):
        here = pl.ds(pl.multiple_of(jnp.bitwise_xor(x_place, part) * BLOCK, 8), BLOCK)
        for r in range(count):
            downs[r // 4][part, r % 4] = acc[here, places[r]].astype(bf16)
    mine = jnp.concatenate([ma[...], mb[...]], axis=0)
    other = jnp.concatenate([oa[...], ob[...]], axis=0)
    for part, context in enumerate((mine, other)):
        acc[0:COLS] = lax.dot_general(context, low[...], ROWS_BY_COLS, preferred_element_type=f32)
        for r in range(count):
            outs[part][r] = acc[0:COLS, places[r]].astype(bf16)
    for r, target in ((1, res_other), (0, res_mine)):
        target[...] = lax.dot_general(
            hid_ref[r * rows : (r + 1) * rows], wd_ref[...], COLS_BY_COLS, preferred_element_type=f32
        ).astype(bf16)


def down_call(count, idx, hidden, wd, c0, c1, mine, other, low):
    rows = c0.shape[0]
    split = 2 if count > 1 else 1
    vmem = pl.BlockSpec(memory_space=pltpu.VMEM)
    return pl.pallas_call(
        partial(down_kernel, count),
        in_specs=[SMEM] + [vmem] * 9,
        out_specs=[vmem] * (4 + split),
        out_shape=[sds((rows, WIDTH))] * 2
        + [sds((count, COLS, WIDTH // count))] * 2
        + [sds((2, count // split, BLOCK, WIDTH // count))] * split,
        scratch_shapes=[pltpu.VMEM((PADDED, WIDTH), f32)],
        compiler_params=params(),
        cost_estimate=cost(15),
        name="down_project",
    )(idx, hidden, wd, c0, c1, *mine, *other, low)


def norm_two_kernel(x0, x1, po, pr, so, sr, c0, c1, g_ref, wsel, res_o, low_o, mine_o, other_o, gain_o):
    step = pl.program_id(0)
    half = pl.num_programs(0) // 2
    first = step < half
    gain = g_ref[1:2]
    x = jnp.where(first, x0[...], x1[...])
    c = jnp.where(first, c0[...], c1[...])
    after = x.astype(f32) + po[...].astype(f32) + pr[...].astype(f32)
    xhat, inv_scale = normalize(after)
    second = so[...].astype(f32) + sr[...].astype(f32)
    res = c.astype(f32) + norm_back(second * gain, xhat, inv_scale)

    @pl.when(step == 0)
    def _():
        gain_o[...] = jnp.zeros_like(gain_o)

    @pl.when(first)
    def _():
        res_o[...] = res
        gain_o[...] += jnp.sum(second * xhat, axis=0, keepdims=True)

    low = res.astype(bf16)
    low_o[...] = low
    value = lax.dot_general(low, wsel[...], COLS_BY_COLS, preferred_element_type=f32).astype(bf16)
    mine_o[...] = value[:, :COLS]
    other_o[...] = value[:, COLS:]


def norm_two_call(x0, x1, po, pr, so, sr, c0, c1, gains, wsel, half=2):
    rows = x0.shape[0]
    size = rows // half
    spec = lambda width, at: pl.BlockSpec((size, width), lambda s: (at(s), 0))
    lower = lambda s: jnp.minimum(s, half - 1)
    upper = lambda s: jnp.maximum(s - half, 0)
    same = lambda s: s
    other = lambda s: lax.rem(s + half, 2 * half)
    whole = lambda shape: pl.BlockSpec(shape, lambda s: (0, 0))
    return pl.pallas_call(
        norm_two_kernel,
        grid=(2 * half,),
        in_specs=[
            spec(WIDTH, lower),
            spec(WIDTH, upper),
            spec(WIDTH, same),
            spec(WIDTH, other),
            spec(WIDTH, same),
            spec(WIDTH, other),
            spec(WIDTH, lower),
            spec(WIDTH, upper),
            whole((8, WIDTH)),
            whole((2 * COLS, WIDTH)),
        ],
        out_specs=[
            spec(WIDTH, lower),
            spec(WIDTH, same),
            spec(COLS, same),
            spec(COLS, same),
            whole((8, WIDTH)),
        ],
        out_shape=[
            sds((rows, WIDTH), f32),
            sds((2 * rows, WIDTH)),
            sds((2 * rows, COLS)),
            sds((2 * rows, COLS)),
            sds((8, WIDTH), f32),
        ],
        compiler_params=params(),
        cost_estimate=cost(8),
        name="norm_two_back",
    )(x0, x1, po, pr, so, sr, c0, c1, gains, wsel)


def wide_kernel(count, idx, sn_ref, gug_ref, *refs):
    shard = idx[0]
    part = pl.program_id(0)
    size = WIDTH // count
    if count == 1:
        out, acc = refs
        acc[...] = lax.dot_general(sn_ref[...], gug_ref[0], ROWS_BY_COLS, preferred_element_type=f32)
        out[0, 0] = acc[...].astype(bf16)
        return
    keep_a, send_a, keep_b, send_b, acc = refs
    acc[...] = lax.dot_general(sn_ref[...], gug_ref[0], ROWS_BY_COLS, preferred_element_type=f32)
    for k, r in enumerate(CHUNKS):
        place = aligned(jnp.bitwise_xor(shard, r), size)
        (keep_a, send_a)[k // 4][0, k % 4] = acc[place, :SPLIT].astype(bf16)

    def store(target):
        for k, r in enumerate(CHUNKS):
            place = aligned(jnp.bitwise_xor(shard, r), size)
            target[k] = acc[place, SPLIT:].astype(bf16)

    @pl.when(part == 0)
    def _():
        store(keep_b)

    @pl.when(part == 1)
    def _():
        store(send_b)


def wide_call(count, idx, sn, gug):
    tokens = sn.shape[0]
    size = WIDTH // count
    spec = lambda shape, at: pl.BlockSpec(shape, at)
    whole = lambda shape: pl.BlockSpec(shape, lambda p, s: (0,) * len(shape))
    by_part = lambda shape: pl.BlockSpec((1, *shape[1:]), lambda p, s: (p, 0, 0, 0))
    first, second = (2, 4, size, SPLIT), (8, size, PADDED - SPLIT)
    alone = (2, 1, WIDTH, PADDED)
    grid_spec = pltpu.PrefetchScalarGridSpec(
        num_scalar_prefetch=1,
        grid=(2,),
        in_specs=[
            spec((tokens, WIDTH), lambda p, s: (0, 0)),
            spec((1, tokens, PADDED), lambda p, s: (jnp.bitwise_xor(p, s[2]), 0, 0)),
        ],
        out_specs=[by_part(first)] * 2 + [whole(second)] * 2 if count > 1 else [by_part(alone)],
        scratch_shapes=[pltpu.VMEM((WIDTH, PADDED), f32)],
    )
    return pl.pallas_call(
        partial(wide_kernel, count),
        grid_spec=grid_spec,
        out_shape=[sds(first)] * 2 + [sds(second)] * 2 if count > 1 else [sds(alone)],
        compiler_params=params(),
        cost_estimate=cost(12),
        name="wide_grad",
    )(idx, sn, gug)


def back_project_kernel(q0, q1, f0, f1, k0n, k1n, k0f, k1f, v0n, v1n, v0f, v1f, w_ref, both_o):
    for half, parts in (
        (1, (f0, f1, k0f, k1f, v0f, v1f)),
        (0, (q0, q1, k0n, k1n, v0n, v1n)),
    ):
        raw = jnp.concatenate([part[...] for part in parts], axis=1)
        both_o[half] = lax.dot_general(
            raw, w_ref[...], COLS_BY_COLS, preferred_element_type=f32
        ).astype(bf16)


def back_project(raw_pairs, w, chunk):
    rows = raw_pairs[0][0].shape[0] // 2
    at = lambda where: pl.BlockSpec((rows, 128), lambda i: (where, 0))
    q0, f0, k0, v0 = raw_pairs[0]
    q1, f1, k1, v1 = raw_pairs[1]
    return pl.pallas_call(
        back_project_kernel,
        grid=(1,),
        in_specs=[at(chunk)] * 6
        + [at(chunk + 2)] * 2
        + [at(chunk)] * 2
        + [at(chunk + 2)] * 2
        + [pl.BlockSpec((WIDTH, 3 * COLS), lambda i: (0, 0))],
        out_specs=pl.BlockSpec((2, rows, WIDTH), lambda i: (0, 0, 0)),
        out_shape=sds((2, rows, WIDTH)),
        compiler_params=params(),
        cost_estimate=cost(5),
        name="back_project",
    )(q0, q1, f0, f1, k0, k1, k0, k1, v0, v1, v0, v1, w)


def qkv_grad_kernel(count, idx, fn_ref, qn, qf, k_ref, v_ref, wq, wk, wv, g_ref, keep_o, *refs):
    if count > 1:
        send_o, gain_o, acc = refs
    else:
        gain_o, acc = refs
    rows = qn.shape[0]
    q = jnp.concatenate([qn[...], qf[...]], axis=0)
    raw = jnp.concatenate([q, k_ref[...], v_ref[...]], axis=1)
    acc[...] = lax.dot_general(fn_ref[...], raw, ROWS_BY_COLS, preferred_element_type=f32)
    shard = idx[0]
    size = WIDTH // count
    for k, r in enumerate(CHUNKS[:count]):
        place = aligned(jnp.bitwise_xor(shard, r), size) if count > 1 else pl.ds(0, size)
        target = (keep_o, send_o)[k // 4] if count > 1 else keep_o
        for part in range(3):
            value = acc[place, part * 128 : (part + 1) * 128]
            target[k % 4, part * size : (part + 1) * size] = value.astype(bf16)
    w = jnp.concatenate([wq[...], wk[...], wv[...]], axis=1)
    both = acc[...] * w.astype(f32)
    high = both.astype(bf16)
    rest = (both - high.astype(f32)).astype(bf16)
    ones = jnp.ones((8, w.shape[1]), bf16)
    total = lax.dot_general(ones, high, COLS_BY_COLS, preferred_element_type=f32)
    total += lax.dot_general(ones, rest, COLS_BY_COLS, preferred_element_type=f32)
    gain_o[...] = total / g_ref[0:1]


def qkv_grad_call(count, idx, first_low, raw, w, gains, pair):
    vmem = pl.BlockSpec(memory_space=pltpu.VMEM)
    split = 2 if count > 1 else 1
    size = WIDTH // count
    width = 3 * 128
    whole = lambda shape: pl.BlockSpec(shape, lambda i: (0,) * len(shape))
    weight = lambda part: pl.BlockSpec((WIDTH, 128), lambda i: (0, 2 * part + pair))
    grads = [(count // split, 3 * size, 128)] * split + [(8, WIDTH)]
    return pl.pallas_call(
        partial(qkv_grad_kernel, count),
        grid=(1,),
        in_specs=[SMEM, whole(first_low.shape)]
        + [whole(value.shape) for value in raw]
        + [weight(0), weight(1), weight(2), whole(gains.shape)],
        out_specs=[whole(shape) for shape in grads],
        out_shape=[sds(shape) for shape in grads[:-1]] + [sds(grads[-1], f32)],
        scratch_shapes=[pltpu.VMEM((WIDTH, width), f32)],
        compiler_params=params(),
        cost_estimate=cost(6),
        name="project_grad",
    )(idx, first_low, *raw, w, w, w, gains)


def norm_one_kernel(x_ref, res_ref, own, core, far, g_ref, o_ref):
    xhat, inv_scale = normalize(x_ref[...].astype(f32))
    first = own[0].astype(f32) + core[0].astype(f32) + far[...].astype(f32)
    o_ref[...] = res_ref[...] + norm_back(first * g_ref[0:1], xhat, inv_scale)


def norm_one_call(x, res, own, core, far, gains, steps=4):
    rows = x.shape[0]
    block = pl.BlockSpec((rows // steps, WIDTH), lambda i: (i, 0))
    return pl.pallas_call(
        norm_one_kernel,
        grid=(steps,),
        in_specs=[
            block,
            block,
            pl.BlockSpec((1, rows // steps, WIDTH), lambda i: (0, i, 0)),
            pl.BlockSpec((1, rows // steps, WIDTH), lambda i: (0, i, 0)),
            block,
            pl.BlockSpec((8, WIDTH), lambda i: (0, 0)),
        ],
        out_specs=block,
        out_shape=sds(res.shape, f32),
        compiler_params=params(),
        cost_estimate=cost(3),
        name="norm_one_back",
    )(x, res, own, core, far, gains)


def swap(value, axis, bits):
    size = lax.axis_size(axis)
    return lax.ppermute(value, axis, [(place, place ^ bits) for place in range(size)])


def plus(left, right):
    return (left.astype(f32) + right.astype(f32)).astype(bf16)


def together(*values):
    return lax.optimization_barrier(values)


def per_device(inputs, attn_gain, qkv_weight, out_weight, mlp_gain, in_weight, mlp_out, cotangent):
    _, rows, width = inputs.shape
    shards = lax.axis_size("shard")
    eight = shards == 8
    count = 8 if eight else 1
    piece = width // shards
    seq, shard = lax.axis_index("seq"), lax.axis_index("shard")
    x_place, core = seq // 2, seq % 2
    owners = [jnp.bitwise_xor(lax.rem(shard + 8 - 2 * (r % 4), 8), r // 4) for r in range(8)]
    idx = jnp.stack([shard, seq, x_place, core, *owners]).astype(jnp.int32)

    order = jnp.bitwise_xor(seq, jnp.arange(4))
    places = (order[:, None] * rows + jnp.arange(rows)[None, :]).reshape(-1)
    frequency = 1.0 / rope_base ** (jnp.arange(0, HD, 2, dtype=f32) / HD)
    angles = places.astype(f32)[:, None] * jnp.tile(frequency, 4)[None, :]
    sign = jnp.where(jnp.arange(128) % HD < HD // 2, -1.0, 1.0)
    cosine, sine = jnp.cos(angles), jnp.sin(angles) * sign

    x0 = inputs[0]
    c0 = cotangent[0]
    w_qkv = lax.dynamic_slice_in_dim(qkv_weight, seq * COLS, COLS, 2)
    w_qkv = jnp.transpose(w_qkv, (1, 0, 2)).reshape(piece, 3 * COLS)
    w_in = in_weight.reshape(piece, 2, 2, HALF)
    w_in = lax.dynamic_index_in_dim(w_in, core, 2, keepdims=False)
    w_in = jnp.pad(w_in, ((0, 0), (0, 0), (0, PADDED - HALF)))
    w_mine = lax.dynamic_index_in_dim(w_in, x_place, 1, keepdims=False)
    w_other = lax.dynamic_index_in_dim(w_in, 1 - x_place, 1, keepdims=False)
    w_down = lax.dynamic_slice_in_dim(mlp_out, core * HALF, HALF, 0).T
    w_down = jnp.pad(w_down, ((0, 0), (0, PADDED - HALF)))

    x2 = swap(x0, "seq", 2)
    by_y = lambda value: swap(value, "shard", 1)
    by_z = lambda value: swap(value, "shard", 2)
    by_zz = lambda value: swap(value, "shard", 4)
    by_x = lambda value: swap(value, "seq", 2)
    by_core = lambda value: swap(value, "seq", 1)
    if eight:
        gain_rows = jnp.concatenate([attn_gain, mlp_gain, jnp.zeros(3 * COLS - 2 * piece, bf16)])[None]
        a0 = jnp.concatenate([w_qkv, jnp.pad(gain_rows, ((0, EXTRA - 1), (0, 0)))], axis=0)
        f0 = jnp.concatenate([w_mine, out_weight, w_down], axis=1)
        narrow = lambda value: value[..., :PADDED]
        ring = lambda value: lax.ppermute(
            value, "shard", [(place, (place + 2) % 8) for place in range(8)]
        )
        a4, a2, a1 = by_zz(a0), by_z(a0), by_y(a0)
        a4, a2, a1, x0, cosine, sine, idx, f0, w_other = together(
            a4, a2, a1, x0, cosine, sine, idx, f0, w_other
        )
        a6, a35 = by_z(a4), by_y(jnp.stack([a2, a4]))
        x1 = by_core(x0)
        a6, a35, x2 = together(a6, a35, x2)
        a7 = by_y(a6)
        x3 = by_core(x2)
        x3, x1, a7, f0 = together(x3, x1, a7, f0)
        f1, f4 = ring(f0), by_y(f0)
        c1 = by_core(c0)
        first_low, q, k, v, w_full, gains = qkv_call(
            count,
            idx,
            (x0, x1, x2, x3),
            (
                (a0, a1, a2, a4, a35, a6, a7),
                tuple((array, lead, 0) for array, lead in
                    ((0, None), (1, None), (2, None), (4, 0), (3, None), (4, 1), (5, None), (6, None))),
            ),
            None,
            cosine,
            sine,
        )
        q, f1, f4, c1 = together(q, f1, f4, c1)
        f2, f5 = ring(f1), by_y(f1)
        e14 = by_x(jnp.stack([narrow(f1), narrow(f4)]))
        ctx_fa, lse_fa = attend(q, k, v, 2)
        ctx_fa, q = together(ctx_fa, q)
        oth_a = by_x(ctx_fa)
        ctx_fb, lse_fb = attend(q, k, v, 3)
        ctx_fb, q, f2, f5, e14, oth_a = together(ctx_fb, q, f2, f5, e14, oth_a)
        oth_b = by_x(ctx_fb)
        f3, f6 = ring(f2), by_y(f2)
        e25 = by_x(jnp.stack([narrow(f2), narrow(f5)]))
        ctx_na, lse_na = attend(q, k, v, 0)
        ctx_na, q = together(ctx_na, q)
        ctx_nb, lse_nb = attend(q, k, v, 1)
        ctx_nb, f3, f6, e25, oth_b = together(ctx_nb, f3, f6, e25, oth_b)
        f7 = by_y(f3)
        e36 = by_x(jnp.stack([narrow(f3), narrow(f6)]))
        ctx_nb, f7 = together(ctx_nb, f7)
        e7 = by_x(narrow(f7))
        arrays = (f0, f1, f2, f3, f4, f5, f6, f7, w_other, e14, e25, e36, e7)
        mine_at = tuple((array, None, 0) for array in range(8))
        out_pieces = (arrays[:8], tuple((array, None, PADDED) for array in range(8)))
        down_at = tuple((array, None, PADDED + WIDTH) for array in range(8))
        other_at = tuple(
            (array, lead, 0)
            for array, lead in ((8, None), (9, 0), (10, 0), (11, 0), (9, 1), (10, 1), (11, 1), (12, None))
        )
    else:
        x1, x3 = by_core(x0), by_core(x2)
        gather = lambda value: lax.all_gather(value, "shard", axis=0, tiled=True)
        alone = ((0, None, 0),)
        first_low, q, k, v, w_full, gains = qkv_call(
            count,
            idx,
            (x0, x1, x2, x3),
            ((gather(w_qkv),), alone),
            jnp.stack([gather(attn_gain), gather(mlp_gain)]),
            cosine,
            sine,
        )
        arrays = (gather(w_mine), gather(w_down))
        arrays += (by_x(arrays[0]),)
        out_pieces = ((gather(out_weight),), alone)
        mine_at, down_at, other_at = alone, ((1, None, 0),), ((2, None, 0),)
        (ctx_fa, lse_fa), (ctx_fb, lse_fb) = attend(q, k, v, 2), attend(q, k, v, 3)
        oth_a, oth_b = by_x(ctx_fa), by_x(ctx_fb)
        c1 = by_core(c0)
        (ctx_na, lse_na), (ctx_nb, lse_nb) = attend(q, k, v, 0), attend(q, k, v, 1)

    near, far, other = (ctx_na, ctx_nb), (ctx_fa, ctx_fb), (oth_a, oth_b)
    lse_near, lse_far = (lse_na, lse_nb), (lse_fa, lse_fb)
    out_own, w_sel = out_call(count, idx, near, other, out_pieces)
    if eight:
        out_own, *last = together(out_own, *arrays)
        arrays = tuple(last)
    out_core = by_core(out_own)
    second_low, hidden, gate_up_grad, second_own, w_down_full = mlp_call(
        count, idx, x0, x1, out_own, out_core, c0, c1, gains, arrays, mine_at, other_at, down_at
    )
    second_core = by_core(second_own)
    wide = list(wide_call(count, idx, second_low, gate_up_grad))
    wide[-1], second_core = together(wide[-1], second_core)
    res, res_low, grad_near, grad_other, gain_two = norm_two_call(
        x0, x1, out_own, out_core, second_own, second_core, c0, c1, gains, w_sel
    )
    grad_far = by_x(grad_other)
    down_other, down_mine, out_keep, out_send, *down = down_call(
        count, idx, hidden, w_down_full, c0, c1, near, other, res_low
    )
    part = lambda half, pair, grads, earlier=None: attend_back(
        half, pair, q, grads, (near, far)[half], (lse_near, lse_far)[half], k, v, cosine, sine, earlier
    )
    if eight:
        a_keep, a_send, b_keep, b_send = wide
        a_got, b_got = by_y(a_send), by_x(b_send)
        out_send, grad_near, down[1] = together(out_send, grad_near, down[1])
        out_got, down_got = by_x(out_send), by_y(down[1])
        down_core = by_core(down_other)
    else:
        down_core = by_core(down_other)
    q_n0, dk0, dv0 = part(0, 0, grad_near)
    if eight:
        q_n0, grad_near, grad_far, down_core, a_got, b_got = together(
            q_n0, grad_near, grad_far, down_core, a_got, b_got
        )
        a_keep, a_got = plus(a_keep[0], a_got[0]), by_x(plus(a_keep[1], a_got[1]))
        b_keep, b_got = plus(b_keep[:4], b_got[:4]), by_y(plus(b_keep[4:], b_got[4:]))
    q_n1, dk1, dv1 = part(0, 1, grad_near)
    q_n1, grad_far = together(q_n1, grad_far)
    q_f0, k0, v0 = part(1, 0, grad_far, (dk0, dv0))
    if eight:
        q_f0, out_got, down_got, a_got, b_got, grad_far = together(
            q_f0, out_got, down_got, a_got, b_got, grad_far
        )
        both = lambda lo, hi: jnp.concatenate(
            [plus(a_keep[lo:hi], a_got[lo:hi]), plus(b_keep[lo:hi], b_got[lo:hi])], axis=-1
        )
        wide_next, wide_keep = by_z(both(2, 4)), both(0, 2)
        down_keep, down_got = plus(down[0][0], down_got[0]), by_x(plus(down[0][1], down_got[1]))
    raw0 = (q_n0, q_f0, k0, v0)
    *terms0, gain_a = qkv_grad_call(count, idx, first_low, raw0, w_full, gains, 0)
    if eight:
        terms0[0], terms0[1], grad_far = together(terms0[0], terms0[1], grad_far)
        out_next = by_y(jnp.concatenate([plus(out_keep[4:], out_got[4:]), terms0[1]], axis=1))
        out_keep = plus(out_keep[:4], out_got[:4])
    q_f1, k1, v1 = part(1, 1, grad_far, (dk1, dv1))
    if eight:
        q_f1, wide_next, out_next = together(q_f1, wide_next, out_next)
        wide_last, wide_keep = by_zz(plus(wide_keep[1], wide_next[1])), plus(wide_keep[0], wide_next[0])
    raw1 = (q_n1, q_f1, k1, v1)
    first_core = back_project((raw0, raw1), w_full, 1)
    first_got = by_core(first_core)
    if eight:
        first_core, q_f1 = together(first_core, q_f1)
    raw1 = (q_n1, q_f1, k1, v1)
    *terms1, gain_b = qkv_grad_call(count, idx, first_low, raw1, w_full, gains, 1)
    if eight:
        terms1[0], terms1[1], first_got, q_f1 = together(terms1[0], terms1[1], first_got, q_f1)
        terms1_got = by_y(terms1[1])
    raw1 = (q_n1, q_f1, k1, v1)
    first_own = back_project((raw0, raw1), w_full, 0)
    if eight:
        first_own, first_got = together(first_own, first_got)
    far_sum = plus(first_own[1], first_got[1])
    first_far = by_x(far_sum)
    gain_terms = jnp.concatenate([gain_a[:1] + gain_b[:1], gain_two[:1]], axis=0)
    final = lambda mine, got: mine.astype(f32) + got.astype(f32)
    crossed = (seq == 1) | (seq == 2)
    cross = [(1, 2), (2, 1)]
    if eight:
        first_own, far_sum, down_got, gain_terms = together(first_own, far_sum, down_got, gain_terms)
        rest = lambda lo, hi: jnp.concatenate(
            [
                plus(down_keep[lo:hi], down_got[lo:hi]),
                plus(out_keep[lo:hi], out_next[lo:hi, :COLS]),
                plus(terms0[0][lo:hi], out_next[lo:hi, COLS:]),
            ],
            axis=1,
        )
        rest_next, rest_keep = by_z(rest(2, 4)), rest(0, 2)
        gain_got = by_core(gain_terms)
        terms1_got, gain_got, down_core = together(terms1_got, gain_got, down_core)
        terms1_next = by_z(plus(terms1[0][2:], terms1_got[2:]))
        terms1_keep = plus(terms1[0][:2], terms1_got[:2])
        gain_terms = gain_terms + gain_got
        gain_got = by_y(gain_terms)
        result = (
            x0.astype(f32)
            + out_own[:rows].astype(f32)
            + out_core[rows:].astype(f32)
            + down_mine.astype(f32)
            + down_core.astype(f32)
        ).astype(bf16)[None]
        rest_next, wide_last, gain_got, result = together(rest_next, wide_last, gain_got, result)
        rest_last, rest_keep = plus(rest_keep[1], rest_next[1]), plus(rest_keep[0], rest_next[0])
        down_last, down_keep = rest_last[:BLOCK], rest_keep[:BLOCK]
        down_last = lax.ppermute(
            down_last,
            ("seq", "shard"),
            [(8 * j + i, 8 * (0, 2, 1, 3)[j] + (i ^ 4)) for j in range(4) for i in range(8)],
        )
        down_moved = lax.ppermute(down_keep, "seq", cross)
        rest_last, rest_keep = by_zz(rest_last[BLOCK:]), rest_keep[BLOCK:]
        gain_terms = gain_terms + gain_got
        gain_got = by_z(gain_terms)
        terms1_next, gain_got, first_far = together(terms1_next, gain_got, first_far)
        terms1_last = by_zz(plus(terms1_keep[1], terms1_next[1]))
        terms1_keep = plus(terms1_keep[0], terms1_next[0])
        gain_terms = gain_terms + gain_got
        gain_terms = gain_terms + by_zz(gain_terms)
        gain_terms = gain_terms + by_x(gain_terms)
        wide_total = final(wide_keep, wide_last)
        rest_total = final(rest_keep, rest_last)
        down_total = final(jnp.where(crossed, down_moved, down_keep), down_last)
        out_total = rest_total[:COLS]
        totals = [rest_total[COLS:], final(terms1_keep, terms1_last)]
    else:
        wide_sum = plus(wide[0][0, 0], by_x(wide[0][1, 0]))
        scatter = lambda value, dim: lax.psum_scatter(
            value, "shard", scatter_dimension=dim, tiled=True
        ).astype(f32)
        wide_total = scatter(wide_sum, 0)
        down_total = scatter(plus(down[0][0, 0], by_x(down[0][1, 0])), 1)
        moved = lax.ppermute(down_total.astype(bf16), "seq", cross).astype(f32)
        down_total = jnp.where(crossed, moved, down_total)
        out_total = scatter(plus(out_keep, by_x(out_send))[0], 1)
        totals = [scatter(terms[0].reshape(3, width, 128), 1) for terms in (terms0, terms1)]
        gain_terms = lax.psum(gain_terms, ("seq", "shard"))
        result = (
            x0.astype(f32)
            + out_own[:rows].astype(f32)
            + out_core[rows:].astype(f32)
            + down_mine.astype(f32)
            + down_core.astype(f32)
        ).astype(bf16)[None]
    input_grad = norm_one_call(x0, res, first_own, first_got, first_far, gains)[None]
    take = width // (4 * shards)
    gain_out = lax.dynamic_slice_in_dim(gain_terms, (seq * shards + shard) * take, take, 1)
    qkv_out = jnp.concatenate([total.reshape(3, piece, 128) for total in totals], axis=2)
    return (
        result,
        input_grad,
        gain_out[0],
        qkv_out,
        out_total,
        gain_out[1],
        wide_total[:, :HALF],
        down_total,
    )


def solution(mesh):
    placed = (
        P("shard", "seq", None),
        P("shard"),
        P(None, "shard", None),
        P("shard", None),
        P("shard"),
        P("shard", None),
        P(None, "shard"),
        P("shard", "seq", None),
    )
    return jax.shard_map(
        per_device,
        mesh=mesh,
        in_specs=placed,
        out_specs=(
            P("shard", "seq", None),
            P("shard", "seq", None),
            P(("seq", "shard")),
            P(None, "shard", "seq"),
            P("seq", "shard"),
            P(("seq", "shard")),
            P("shard", "seq"),
            P("seq", "shard"),
        ),
        check_vma=False,
    )
```

```python
from functools import partial
import math

import jax
import jax.numpy as jnp
from jax import lax
from jax.experimental import pallas as pl
from jax.experimental.pallas import tpu as pltpu
from jax.sharding import PartitionSpec as P

HEADS = 16
HD = 64
FF = 2624

epsilon = 1e-05
rope_base = 160000.0

f32 = jnp.float32
bf16 = jnp.bfloat16

WIDTH = 1024
HALF = FF // 2
PADDED = 1408
BLOCK = FF // 4
COLS = 256
CHUNKS = (0, 4, 2, 6, 1, 5, 3, 7)
SPLIT = 768
EXTRA = 16
ROWS_BY_COLS = (((0,), (0,)), ((), ()))
COLS_BY_COLS = (((1,), (1,)), ((), ()))
VMEM_LIMIT = 58 * 1024 * 1024

ANY = pl.BlockSpec(memory_space=pl.ANY)
SMEM = pl.BlockSpec(memory_space=pltpu.SMEM)


def cost(micros):
    return pl.CostEstimate(flops=int(micros), transcendentals=0, bytes_accessed=int(micros))


def params():
    return pltpu.CompilerParams(vmem_limit_bytes=VMEM_LIMIT)


def sds(shape, dtype=bf16):
    return jax.ShapeDtypeStruct(shape, dtype)


def aligned(index, size):
    return pl.ds(pl.multiple_of(index * size, size), size)


def normalize(values):
    center = values - jnp.mean(values, axis=-1, keepdims=True)
    inv_scale = lax.rsqrt(jnp.mean(center * center, axis=-1, keepdims=True) + epsilon)
    return center * inv_scale, inv_scale


def norm_back(grads, xhat, inv_scale):
    mean_grad = jnp.mean(grads, axis=-1, keepdims=True)
    mean_both = jnp.mean(grads * xhat, axis=-1, keepdims=True)
    return inv_scale * (grads - mean_grad - xhat * mean_both)


def turned(values):
    lane = lax.broadcasted_iota(jnp.int32, values.shape, 1)
    width = values.shape[1]
    return jnp.where(
        lane % HD < HD // 2, pltpu.roll(values, width - HD // 2, 1), pltpu.roll(values, HD // 2, 1)
    )


def twice(table):
    return jnp.concatenate([table, table], axis=1)


def piece_of(refs, place, rows=None, width=None):
    array, lead, column = place
    index = () if lead is None else (lead,)
    rows = slice(None) if rows is None else rows
    cols = slice(None) if width is None else pl.ds(column, width)
    return refs[array].at[(*index, rows, cols)]


def fetch_rows(count, idx, refs, places, width, target, sem):
    size = target.shape[0] // count
    copies = []
    for r in range(count):
        rows = aligned(idx[4 + r], size) if count > 1 else pl.ds(0, size)
        copies.append(
            pltpu.make_async_copy(piece_of(refs, places[r], width=width), target.at[rows], sem.at[r])
        )
    return copies


def qkv_kernel(count, places, idx, *refs):
    x_refs, refs = refs[:4], refs[4:]
    n_arrays = 1 + max(array for array, _, _ in places)
    w_refs, refs = refs[:n_arrays], refs[n_arrays:]
    if count == 1:
        gain_ref, refs = refs[0], refs[1:]
    cos_ref, sin_ref, fn_o, q_o, k_o, v_o, w_o, g_o, xs, gs, semx, semw, semg = refs
    step = pl.program_id(0)
    shard = idx[0]
    size = WIDTH // count

    def x_copy(r):
        return pltpu.make_async_copy(x_refs[r], xs.at[r], semx.at[r])

    def w_copy(r):
        return pltpu.make_async_copy(
            piece_of(w_refs, places[r], rows=pl.ds(0, size)), w_o.at[aligned(jnp.bitwise_xor(shard, r), size)], semw.at[r]
        )

    def g_copy(r):
        return pltpu.make_async_copy(
            piece_of(w_refs, places[r], rows=pl.ds(size, EXTRA)), gs.at[jnp.bitwise_xor(shard, r)], semg.at[r]
        )

    @pl.when(step == 0)
    def _():
        if count == 1:
            w_all = pltpu.make_async_copy(w_refs[0], w_o, semw.at[0])
            w_all.start()
        else:
            for r in range(count):
                w_copy(r).start()
                g_copy(r).start()
        for r in range(4):
            x_copy(r).start()
        if count == 1:
            w_all.wait()
            g_o[0:1] = gain_ref[0:1].astype(f32)
            g_o[1:2] = gain_ref[1:2].astype(f32)
        else:
            for r in range(count):
                w_copy(r).wait()
                g_copy(r).wait()
            for r in range(count):
                part = gs[r].astype(f32)
                g_o[0:1, r * size : (r + 1) * size] = part[0:1, 0:size]
                g_o[1:2, r * size : (r + 1) * size] = part[0:1, size : 2 * size]

    for r in range(4):

        @pl.when(step == r)
        def _():
            x_copy(r).wait()

    xhat, _ = normalize(xs[step].astype(f32))
    first_low = (xhat * g_o[0:1]).astype(bf16)
    fn_o[...] = first_low
    cosine, sine = twice(cos_ref[...]), twice(sin_ref[...])
    outs = (q_o, k_o, v_o)
    for part in range(3):
        value = jnp.dot(first_low, w_o[:, part * COLS : (part + 1) * COLS], preferred_element_type=f32)
        if part < 2:
            value = value * cosine + turned(value) * sine
        value = value.astype(bf16)
        if part == 0:
            value = value * jnp.asarray(1.0 / math.sqrt(HD), bf16)
        outs[part][...] = value


def qkv_call(count, idx, chunks, pieces, gains, cosine, sine):
    arrays, where = pieces
    rows = chunks[0].shape[0]
    by_step = lambda width: pl.BlockSpec((rows, width), lambda r: (r, 0))
    whole = lambda shape: pl.BlockSpec(shape, lambda r: (0, 0))
    extra = [] if count > 1 else [gains]
    return pl.pallas_call(
        partial(qkv_kernel, count, where),
        grid=(4,),
        in_specs=[SMEM]
        + [ANY] * (4 + len(arrays))
        + ([] if count > 1 else [whole((2, WIDTH))])
        + [by_step(128), by_step(128)],
        out_specs=[
            by_step(WIDTH),
            by_step(COLS),
            by_step(COLS),
            by_step(COLS),
            whole((WIDTH, 3 * COLS)),
            whole((8, WIDTH)),
        ],
        out_shape=[
            sds((4 * rows, WIDTH)),
            sds((4 * rows, COLS)),
            sds((4 * rows, COLS)),
            sds((4 * rows, COLS)),
            sds((WIDTH, 3 * COLS)),
            sds((8, WIDTH), f32),
        ],
        scratch_shapes=[
            pltpu.VMEM((4, rows, WIDTH), bf16),
            pltpu.VMEM((8, EXTRA, 3 * COLS), bf16),
            pltpu.SemaphoreType.DMA((4,)),
            pltpu.SemaphoreType.DMA((count,)),
            pltpu.SemaphoreType.DMA((count,)),
        ],
        compiler_params=params(),
        cost_estimate=cost(11),
        name="project",
    )(idx, *chunks, *arrays, *extra, cosine, sine)


def head_of(shape):
    return lax.broadcasted_iota(jnp.int32, shape, len(shape) - 1) // HD


def attend_kernel(q_ref, k_ref, v_ref, o_ref, lse_ref):
    q, k, v = q_ref[...], k_ref[...], v_ref[...]
    heads = head_of(q.shape)
    total = jnp.zeros(q.shape, f32)
    lses = jnp.zeros((q.shape[0], 128), f32)
    lane = lax.broadcasted_iota(jnp.int32, lses.shape, 1)
    for h in range(COLS // HD):
        q_h = jnp.where(heads == h, q, jnp.zeros_like(q))
        scores = lax.dot_general(q_h, k, COLS_BY_COLS, preferred_element_type=f32)
        row_max = jnp.max(scores, axis=1, keepdims=True)
        exponent = jnp.exp(scores - row_max)
        row_total = jnp.sum(exponent, axis=1, keepdims=True)
        context = jnp.dot(exponent.astype(bf16), v, preferred_element_type=f32)
        total = jnp.where(heads == h, context * (1.0 / row_total), total)
        lses = jnp.where(lane == h, row_max + jnp.log(row_total), lses)
    o_ref[...] = total.astype(bf16)
    lse_ref[...] = lses.T[:8]


def attend(q, k, v, chunk, after=()):
    span = k.shape[0]
    rows = span // 4
    kept = pl.BlockSpec((span, COLS), lambda i: (0, 0))
    return pl.pallas_call(
        lambda *refs: attend_kernel(*refs[:3], *refs[3 + len(after) :]),
        grid=(1,),
        in_specs=[pl.BlockSpec((rows, COLS), lambda i: (chunk, 0)), kept, kept] + [ANY] * len(after),
        out_specs=[
            pl.BlockSpec((rows, COLS), lambda i: (0, 0)),
            pl.BlockSpec((8, rows), lambda i: (0, 0)),
        ],
        out_shape=[sds((rows, COLS)), sds((8, rows), f32)],
        compiler_params=params(),
        cost_estimate=cost(8),
        name="attend",
    )(q, k, v, *after)


def attend_back_kernel(last, pair, *refs):
    q_ref, do_ref, oa_ref, ob_ref, la_ref, lb_ref, k_ref, v_ref, qcos, qsin, refs = *refs[:10], refs[10:]
    if last:
        dk_i, dv_i, kcos, ksin, refs = *refs[:4], refs[4:]
    dq_ref, dk_ref, dv_ref, do_s, inner_s, lse_s, dq_s = refs
    step = pl.program_id(0)
    width = q_ref.shape[1]
    n_heads = width // HD

    @pl.when(step == 0)
    def _():
        do = do_ref[...]
        context = jnp.concatenate([oa_ref[...], ob_ref[...]], axis=0)
        product = do.astype(f32) * context.astype(f32)
        high = product.astype(bf16)
        rest = (product - high.astype(f32)).astype(bf16)
        chosen = (
            head_of((8, width)) == lax.broadcasted_iota(jnp.int32, (8, width), 0)
        ).astype(bf16)
        inner_s[...] = lax.dot_general(
            chosen, high, COLS_BY_COLS, preferred_element_type=f32
        ) + lax.dot_general(chosen, rest, COLS_BY_COLS, preferred_element_type=f32)
        lse_s[...] = jnp.concatenate([la_ref[...], lb_ref[...]], axis=1)
        heads = head_of(do.shape)
        for h in range(n_heads):
            do_s[h] = jnp.where(heads == h, do, jnp.zeros_like(do))
        dq_s[...] = jnp.zeros_like(dq_s)

    q, k, v = q_ref[...], k_ref[...], v_ref[...]
    heads = head_of(k.shape)
    dk = jnp.zeros(k.shape, f32)
    dv = jnp.zeros(k.shape, f32)
    dq = dq_s[...]
    for h in range(n_heads):
        at = n_heads * pair + h
        k_h = jnp.where(heads == h, k, jnp.zeros_like(k))
        scores = lax.dot_general(k_h, q, COLS_BY_COLS, preferred_element_type=f32)
        probs = jnp.exp(scores - lse_s[at : at + 1, :])
        probs_grad = lax.dot_general(v, do_s[h], COLS_BY_COLS, preferred_element_type=f32)
        scores_grad = (probs * (probs_grad - inner_s[h : h + 1, :])).astype(bf16)
        dv = dv + jnp.dot(probs.astype(bf16), do_s[h], preferred_element_type=f32)
        dk = jnp.where(heads == h, jnp.dot(scores_grad, q, preferred_element_type=f32), dk)
        dq = dq + lax.dot_general(scores_grad, k_h, ROWS_BY_COLS, preferred_element_type=f32)
    dq_s[...] = dq
    if last:
        dk = dk + dk_i[...]
        dv = dv + dv_i[...]
        dk_ref[...] = (dk * kcos[...] - turned(dk) * ksin[...]).astype(bf16)
        dv_ref[...] = dv.astype(bf16)
    else:
        dk_ref[...] = dk
        dv_ref[...] = dv

    @pl.when(step == pl.num_programs(0) - 1)
    def _():
        dq = dq_s[...] * (1.0 / math.sqrt(HD))
        dq_ref[...] = (dq * qcos[...] - turned(dq) * qsin[...]).astype(bf16)


def attend_back(part, pair, q, do, contexts, lses, k, v, cosine, sine, earlier=None, after=(), tile=512):
    span = k.shape[0]
    rows = do.shape[0]
    last = earlier is not None
    rows_at = lambda at, col, count=rows, width=128: pl.BlockSpec((count, width), lambda i: (at, col))
    keys = lambda col: pl.BlockSpec((tile, 128), lambda i: (i, col))
    grads = bf16 if last else f32
    n_in = 10 + (4 if last else 0)
    return pl.pallas_call(
        lambda *refs: attend_back_kernel(last, pair, *refs[:n_in], *refs[n_in + len(after) :]),
        grid=(span // tile,),
        in_specs=[
            rows_at(part, pair),
            rows_at(0, pair),
            rows_at(0, pair, rows // 2),
            rows_at(0, pair, rows // 2),
            rows_at(0, 0, 8, rows // 2),
            rows_at(0, 0, 8, rows // 2),
            keys(pair),
            keys(pair),
            rows_at(part, 0),
            rows_at(part, 0),
        ]
        + ([keys(0), keys(0), keys(0), keys(0)] if last else [])
        + [ANY] * len(after),
        out_specs=[rows_at(0, 0), keys(0), keys(0)],
        out_shape=[sds((rows, 128)), sds((span, 128), grads), sds((span, 128), grads)],
        scratch_shapes=[
            pltpu.VMEM((128 // HD, rows, 128), bf16),
            pltpu.VMEM((8, rows), f32),
            pltpu.VMEM((8, rows), f32),
            pltpu.VMEM((rows, 128), f32),
        ],
        compiler_params=params(),
        cost_estimate=cost(15),
        name="attend_back",
    )(q, do, *contexts, *lses, k, v, cosine, sine, *((*earlier, cosine, sine) if last else ()), *after)


def out_kernel(count, places, idx, ma_ref, mb_ref, oa_ref, ob_ref, *refs):
    w_refs, (o_ref, wsel_ref, w_s, sem) = refs[:-4], refs[-4:]
    copies = fetch_rows(count, idx, w_refs, places, WIDTH, w_s, sem)
    for copy in copies:
        copy.start()
    for copy in copies:
        copy.wait()
    seq = idx[1]
    wsel_ref[0:COLS] = w_s[aligned(seq, COLS)]
    wsel_ref[COLS:] = w_s[aligned(jnp.bitwise_xor(seq, 2), COLS)]
    rows = ma_ref.shape[0]
    for r, (mine, other) in enumerate(((ma_ref, oa_ref), (mb_ref, ob_ref))):
        both = jnp.concatenate([mine[...], other[...]], axis=1)
        value = jnp.dot(both, wsel_ref[...], preferred_element_type=f32)
        o_ref[r * rows : (r + 1) * rows] = value.astype(bf16)


def out_call(count, idx, mine, other, pieces):
    vmem = pl.BlockSpec(memory_space=pltpu.VMEM)
    arrays, where = pieces
    return pl.pallas_call(
        partial(out_kernel, count, where),
        in_specs=[SMEM] + [vmem] * 4 + [ANY] * len(arrays),
        out_specs=[vmem, vmem],
        out_shape=[sds((2 * mine[0].shape[0], WIDTH)), sds((2 * COLS, WIDTH))],
        scratch_shapes=[pltpu.VMEM((WIDTH, WIDTH), bf16), pltpu.SemaphoreType.DMA((count,))],
        compiler_params=params(),
        cost_estimate=cost(5),
        name="out_project",
    )(idx, *mine, *other, *arrays)


def mlp_kernel(count, n_arrays, mine, other, down, idx, *refs):
    x0, x1, po, pr, c0, c1, g_ref, refs = *refs[:7], refs[7:]
    w_refs, refs = refs[:n_arrays], refs[n_arrays:]
    hid_o, sgp_o, wd_o, refs = *refs[:3], refs[3:]
    grads, refs = (refs[:4], refs[4:]) if count > 1 else (refs[:1], refs[1:])
    xs, pos, prs, cs, wi, wd, sn_s, hid_s, gug_s, sgp_s, turned_s, acc, refs = *refs[:12], refs[12:]
    sem_a, sem_m, sem_i, sem_d, sem_o = refs
    shard, x_place = idx[0], idx[2]
    rows = xs.shape[1]
    loads = [
        pltpu.make_async_copy(x0, xs.at[0], sem_a.at[0]),
        pltpu.make_async_copy(x1, xs.at[1], sem_a.at[1]),
        pltpu.make_async_copy(po, pos, sem_a.at[2]),
        pltpu.make_async_copy(pr, prs, sem_a.at[3]),
        pltpu.make_async_copy(c0, cs.at[pl.ds(0, rows)], sem_a.at[4]),
        pltpu.make_async_copy(c1, cs.at[pl.ds(rows, rows)], sem_a.at[5]),
    ]
    here = wi.at[:, aligned(x_place, PADDED)]
    there = wi.at[:, aligned(1 - x_place, PADDED)]
    wi_loads = fetch_rows(count, idx, w_refs, mine, PADDED, here, sem_m)
    wi_loads += fetch_rows(count, idx, w_refs, other, PADDED, there, sem_i)
    wd_loads = fetch_rows(count, idx, w_refs, down, PADDED, wd, sem_d)
    for copy in loads[:4] + wi_loads + loads[4:] + wd_loads:
        copy.start()
    for copy in loads[:4]:
        copy.wait()
    for r in range(2):
        here, there = pl.ds(r * rows, rows), pl.ds((1 - r) * rows, rows)
        after = xs[r].astype(f32) + pos[here].astype(f32) + prs[there].astype(f32)
        xhat, _ = normalize(after)
        sn_s[here] = (xhat * g_ref[1:2]).astype(bf16)
    stores = []

    def store(source, target):
        copy = pltpu.make_async_copy(source, target, sem_o.at[len(stores)])
        copy.start()
        stores.append(copy)

    turned_s[...] = sn_s[...].T
    for copy in wi_loads + loads[4:] + wd_loads:
        copy.wait()
    store(wd, wd_o)
    start = 0
    while start < PADDED:
        size = min(256, PADDED - start)
        here = pl.ds(start, size)
        gate = jnp.dot(sn_s[...], wi[:, here], preferred_element_type=f32)
        up = jnp.dot(sn_s[...], wi[:, pl.ds(PADDED + start, size)], preferred_element_type=f32)
        back = jnp.dot(cs[...], wd[:, here], preferred_element_type=f32)
        below = 0.5 * (1.0 + lax.erf(gate * math.sqrt(0.5)))
        density = jnp.exp(-0.5 * gate * gate) * (1.0 / math.sqrt(2.0 * math.pi))
        unit = gate * below
        hid_s[:, here] = (unit * up).astype(bf16)
        gug_s[0, :, here] = (back * up * (below + gate * density)).astype(bf16)
        gug_s[1, :, here] = (back * unit).astype(bf16)
        start += size
    store(hid_s, hid_o)
    value = lax.dot_general(gug_s[0], wi[:, :PADDED], COLS_BY_COLS, preferred_element_type=f32)
    value = value + lax.dot_general(gug_s[1], wi[:, PADDED:], COLS_BY_COLS, preferred_element_type=f32)
    sgp_s[...] = value.astype(bf16)
    store(sgp_s, sgp_o)
    size = WIDTH // count
    for part in range(2):
        terms = gug_s[jnp.bitwise_xor(x_place, part)]
        acc[part] = jnp.dot(turned_s[...], terms, preferred_element_type=f32).astype(bf16)
        if count == 1:
            store(acc.at[part], grads[0].at[part, 0])
            continue
        keep_a, send_a, keep_b, send_b = grads
        for k, r in enumerate(CHUNKS):
            place = aligned(jnp.bitwise_xor(shard, r), size)
            store(acc.at[part, place, pl.ds(0, SPLIT)], (keep_a, send_a)[k // 4].at[part, k % 4])
            store(acc.at[part, place, pl.ds(SPLIT, PADDED - SPLIT)], (keep_b, send_b)[part].at[k])
    for copy in stores:
        copy.wait()


def mlp_call(count, idx, x0, x1, po, pr, c0, c1, gains, arrays, mine, other, down):
    rows = x0.shape[0]
    size = WIDTH // count
    grads = [sds((2, 4, size, SPLIT))] * 2 + [sds((8, size, PADDED - SPLIT))] * 2
    if count == 1:
        grads = [sds((2, 1, WIDTH, PADDED))]
    return pl.pallas_call(
        partial(mlp_kernel, count, len(arrays), mine, other, down),
        in_specs=[SMEM] + [ANY] * 6 + [pl.BlockSpec(memory_space=pltpu.VMEM)] + [ANY] * len(arrays),
        out_specs=[ANY] * (3 + len(grads)),
        out_shape=[sds((2 * rows, PADDED)), sds((2 * rows, WIDTH)), sds((WIDTH, PADDED))] + grads,
        scratch_shapes=[
            pltpu.VMEM((2, rows, WIDTH), bf16),
            pltpu.VMEM((2 * rows, WIDTH), bf16),
            pltpu.VMEM((2 * rows, WIDTH), bf16),
            pltpu.VMEM((2 * rows, WIDTH), bf16),
            pltpu.VMEM((WIDTH, 2 * PADDED), bf16),
            pltpu.VMEM((WIDTH, PADDED), bf16),
            pltpu.VMEM((2 * rows, WIDTH), bf16),
            pltpu.VMEM((2 * rows, PADDED), bf16),
            pltpu.VMEM((2, 2 * rows, PADDED), bf16),
            pltpu.VMEM((2 * rows, WIDTH), bf16),
            pltpu.VMEM((WIDTH, 2 * rows), bf16),
            pltpu.VMEM((2, WIDTH, PADDED), bf16),
            pltpu.SemaphoreType.DMA((6,)),
            pltpu.SemaphoreType.DMA((count,)),
            pltpu.SemaphoreType.DMA((count,)),
            pltpu.SemaphoreType.DMA((count,)),
            pltpu.SemaphoreType.DMA((40,)),
        ],
        compiler_params=params(),
        cost_estimate=cost(25),
        name="feed_forward",
    )(idx, x0, x1, po, pr, c0, c1, gains, *arrays)


def down_kernel(count, idx, *refs):
    sources, refs = refs[:4], refs[4:]
    res_other, res_mine, refs = *refs[:2], refs[2:]
    downs, refs = refs[: 2 if count > 1 else 1], refs[2 if count > 1 else 1 :]
    hid, wd, cs, acc, res, sem_i, sem_o = refs
    shard, x_place = idx[0], idx[2]
    rows = cs.shape[0] // 2
    width = WIDTH // count
    targets = [hid, wd, cs.at[pl.ds(0, rows)], cs.at[pl.ds(rows, rows)]]
    loads = [pltpu.make_async_copy(*pair, sem_i.at[k]) for k, pair in enumerate(zip(sources, targets))]
    for k in (0, 2, 3, 1):
        loads[k].start()
    places = [
        aligned(jnp.bitwise_xor(shard, r), width) if count > 1 else pl.ds(0, width) for r in CHUNKS[:count]
    ]
    stores = []

    def store(source, target):
        copy = pltpu.make_async_copy(source, target, sem_o.at[len(stores)])
        copy.start()
        stores.append(copy)

    for k in (0, 2, 3):
        loads[k].wait()
    acc[...] = lax.dot_general(hid[...], cs[...], ROWS_BY_COLS, preferred_element_type=f32).astype(bf16)
    for part in range(2):
        here = pl.ds(pl.multiple_of(jnp.bitwise_xor(x_place, part) * BLOCK, 16), BLOCK)
        for r in range(count):
            store(acc.at[here, places[r]], downs[r // 4].at[part, r % 4])
    loads[1].wait()
    for r, target in ((1, res_other), (0, res_mine)):
        res[r] = lax.dot_general(
            hid[r * rows : (r + 1) * rows], wd[...], COLS_BY_COLS, preferred_element_type=f32
        ).astype(bf16)
        store(res.at[r], target)
    for copy in stores:
        copy.wait()


def down_call(count, idx, hidden, wd, c0, c1):
    rows = c0.shape[0]
    split = 2 if count > 1 else 1
    return pl.pallas_call(
        partial(down_kernel, count),
        in_specs=[SMEM] + [ANY] * 4,
        out_specs=[ANY] * (2 + split),
        out_shape=[sds((rows, WIDTH))] * 2
        + [sds((2, count // split, BLOCK, WIDTH // count))] * split,
        scratch_shapes=[
            pltpu.VMEM((2 * rows, PADDED), bf16),
            pltpu.VMEM((WIDTH, PADDED), bf16),
            pltpu.VMEM((2 * rows, WIDTH), bf16),
            pltpu.VMEM((PADDED, WIDTH), bf16),
            pltpu.VMEM((2, rows, WIDTH), bf16),
            pltpu.SemaphoreType.DMA((4,)),
            pltpu.SemaphoreType.DMA((2 * count + 2,)),
        ],
        compiler_params=params(),
        cost_estimate=cost(15),
        name="down_project",
    )(idx, hidden, wd, c0, c1)


def norm_two_kernel(x0, x1, po, pr, so, sr, c0, c1, g_ref, wsel, res_o, low_o, mine_o, other_o, gain_o):
    step = pl.program_id(0)
    half = pl.num_programs(0) // 2
    first = step < half
    gain = g_ref[1:2]
    x = jnp.where(first, x0[...], x1[...])
    c = jnp.where(first, c0[...], c1[...])
    after = x.astype(f32) + po[...].astype(f32) + pr[...].astype(f32)
    xhat, inv_scale = normalize(after)
    second = so[...].astype(f32) + sr[...].astype(f32)
    res = c.astype(f32) + norm_back(second * gain, xhat, inv_scale)

    @pl.when(step == 0)
    def _():
        gain_o[...] = jnp.zeros_like(gain_o)

    @pl.when(first)
    def _():
        res_o[...] = res
        gain_o[...] += jnp.sum(second * xhat, axis=0, keepdims=True)

    low = res.astype(bf16)
    low_o[...] = low
    value = lax.dot_general(low, wsel[...], COLS_BY_COLS, preferred_element_type=f32).astype(bf16)
    mine_o[...] = value[:, :COLS]
    other_o[...] = value[:, COLS:]


def norm_two_call(x0, x1, po, pr, so, sr, c0, c1, gains, wsel, half=2):
    rows = x0.shape[0]
    size = rows // half
    spec = lambda width, at: pl.BlockSpec((size, width), lambda s: (at(s), 0))
    lower = lambda s: jnp.minimum(s, half - 1)
    upper = lambda s: jnp.maximum(s - half, 0)
    same = lambda s: s
    other = lambda s: lax.rem(s + half, 2 * half)
    whole = lambda shape: pl.BlockSpec(shape, lambda s: (0, 0))
    return pl.pallas_call(
        norm_two_kernel,
        grid=(2 * half,),
        in_specs=[
            spec(WIDTH, lower),
            spec(WIDTH, upper),
            spec(WIDTH, same),
            spec(WIDTH, other),
            spec(WIDTH, same),
            spec(WIDTH, other),
            spec(WIDTH, lower),
            spec(WIDTH, upper),
            whole((8, WIDTH)),
            whole((2 * COLS, WIDTH)),
        ],
        out_specs=[
            spec(WIDTH, lower),
            spec(WIDTH, same),
            spec(COLS, same),
            spec(COLS, same),
            whole((8, WIDTH)),
        ],
        out_shape=[
            sds((rows, WIDTH), f32),
            sds((2 * rows, WIDTH)),
            sds((2 * rows, COLS)),
            sds((2 * rows, COLS)),
            sds((8, WIDTH), f32),
        ],
        compiler_params=params(),
        cost_estimate=cost(8),
        name="norm_two_back",
    )(x0, x1, po, pr, so, sr, c0, c1, gains, wsel)


def out_grad_kernel(count, idx, ma, mb, oa, ob, low, keep_o, send_o, acc):
    shard = idx[0]
    width = WIDTH // count
    for (first, second), target in (((oa, ob), send_o), ((ma, mb), keep_o)):
        context = jnp.concatenate([first[...], second[...]], axis=0)
        acc[...] = lax.dot_general(context, low[...], ROWS_BY_COLS, preferred_element_type=f32)
        for k, r in enumerate(CHUNKS[:count]):
            place = aligned(jnp.bitwise_xor(shard, r), width) if count > 1 else pl.ds(0, width)
            target[k] = acc[:, place].astype(bf16)


def out_grad_call(count, idx, mine, other, low):
    vmem = pl.BlockSpec(memory_space=pltpu.VMEM)
    return pl.pallas_call(
        partial(out_grad_kernel, count),
        in_specs=[SMEM] + [vmem] * 5,
        out_specs=[vmem] * 2,
        out_shape=[sds((count, COLS, WIDTH // count))] * 2,
        scratch_shapes=[pltpu.VMEM((COLS, WIDTH), f32)],
        compiler_params=params(),
        cost_estimate=cost(4),
        name="out_grad",
    )(idx, *mine, *other, low)


def back_project_kernel(q0, q1, f0, f1, k0n, k1n, k0f, k1f, v0n, v1n, v0f, v1f, w_ref, both_o):
    for half, parts in (
        (1, (f0, f1, k0f, k1f, v0f, v1f)),
        (0, (q0, q1, k0n, k1n, v0n, v1n)),
    ):
        raw = jnp.concatenate([part[...] for part in parts], axis=1)
        both_o[half] = lax.dot_general(
            raw, w_ref[...], COLS_BY_COLS, preferred_element_type=f32
        ).astype(bf16)


def back_project(raw_pairs, w, chunk):
    rows = raw_pairs[0][0].shape[0] // 2
    at = lambda where: pl.BlockSpec((rows, 128), lambda i: (where, 0))
    q0, f0, k0, v0 = raw_pairs[0]
    q1, f1, k1, v1 = raw_pairs[1]
    return pl.pallas_call(
        back_project_kernel,
        grid=(1,),
        in_specs=[at(chunk)] * 6
        + [at(chunk + 2)] * 2
        + [at(chunk)] * 2
        + [at(chunk + 2)] * 2
        + [pl.BlockSpec((WIDTH, 3 * COLS), lambda i: (0, 0))],
        out_specs=pl.BlockSpec((2, rows, WIDTH), lambda i: (0, 0, 0)),
        out_shape=sds((2, rows, WIDTH)),
        compiler_params=params(),
        cost_estimate=cost(5),
        name="back_project",
    )(q0, q1, f0, f1, k0, k1, k0, k1, v0, v1, v0, v1, w)


def qkv_grad_kernel(count, idx, fn_ref, qn, qf, k_ref, v_ref, wq, wk, wv, g_ref, keep_o, *refs):
    if count > 1:
        send_o, gain_o, acc = refs
    else:
        gain_o, acc = refs
    rows = qn.shape[0]
    q = jnp.concatenate([qn[...], qf[...]], axis=0)
    raw = jnp.concatenate([q, k_ref[...], v_ref[...]], axis=1)
    acc[...] = lax.dot_general(fn_ref[...], raw, ROWS_BY_COLS, preferred_element_type=f32)
    shard = idx[0]
    size = WIDTH // count
    for k, r in enumerate(CHUNKS[:count]):
        place = aligned(jnp.bitwise_xor(shard, r), size) if count > 1 else pl.ds(0, size)
        target = (keep_o, send_o)[k // 4] if count > 1 else keep_o
        for part in range(3):
            value = acc[place, part * 128 : (part + 1) * 128]
            target[k % 4, part * size : (part + 1) * size] = value.astype(bf16)
    w = jnp.concatenate([wq[...], wk[...], wv[...]], axis=1)
    both = acc[...] * w.astype(f32)
    high = both.astype(bf16)
    rest = (both - high.astype(f32)).astype(bf16)
    ones = jnp.ones((8, w.shape[1]), bf16)
    total = lax.dot_general(ones, high, COLS_BY_COLS, preferred_element_type=f32)
    total += lax.dot_general(ones, rest, COLS_BY_COLS, preferred_element_type=f32)
    gain_o[...] = total / g_ref[0:1]


def qkv_grad_call(count, idx, first_low, raw, w, gains, pair):
    vmem = pl.BlockSpec(memory_space=pltpu.VMEM)
    split = 2 if count > 1 else 1
    size = WIDTH // count
    width = 3 * 128
    whole = lambda shape: pl.BlockSpec(shape, lambda i: (0,) * len(shape))
    weight = lambda part: pl.BlockSpec((WIDTH, 128), lambda i: (0, 2 * part + pair))
    grads = [(count // split, 3 * size, 128)] * split + [(8, WIDTH)]
    return pl.pallas_call(
        partial(qkv_grad_kernel, count),
        grid=(1,),
        in_specs=[SMEM, whole(first_low.shape)]
        + [whole(value.shape) for value in raw]
        + [weight(0), weight(1), weight(2), whole(gains.shape)],
        out_specs=[whole(shape) for shape in grads],
        out_shape=[sds(shape) for shape in grads[:-1]] + [sds(grads[-1], f32)],
        scratch_shapes=[pltpu.VMEM((WIDTH, width), f32)],
        compiler_params=params(),
        cost_estimate=cost(6),
        name="project_grad",
    )(idx, first_low, *raw, w, w, w, gains)


def norm_one_kernel(x_ref, res_ref, own, core, far, g_ref, o_ref):
    xhat, inv_scale = normalize(x_ref[...].astype(f32))
    first = own[0].astype(f32) + core[0].astype(f32) + far[...].astype(f32)
    o_ref[...] = res_ref[...] + norm_back(first * g_ref[0:1], xhat, inv_scale)


def norm_one_call(x, res, own, core, far, gains, steps=2):
    rows = x.shape[0]
    block = pl.BlockSpec((rows // steps, WIDTH), lambda i: (i, 0))
    return pl.pallas_call(
        norm_one_kernel,
        grid=(steps,),
        in_specs=[
            block,
            block,
            pl.BlockSpec((1, rows // steps, WIDTH), lambda i: (0, i, 0)),
            pl.BlockSpec((1, rows // steps, WIDTH), lambda i: (0, i, 0)),
            block,
            pl.BlockSpec((8, WIDTH), lambda i: (0, 0)),
        ],
        out_specs=block,
        out_shape=sds(res.shape, f32),
        compiler_params=params(),
        cost_estimate=cost(3),
        name="norm_one_back",
    )(x, res, own, core, far, gains)


def swap(value, axis, bits):
    size = lax.axis_size(axis)
    return lax.ppermute(value, axis, [(place, place ^ bits) for place in range(size)])


def plus(left, right):
    return (left.astype(f32) + right.astype(f32)).astype(bf16)


def together(*values):
    return lax.optimization_barrier(values)


def per_device(inputs, attn_gain, qkv_weight, out_weight, mlp_gain, in_weight, mlp_out, cotangent):
    _, rows, width = inputs.shape
    shards = lax.axis_size("shard")
    eight = shards == 8
    count = 8 if eight else 1
    piece = width // shards
    seq, shard = lax.axis_index("seq"), lax.axis_index("shard")
    x_place, core = seq // 2, seq % 2
    owners = [jnp.bitwise_xor(lax.rem(shard + 8 - 2 * (r % 4), 8), r // 4) for r in range(8)]
    idx = jnp.stack([shard, seq, x_place, core, *owners]).astype(jnp.int32)

    order = jnp.bitwise_xor(seq, jnp.arange(4))
    places = (order[:, None] * rows + jnp.arange(rows)[None, :]).reshape(-1)
    frequency = 1.0 / rope_base ** (jnp.arange(0, HD, 2, dtype=f32) / HD)
    angles = places.astype(f32)[:, None] * jnp.tile(frequency, 4)[None, :]
    sign = jnp.where(jnp.arange(128) % HD < HD // 2, -1.0, 1.0)
    cosine, sine = jnp.cos(angles), jnp.sin(angles) * sign

    x0 = inputs[0]
    c0 = cotangent[0]
    w_qkv = lax.dynamic_slice_in_dim(qkv_weight, seq * COLS, COLS, 2)
    w_qkv = jnp.transpose(w_qkv, (1, 0, 2)).reshape(piece, 3 * COLS)
    w_in = in_weight.reshape(piece, 2, 2, HALF)
    w_in = lax.dynamic_index_in_dim(w_in, core, 2, keepdims=False)
    w_in = jnp.pad(w_in, ((0, 0), (0, 0), (0, PADDED - HALF)))
    w_mine = lax.dynamic_index_in_dim(w_in, x_place, 1, keepdims=False)
    w_other = lax.dynamic_index_in_dim(w_in, 1 - x_place, 1, keepdims=False)
    w_down = lax.dynamic_slice_in_dim(mlp_out, core * HALF, HALF, 0).T
    w_down = jnp.pad(w_down, ((0, 0), (0, PADDED - HALF)))

    x2 = swap(x0, "seq", 2)
    by_y = lambda value: swap(value, "shard", 1)
    by_z = lambda value: swap(value, "shard", 2)
    by_zz = lambda value: swap(value, "shard", 4)
    by_x = lambda value: swap(value, "seq", 2)
    by_core = lambda value: swap(value, "seq", 1)
    if eight:
        gain_rows = jnp.concatenate([attn_gain, mlp_gain, jnp.zeros(3 * COLS - 2 * piece, bf16)])[None]
        a0 = jnp.concatenate([w_qkv, jnp.pad(gain_rows, ((0, EXTRA - 1), (0, 0)))], axis=0)
        f0 = jnp.concatenate([w_mine, out_weight, w_down], axis=1)
        narrow = lambda value: value[..., :PADDED]
        ring = lambda value: lax.ppermute(
            value, "shard", [(place, (place + 2) % 8) for place in range(8)]
        )
        a4, a2, a1 = by_zz(a0), by_z(a0), by_y(a0)
        a4, a2, a1, x0, cosine, sine, idx, f0, w_other = together(
            a4, a2, a1, x0, cosine, sine, idx, f0, w_other
        )
        a6, a35 = by_z(a4), by_y(jnp.stack([a2, a4]))
        x1 = by_core(x0)
        a6, a35, x2 = together(a6, a35, x2)
        a7 = by_y(a6)
        x3 = by_core(x2)
        x3, x1, a7, f0 = together(x3, x1, a7, f0)
        f1, f4 = ring(f0), by_y(f0)
        c1 = by_core(c0)
        first_low, q, k, v, w_full, gains = qkv_call(
            count,
            idx,
            (x0, x1, x2, x3),
            (
                (a0, a1, a2, a4, a35, a6, a7),
                tuple((array, lead, 0) for array, lead in
                    ((0, None), (1, None), (2, None), (4, 0), (3, None), (4, 1), (5, None), (6, None))),
            ),
            None,
            cosine,
            sine,
        )
        q, f1, f4, c1 = together(q, f1, f4, c1)
        f2, f5 = ring(f1), by_y(f1)
        e14 = by_x(jnp.stack([narrow(f1), narrow(f4)]))
        ctx_fa, lse_fa = attend(q, k, v, 2)
        ctx_fa, q = together(ctx_fa, q)
        oth_a = by_x(ctx_fa)
        ctx_fb, lse_fb = attend(q, k, v, 3)
        ctx_fb, q, f2, f5, e14, oth_a = together(ctx_fb, q, f2, f5, e14, oth_a)
        oth_b = by_x(ctx_fb)
        f3, f6 = ring(f2), by_y(f2)
        e25 = by_x(jnp.stack([narrow(f2), narrow(f5)]))
        ctx_na, lse_na = attend(q, k, v, 0)
        ctx_na, q = together(ctx_na, q)
        ctx_nb, lse_nb = attend(q, k, v, 1)
        ctx_nb, f3, f6, e25, oth_b = together(ctx_nb, f3, f6, e25, oth_b)
        f7 = by_y(f3)
        e36 = by_x(jnp.stack([narrow(f3), narrow(f6)]))
        ctx_nb, f7 = together(ctx_nb, f7)
        e7 = by_x(narrow(f7))
        arrays = (f0, f1, f2, f3, f4, f5, f6, f7, w_other, e14, e25, e36, e7)
        mine_at = tuple((array, None, 0) for array in range(8))
        out_pieces = (arrays[:8], tuple((array, None, PADDED) for array in range(8)))
        down_at = tuple((array, None, PADDED + WIDTH) for array in range(8))
        other_at = tuple(
            (array, lead, 0)
            for array, lead in ((8, None), (9, 0), (10, 0), (11, 0), (9, 1), (10, 1), (11, 1), (12, None))
        )
    else:
        x1, x3 = by_core(x0), by_core(x2)
        gather = lambda value: lax.all_gather(value, "shard", axis=0, tiled=True)
        alone = ((0, None, 0),)
        first_low, q, k, v, w_full, gains = qkv_call(
            count,
            idx,
            (x0, x1, x2, x3),
            ((gather(w_qkv),), alone),
            jnp.stack([gather(attn_gain), gather(mlp_gain)]),
            cosine,
            sine,
        )
        arrays = (gather(w_mine), gather(w_down))
        arrays += (by_x(arrays[0]),)
        out_pieces = ((gather(out_weight),), alone)
        mine_at, down_at, other_at = alone, ((1, None, 0),), ((2, None, 0),)
        (ctx_fa, lse_fa), (ctx_fb, lse_fb) = attend(q, k, v, 2), attend(q, k, v, 3)
        oth_a, oth_b = by_x(ctx_fa), by_x(ctx_fb)
        c1 = by_core(c0)
        (ctx_na, lse_na), (ctx_nb, lse_nb) = attend(q, k, v, 0), attend(q, k, v, 1)

    near, far, other = (ctx_na, ctx_nb), (ctx_fa, ctx_fb), (oth_a, oth_b)
    lse_near, lse_far = (lse_na, lse_nb), (lse_fa, lse_fb)
    out_own, w_sel = out_call(count, idx, near, other, out_pieces)
    if eight:
        out_own, *last = together(out_own, *arrays)
        arrays = tuple(last)
    out_core = by_core(out_own)
    hidden, second_own, w_down_full, *wide = mlp_call(
        count, idx, x0, x1, out_own, out_core, c0, c1, gains, arrays, mine_at, other_at, down_at
    )
    second_core = by_core(second_own)
    down_other, down_mine, *down = down_call(count, idx, hidden, w_down_full, c0, c1)
    down_mine, second_core = together(down_mine, second_core)
    res, res_low, grad_near, grad_other, gain_two = norm_two_call(
        x0, x1, out_own, out_core, second_own, second_core, c0, c1, gains, w_sel
    )
    grad_far = by_x(grad_other)
    out_keep, out_send = out_grad_call(count, idx, near, other, res_low)
    part = lambda half, pair, grads, earlier=None: attend_back(
        half, pair, q, grads, (near, far)[half], (lse_near, lse_far)[half], k, v, cosine, sine, earlier
    )
    if eight:
        a_keep, a_send, b_keep, b_send = wide
        a_got, b_got = by_y(a_send), by_x(b_send)
        down_got = by_y(down[1])
        out_send, grad_near = together(out_send, grad_near)
        out_got = by_x(out_send)
        down_core = by_core(down_other)
    else:
        down_core = by_core(down_other)
    q_n0, dk0, dv0 = part(0, 0, grad_near)
    if eight:
        q_n0, grad_near, grad_far, down_core, a_got, b_got = together(
            q_n0, grad_near, grad_far, down_core, a_got, b_got
        )
        a_keep, a_got = plus(a_keep[0], a_got[0]), by_x(plus(a_keep[1], a_got[1]))
        b_keep, b_got = plus(b_keep[:4], b_got[:4]), by_y(plus(b_keep[4:], b_got[4:]))
    q_n1, dk1, dv1 = part(0, 1, grad_near)
    q_n1, grad_far = together(q_n1, grad_far)
    q_f0, k0, v0 = part(1, 0, grad_far, (dk0, dv0))
    if eight:
        q_f0, out_got, down_got, a_got, b_got, grad_far = together(
            q_f0, out_got, down_got, a_got, b_got, grad_far
        )
        both = lambda lo, hi: jnp.concatenate(
            [plus(a_keep[lo:hi], a_got[lo:hi]), plus(b_keep[lo:hi], b_got[lo:hi])], axis=-1
        )
        wide_next, wide_keep = by_z(both(2, 4)), both(0, 2)
        down_keep, down_got = plus(down[0][0], down_got[0]), by_x(plus(down[0][1], down_got[1]))
    raw0 = (q_n0, q_f0, k0, v0)
    *terms0, gain_a = qkv_grad_call(count, idx, first_low, raw0, w_full, gains, 0)
    if eight:
        terms0[0], terms0[1], grad_far = together(terms0[0], terms0[1], grad_far)
        out_next = by_y(jnp.concatenate([plus(out_keep[4:], out_got[4:]), terms0[1]], axis=1))
        out_keep = plus(out_keep[:4], out_got[:4])
    q_f1, k1, v1 = part(1, 1, grad_far, (dk1, dv1))
    if eight:
        q_f1, wide_next, out_next = together(q_f1, wide_next, out_next)
        wide_last, wide_keep = by_zz(plus(wide_keep[1], wide_next[1])), plus(wide_keep[0], wide_next[0])
    raw1 = (q_n1, q_f1, k1, v1)
    first_core = back_project((raw0, raw1), w_full, 1)
    first_got = by_core(first_core)
    if eight:
        first_core, q_f1 = together(first_core, q_f1)
    raw1 = (q_n1, q_f1, k1, v1)
    *terms1, gain_b = qkv_grad_call(count, idx, first_low, raw1, w_full, gains, 1)
    if eight:
        terms1[0], terms1[1], first_got, q_f1 = together(terms1[0], terms1[1], first_got, q_f1)
        terms1_got = by_y(terms1[1])
    raw1 = (q_n1, q_f1, k1, v1)
    first_own = back_project((raw0, raw1), w_full, 0)
    if eight:
        first_own, first_got = together(first_own, first_got)
    far_sum = plus(first_own[1], first_got[1])
    first_far = by_x(far_sum)
    gain_terms = jnp.concatenate([gain_a[:1] + gain_b[:1], gain_two[:1]], axis=0)
    final = lambda mine, got: mine.astype(f32) + got.astype(f32)
    crossed = (seq == 1) | (seq == 2)
    cross = [(1, 2), (2, 1)]
    if eight:
        first_own, far_sum, down_got, gain_terms = together(first_own, far_sum, down_got, gain_terms)
        rest = lambda lo, hi: jnp.concatenate(
            [
                plus(down_keep[lo:hi], down_got[lo:hi]),
                plus(out_keep[lo:hi], out_next[lo:hi, :COLS]),
                plus(terms0[0][lo:hi], out_next[lo:hi, COLS:]),
            ],
            axis=1,
        )
        rest_next, rest_keep = by_z(rest(2, 4)), rest(0, 2)
        gain_got = by_core(gain_terms)
        terms1_got, gain_got, down_core = together(terms1_got, gain_got, down_core)
        terms1_next = by_z(plus(terms1[0][2:], terms1_got[2:]))
        terms1_keep = plus(terms1[0][:2], terms1_got[:2])
        gain_terms = gain_terms + gain_got
        gain_got = by_y(gain_terms)
        result = (
            x0.astype(f32)
            + out_own[:rows].astype(f32)
            + out_core[rows:].astype(f32)
            + down_mine.astype(f32)
            + down_core.astype(f32)
        ).astype(bf16)[None]
        rest_next, wide_last, gain_got, result = together(rest_next, wide_last, gain_got, result)
        rest_last, rest_keep = plus(rest_keep[1], rest_next[1]), plus(rest_keep[0], rest_next[0])
        down_last, down_keep = rest_last[:BLOCK], rest_keep[:BLOCK]
        down_last = lax.ppermute(
            down_last,
            ("seq", "shard"),
            [(8 * j + i, 8 * (0, 2, 1, 3)[j] + (i ^ 4)) for j in range(4) for i in range(8)],
        )
        down_moved = lax.ppermute(down_keep, "seq", cross)
        rest_last, rest_keep = by_zz(rest_last[BLOCK:]), rest_keep[BLOCK:]
        gain_terms = gain_terms + gain_got
        gain_got = by_z(gain_terms)
        terms1_next, gain_got, first_far = together(terms1_next, gain_got, first_far)
        terms1_last = by_zz(plus(terms1_keep[1], terms1_next[1]))
        terms1_keep = plus(terms1_keep[0], terms1_next[0])
        gain_terms = gain_terms + gain_got
        gain_terms = gain_terms + by_zz(gain_terms)
        gain_terms = gain_terms + by_x(gain_terms)
        wide_total = final(wide_keep, wide_last)
        rest_total = final(rest_keep, rest_last)
        down_total = final(jnp.where(crossed, down_moved, down_keep), down_last)
        out_total = rest_total[:COLS]
        totals = [rest_total[COLS:], final(terms1_keep, terms1_last)]
    else:
        wide_sum = plus(wide[0][0, 0], by_x(wide[0][1, 0]))
        scatter = lambda value, dim: lax.psum_scatter(
            value, "shard", scatter_dimension=dim, tiled=True
        ).astype(f32)
        wide_total = scatter(wide_sum, 0)
        down_total = scatter(plus(down[0][0, 0], by_x(down[0][1, 0])), 1)
        moved = lax.ppermute(down_total.astype(bf16), "seq", cross).astype(f32)
        down_total = jnp.where(crossed, moved, down_total)
        out_total = scatter(plus(out_keep, by_x(out_send))[0], 1)
        totals = [scatter(terms[0].reshape(3, width, 128), 1) for terms in (terms0, terms1)]
        gain_terms = lax.psum(gain_terms, ("seq", "shard"))
        result = (
            x0.astype(f32)
            + out_own[:rows].astype(f32)
            + out_core[rows:].astype(f32)
            + down_mine.astype(f32)
            + down_core.astype(f32)
        ).astype(bf16)[None]
    input_grad = norm_one_call(x0, res, first_own, first_got, first_far, gains)[None]
    take = width // (4 * shards)
    gain_out = lax.dynamic_slice_in_dim(gain_terms, (seq * shards + shard) * take, take, 1)
    qkv_out = jnp.concatenate([total.reshape(3, piece, 128) for total in totals], axis=2)
    return (
        result,
        input_grad,
        gain_out[0],
        qkv_out,
        out_total,
        gain_out[1],
        wide_total[:, :HALF],
        down_total,
    )


def solution(mesh):
    placed = (
        P("shard", "seq", None),
        P("shard"),
        P(None, "shard", None),
        P("shard", None),
        P("shard"),
        P("shard", None),
        P(None, "shard"),
        P("shard", "seq", None),
    )
    return jax.shard_map(
        per_device,
        mesh=mesh,
        in_specs=placed,
        out_specs=(
            P("shard", "seq", None),
            P("shard", "seq", None),
            P(("seq", "shard")),
            P(None, "shard", "seq"),
            P("seq", "shard"),
            P(("seq", "shard")),
            P("shard", "seq"),
            P("seq", "shard"),
        ),
        check_vma=False,
    )
```

```python
from functools import partial
import math

import jax
import jax.numpy as jnp
from jax import lax
from jax.experimental import pallas as pl
from jax.experimental.pallas import tpu as pltpu
from jax.sharding import PartitionSpec as P

HEADS = 16
HD = 64
FF = 2624

epsilon = 1e-05
rope_base = 160000.0

f32 = jnp.float32
bf16 = jnp.bfloat16

WIDTH = 1024
HALF = FF // 2
PADDED = 1408
BLOCK = FF // 4
COLS = 256
CHUNKS = (0, 4, 2, 6, 1, 5, 3, 7)
SPLIT = 768
EXTRA = 16
ROWS_BY_COLS = (((0,), (0,)), ((), ()))
COLS_BY_COLS = (((1,), (1,)), ((), ()))
VMEM_LIMIT = 58 * 1024 * 1024

ANY = pl.BlockSpec(memory_space=pl.ANY)
SMEM = pl.BlockSpec(memory_space=pltpu.SMEM)


def cost(micros):
    return pl.CostEstimate(flops=int(micros), transcendentals=0, bytes_accessed=int(micros))


def params():
    return pltpu.CompilerParams(vmem_limit_bytes=VMEM_LIMIT)


def sds(shape, dtype=bf16):
    return jax.ShapeDtypeStruct(shape, dtype)


def aligned(index, size):
    return pl.ds(pl.multiple_of(index * size, size), size)


def normalize(values):
    center = values - jnp.mean(values, axis=-1, keepdims=True)
    inv_scale = lax.rsqrt(jnp.mean(center * center, axis=-1, keepdims=True) + epsilon)
    return center * inv_scale, inv_scale


def norm_back(grads, xhat, inv_scale):
    mean_grad = jnp.mean(grads, axis=-1, keepdims=True)
    mean_both = jnp.mean(grads * xhat, axis=-1, keepdims=True)
    return inv_scale * (grads - mean_grad - xhat * mean_both)


def turned(values):
    lane = lax.broadcasted_iota(jnp.int32, values.shape, 1)
    width = values.shape[1]
    return jnp.where(
        lane % HD < HD // 2, pltpu.roll(values, width - HD // 2, 1), pltpu.roll(values, HD // 2, 1)
    )


def twice(table):
    return jnp.concatenate([table, table], axis=1)


def piece_of(refs, place, rows=None, width=None):
    array, lead, column = place
    index = () if lead is None else (lead,)
    rows = slice(None) if rows is None else rows
    cols = slice(None) if width is None else pl.ds(column, width)
    return refs[array].at[(*index, rows, cols)]


def fetch_rows(count, idx, refs, places, width, target, sem):
    size = target.shape[0] // count
    copies = []
    for r in range(count):
        rows = aligned(idx[4 + r], size) if count > 1 else pl.ds(0, size)
        copies.append(
            pltpu.make_async_copy(piece_of(refs, places[r], width=width), target.at[rows], sem.at[r])
        )
    return copies


def qkv_kernel(count, places, idx, *refs):
    x_refs, refs = refs[:4], refs[4:]
    n_arrays = 1 + max(array for array, _, _ in places)
    w_refs, refs = refs[:n_arrays], refs[n_arrays:]
    if count == 1:
        gain_ref, refs = refs[0], refs[1:]
    cos_ref, sin_ref, fn_o, q_o, k_o, v_o, w_o, g_o, xs, gs, semx, semw, semg = refs
    step = pl.program_id(0)
    shard = idx[0]
    size = WIDTH // count

    def x_copy(r):
        return pltpu.make_async_copy(x_refs[r], xs.at[r], semx.at[r])

    def w_copy(r):
        return pltpu.make_async_copy(
            piece_of(w_refs, places[r], rows=pl.ds(0, size)), w_o.at[aligned(jnp.bitwise_xor(shard, r), size)], semw.at[r]
        )

    def g_copy(r):
        return pltpu.make_async_copy(
            piece_of(w_refs, places[r], rows=pl.ds(size, EXTRA)), gs.at[jnp.bitwise_xor(shard, r)], semg.at[r]
        )

    @pl.when(step == 0)
    def _():
        if count == 1:
            w_all = pltpu.make_async_copy(w_refs[0], w_o, semw.at[0])
            w_all.start()
        else:
            for r in range(count):
                w_copy(r).start()
                g_copy(r).start()
        for r in range(4):
            x_copy(r).start()
        if count == 1:
            w_all.wait()
            g_o[0:1] = gain_ref[0:1].astype(f32)
            g_o[1:2] = gain_ref[1:2].astype(f32)
        else:
            for r in range(count):
                w_copy(r).wait()
                g_copy(r).wait()
            for r in range(count):
                part = gs[r].astype(f32)
                g_o[0:1, r * size : (r + 1) * size] = part[0:1, 0:size]
                g_o[1:2, r * size : (r + 1) * size] = part[0:1, size : 2 * size]

    for r in range(4):

        @pl.when(step == r)
        def _():
            x_copy(r).wait()

    xhat, _ = normalize(xs[step].astype(f32))
    first_low = (xhat * g_o[0:1]).astype(bf16)
    fn_o[...] = first_low
    cosine, sine = twice(cos_ref[...]), twice(sin_ref[...])
    outs = (q_o, k_o, v_o)
    for part in range(3):
        value = jnp.dot(first_low, w_o[:, part * COLS : (part + 1) * COLS], preferred_element_type=f32)
        if part < 2:
            value = value * cosine + turned(value) * sine
        value = value.astype(bf16)
        if part == 0:
            value = value * jnp.asarray(1.0 / math.sqrt(HD), bf16)
        outs[part][...] = value


def qkv_call(count, idx, chunks, pieces, gains, cosine, sine):
    arrays, where = pieces
    rows = chunks[0].shape[0]
    by_step = lambda width: pl.BlockSpec((rows, width), lambda r: (r, 0))
    whole = lambda shape: pl.BlockSpec(shape, lambda r: (0, 0))
    extra = [] if count > 1 else [gains]
    return pl.pallas_call(
        partial(qkv_kernel, count, where),
        grid=(4,),
        in_specs=[SMEM]
        + [ANY] * (4 + len(arrays))
        + ([] if count > 1 else [whole((2, WIDTH))])
        + [by_step(128), by_step(128)],
        out_specs=[
            by_step(WIDTH),
            by_step(COLS),
            by_step(COLS),
            by_step(COLS),
            whole((WIDTH, 3 * COLS)),
            whole((8, WIDTH)),
        ],
        out_shape=[
            sds((4 * rows, WIDTH)),
            sds((4 * rows, COLS)),
            sds((4 * rows, COLS)),
            sds((4 * rows, COLS)),
            sds((WIDTH, 3 * COLS)),
            sds((8, WIDTH), f32),
        ],
        scratch_shapes=[
            pltpu.VMEM((4, rows, WIDTH), bf16),
            pltpu.VMEM((8, EXTRA, 3 * COLS), bf16),
            pltpu.SemaphoreType.DMA((4,)),
            pltpu.SemaphoreType.DMA((count,)),
            pltpu.SemaphoreType.DMA((count,)),
        ],
        compiler_params=params(),
        cost_estimate=cost(11),
        name="project",
    )(idx, *chunks, *arrays, *extra, cosine, sine)


def head_of(shape):
    return lax.broadcasted_iota(jnp.int32, shape, len(shape) - 1) // HD


def attend_kernel(q_ref, k_ref, v_ref, o_ref, lse_ref):
    q, k, v = q_ref[...], k_ref[...], v_ref[...]
    heads = head_of(q.shape)
    total = jnp.zeros(q.shape, f32)
    lses = jnp.zeros((q.shape[0], 128), f32)
    lane = lax.broadcasted_iota(jnp.int32, lses.shape, 1)
    for h in range(COLS // HD):
        q_h = jnp.where(heads == h, q, jnp.zeros_like(q))
        scores = lax.dot_general(q_h, k, COLS_BY_COLS, preferred_element_type=f32)
        row_max = jnp.max(scores, axis=1, keepdims=True)
        exponent = jnp.exp(scores - row_max)
        row_total = jnp.sum(exponent, axis=1, keepdims=True)
        context = jnp.dot(exponent.astype(bf16), v, preferred_element_type=f32)
        total = jnp.where(heads == h, context * (1.0 / row_total), total)
        lses = jnp.where(lane == h, row_max + jnp.log(row_total), lses)
    o_ref[...] = total.astype(bf16)
    lse_ref[...] = lses.T[:8]


def attend(q, k, v, chunk, after=()):
    span = k.shape[0]
    rows = span // 4
    kept = pl.BlockSpec((span, COLS), lambda i: (0, 0))
    return pl.pallas_call(
        lambda *refs: attend_kernel(*refs[:3], *refs[3 + len(after) :]),
        grid=(1,),
        in_specs=[pl.BlockSpec((rows, COLS), lambda i: (chunk, 0)), kept, kept] + [ANY] * len(after),
        out_specs=[
            pl.BlockSpec((rows, COLS), lambda i: (0, 0)),
            pl.BlockSpec((8, rows), lambda i: (0, 0)),
        ],
        out_shape=[sds((rows, COLS)), sds((8, rows), f32)],
        compiler_params=params(),
        cost_estimate=cost(8),
        name="attend",
    )(q, k, v, *after)


def attend_back_kernel(last, pair, *refs):
    q_ref, do_ref, oa_ref, ob_ref, la_ref, lb_ref, k_ref, v_ref, qcos, qsin, refs = *refs[:10], refs[10:]
    if last:
        dk_i, dv_i, kcos, ksin, refs = *refs[:4], refs[4:]
    dq_ref, dk_ref, dv_ref, do_s, inner_s, lse_s, dq_s = refs
    step = pl.program_id(0)
    width = q_ref.shape[1]
    n_heads = width // HD

    @pl.when(step == 0)
    def _():
        do = do_ref[...]
        context = jnp.concatenate([oa_ref[...], ob_ref[...]], axis=0)
        product = do.astype(f32) * context.astype(f32)
        high = product.astype(bf16)
        rest = (product - high.astype(f32)).astype(bf16)
        chosen = (
            head_of((8, width)) == lax.broadcasted_iota(jnp.int32, (8, width), 0)
        ).astype(bf16)
        inner_s[...] = lax.dot_general(
            chosen, high, COLS_BY_COLS, preferred_element_type=f32
        ) + lax.dot_general(chosen, rest, COLS_BY_COLS, preferred_element_type=f32)
        lse_s[...] = jnp.concatenate([la_ref[...], lb_ref[...]], axis=1)
        heads = head_of(do.shape)
        for h in range(n_heads):
            do_s[h] = jnp.where(heads == h, do, jnp.zeros_like(do))
        dq_s[...] = jnp.zeros_like(dq_s)

    q, k, v = q_ref[...], k_ref[...], v_ref[...]
    heads = head_of(k.shape)
    dk = jnp.zeros(k.shape, f32)
    dv = jnp.zeros(k.shape, f32)
    dq = dq_s[...]
    for h in range(n_heads):
        at = n_heads * pair + h
        k_h = jnp.where(heads == h, k, jnp.zeros_like(k))
        scores = lax.dot_general(k_h, q, COLS_BY_COLS, preferred_element_type=f32)
        probs = jnp.exp(scores - lse_s[at : at + 1, :])
        probs_grad = lax.dot_general(v, do_s[h], COLS_BY_COLS, preferred_element_type=f32)
        scores_grad = (probs * (probs_grad - inner_s[h : h + 1, :])).astype(bf16)
        dv = dv + jnp.dot(probs.astype(bf16), do_s[h], preferred_element_type=f32)
        dk = jnp.where(heads == h, jnp.dot(scores_grad, q, preferred_element_type=f32), dk)
        dq = dq + lax.dot_general(scores_grad, k_h, ROWS_BY_COLS, preferred_element_type=f32)
    dq_s[...] = dq
    if last:
        dk = dk + dk_i[...]
        dv = dv + dv_i[...]
        dk_ref[...] = (dk * kcos[...] - turned(dk) * ksin[...]).astype(bf16)
        dv_ref[...] = dv.astype(bf16)
    else:
        dk_ref[...] = dk
        dv_ref[...] = dv

    @pl.when(step == pl.num_programs(0) - 1)
    def _():
        dq = dq_s[...] * (1.0 / math.sqrt(HD))
        dq_ref[...] = (dq * qcos[...] - turned(dq) * qsin[...]).astype(bf16)


def attend_back(part, pair, q, do, contexts, lses, k, v, cosine, sine, earlier=None, after=(), tile=512):
    span = k.shape[0]
    rows = do.shape[0]
    last = earlier is not None
    rows_at = lambda at, col, count=rows, width=128: pl.BlockSpec((count, width), lambda i: (at, col))
    keys = lambda col: pl.BlockSpec((tile, 128), lambda i: (i, col))
    grads = bf16 if last else f32
    n_in = 10 + (4 if last else 0)
    return pl.pallas_call(
        lambda *refs: attend_back_kernel(last, pair, *refs[:n_in], *refs[n_in + len(after) :]),
        grid=(span // tile,),
        in_specs=[
            rows_at(part, pair),
            rows_at(0, pair),
            rows_at(0, pair, rows // 2),
            rows_at(0, pair, rows // 2),
            rows_at(0, 0, 8, rows // 2),
            rows_at(0, 0, 8, rows // 2),
            keys(pair),
            keys(pair),
            rows_at(part, 0),
            rows_at(part, 0),
        ]
        + ([keys(0), keys(0), keys(0), keys(0)] if last else [])
        + [ANY] * len(after),
        out_specs=[rows_at(0, 0), keys(0), keys(0)],
        out_shape=[sds((rows, 128)), sds((span, 128), grads), sds((span, 128), grads)],
        scratch_shapes=[
            pltpu.VMEM((128 // HD, rows, 128), bf16),
            pltpu.VMEM((8, rows), f32),
            pltpu.VMEM((8, rows), f32),
            pltpu.VMEM((rows, 128), f32),
        ],
        compiler_params=params(),
        cost_estimate=cost(15),
        name="attend_back",
    )(q, do, *contexts, *lses, k, v, cosine, sine, *((*earlier, cosine, sine) if last else ()), *after)


def out_kernel(count, places, idx, ma_ref, mb_ref, oa_ref, ob_ref, *refs):
    w_refs, (o_ref, wsel_ref, w_s, sem) = refs[:-4], refs[-4:]
    copies = fetch_rows(count, idx, w_refs, places, WIDTH, w_s, sem)
    for copy in copies:
        copy.start()
    for copy in copies:
        copy.wait()
    seq = idx[1]
    wsel_ref[0:COLS] = w_s[aligned(seq, COLS)]
    wsel_ref[COLS:] = w_s[aligned(jnp.bitwise_xor(seq, 2), COLS)]
    rows = ma_ref.shape[0]
    for r, (mine, other) in enumerate(((ma_ref, oa_ref), (mb_ref, ob_ref))):
        both = jnp.concatenate([mine[...], other[...]], axis=1)
        value = jnp.dot(both, wsel_ref[...], preferred_element_type=f32)
        o_ref[r * rows : (r + 1) * rows] = value.astype(bf16)


def out_call(count, idx, mine, other, pieces):
    vmem = pl.BlockSpec(memory_space=pltpu.VMEM)
    arrays, where = pieces
    return pl.pallas_call(
        partial(out_kernel, count, where),
        in_specs=[SMEM] + [vmem] * 4 + [ANY] * len(arrays),
        out_specs=[vmem, vmem],
        out_shape=[sds((2 * mine[0].shape[0], WIDTH)), sds((2 * COLS, WIDTH))],
        scratch_shapes=[pltpu.VMEM((WIDTH, WIDTH), bf16), pltpu.SemaphoreType.DMA((count,))],
        compiler_params=params(),
        cost_estimate=cost(5),
        name="out_project",
    )(idx, *mine, *other, *arrays)


def mlp_kernel(count, n_arrays, mine, other, down, idx, *refs):
    x0, x1, po, pr, c0, c1, g_ref, refs = *refs[:7], refs[7:]
    w_refs, refs = refs[:n_arrays], refs[n_arrays:]
    hid_o, sgp_o, wd_o, refs = *refs[:3], refs[3:]
    grads, refs = (refs[:4], refs[4:]) if count > 1 else (refs[:1], refs[1:])
    xs, pos, prs, cs, wi, wd, sn_s, hid_s, gug_s, sgp_s, turned_s, acc, refs = *refs[:12], refs[12:]
    sem_a, sem_m, sem_i, sem_d, sem_o = refs
    shard, x_place = idx[0], idx[2]
    rows = xs.shape[1]
    loads = [
        pltpu.make_async_copy(x0, xs.at[0], sem_a.at[0]),
        pltpu.make_async_copy(x1, xs.at[1], sem_a.at[1]),
        pltpu.make_async_copy(po, pos, sem_a.at[2]),
        pltpu.make_async_copy(pr, prs, sem_a.at[3]),
        pltpu.make_async_copy(c0, cs.at[pl.ds(0, rows)], sem_a.at[4]),
        pltpu.make_async_copy(c1, cs.at[pl.ds(rows, rows)], sem_a.at[5]),
    ]
    here = wi.at[:, aligned(x_place, PADDED)]
    there = wi.at[:, aligned(1 - x_place, PADDED)]
    wi_loads = fetch_rows(count, idx, w_refs, mine, PADDED, here, sem_m)
    wi_loads += fetch_rows(count, idx, w_refs, other, PADDED, there, sem_i)
    wd_loads = fetch_rows(count, idx, w_refs, down, PADDED, wd, sem_d)
    for copy in loads[:4] + wi_loads + loads[4:] + wd_loads:
        copy.start()
    for copy in loads[:4]:
        copy.wait()
    for r in range(2):
        here, there = pl.ds(r * rows, rows), pl.ds((1 - r) * rows, rows)
        after = xs[r].astype(f32) + pos[here].astype(f32) + prs[there].astype(f32)
        xhat, _ = normalize(after)
        sn_s[here] = (xhat * g_ref[1:2]).astype(bf16)
    stores = []

    def store(source, target):
        copy = pltpu.make_async_copy(source, target, sem_o.at[len(stores)])
        copy.start()
        stores.append(copy)

    turned_s[...] = sn_s[...].T
    for copy in wi_loads + loads[4:] + wd_loads:
        copy.wait()
    store(wd, wd_o)
    start = 0
    while start < PADDED:
        size = min(256, PADDED - start)
        here = pl.ds(start, size)
        gate = jnp.dot(sn_s[...], wi[:, here], preferred_element_type=f32)
        up = jnp.dot(sn_s[...], wi[:, pl.ds(PADDED + start, size)], preferred_element_type=f32)
        back = jnp.dot(cs[...], wd[:, here], preferred_element_type=f32)
        below = 0.5 * (1.0 + lax.erf(gate * math.sqrt(0.5)))
        density = jnp.exp(-0.5 * gate * gate) * (1.0 / math.sqrt(2.0 * math.pi))
        unit = gate * below
        hid_s[:, here] = (unit * up).astype(bf16)
        gug_s[0, :, here] = (back * up * (below + gate * density)).astype(bf16)
        gug_s[1, :, here] = (back * unit).astype(bf16)
        start += size
    store(hid_s, hid_o)
    value = lax.dot_general(gug_s[0], wi[:, :PADDED], COLS_BY_COLS, preferred_element_type=f32)
    value = value + lax.dot_general(gug_s[1], wi[:, PADDED:], COLS_BY_COLS, preferred_element_type=f32)
    sgp_s[...] = value.astype(bf16)
    store(sgp_s, sgp_o)
    size = WIDTH // count
    for part in range(2):
        terms = gug_s[jnp.bitwise_xor(x_place, part)]
        acc[part] = jnp.dot(turned_s[...], terms, preferred_element_type=f32).astype(bf16)
        if count == 1:
            store(acc.at[part], grads[0].at[part, 0])
            continue
        keep_a, send_a, keep_b, send_b = grads
        for k, r in enumerate(CHUNKS):
            place = aligned(jnp.bitwise_xor(shard, r), size)
            store(acc.at[part, place, pl.ds(0, SPLIT)], (keep_a, send_a)[k // 4].at[part, k % 4])
            store(acc.at[part, place, pl.ds(SPLIT, PADDED - SPLIT)], (keep_b, send_b)[part].at[k])
    for copy in stores:
        copy.wait()


def mlp_call(count, idx, x0, x1, po, pr, c0, c1, gains, arrays, mine, other, down):
    rows = x0.shape[0]
    size = WIDTH // count
    grads = [sds((2, 4, size, SPLIT))] * 2 + [sds((8, size, PADDED - SPLIT))] * 2
    if count == 1:
        grads = [sds((2, 1, WIDTH, PADDED))]
    return pl.pallas_call(
        partial(mlp_kernel, count, len(arrays), mine, other, down),
        in_specs=[SMEM] + [ANY] * 6 + [pl.BlockSpec(memory_space=pltpu.VMEM)] + [ANY] * len(arrays),
        out_specs=[ANY] * (3 + len(grads)),
        out_shape=[sds((2 * rows, PADDED)), sds((2 * rows, WIDTH)), sds((WIDTH, PADDED))] + grads,
        scratch_shapes=[
            pltpu.VMEM((2, rows, WIDTH), bf16),
            pltpu.VMEM((2 * rows, WIDTH), bf16),
            pltpu.VMEM((2 * rows, WIDTH), bf16),
            pltpu.VMEM((2 * rows, WIDTH), bf16),
            pltpu.VMEM((WIDTH, 2 * PADDED), bf16),
            pltpu.VMEM((WIDTH, PADDED), bf16),
            pltpu.VMEM((2 * rows, WIDTH), bf16),
            pltpu.VMEM((2 * rows, PADDED), bf16),
            pltpu.VMEM((2, 2 * rows, PADDED), bf16),
            pltpu.VMEM((2 * rows, WIDTH), bf16),
            pltpu.VMEM((WIDTH, 2 * rows), bf16),
            pltpu.VMEM((2, WIDTH, PADDED), bf16),
            pltpu.SemaphoreType.DMA((6,)),
            pltpu.SemaphoreType.DMA((count,)),
            pltpu.SemaphoreType.DMA((count,)),
            pltpu.SemaphoreType.DMA((count,)),
            pltpu.SemaphoreType.DMA((40,)),
        ],
        compiler_params=params(),
        cost_estimate=cost(25),
        name="feed_forward",
    )(idx, x0, x1, po, pr, c0, c1, gains, *arrays)


def down_kernel(count, idx, *refs):
    sources, refs = refs[:4], refs[4:]
    res_other, res_mine, refs = *refs[:2], refs[2:]
    downs, refs = refs[: 2 if count > 1 else 1], refs[2 if count > 1 else 1 :]
    hid, wd, cs, acc, res, sem_i, sem_o = refs
    shard, x_place = idx[0], idx[2]
    rows = cs.shape[0] // 2
    width = WIDTH // count
    targets = [hid, wd, cs.at[pl.ds(0, rows)], cs.at[pl.ds(rows, rows)]]
    loads = [pltpu.make_async_copy(*pair, sem_i.at[k]) for k, pair in enumerate(zip(sources, targets))]
    for k in (0, 2, 3, 1):
        loads[k].start()
    places = [
        aligned(jnp.bitwise_xor(shard, r), width) if count > 1 else pl.ds(0, width) for r in CHUNKS[:count]
    ]
    stores = []

    def store(source, target):
        copy = pltpu.make_async_copy(source, target, sem_o.at[len(stores)])
        copy.start()
        stores.append(copy)

    for k in (0, 2, 3):
        loads[k].wait()
    acc[...] = lax.dot_general(hid[...], cs[...], ROWS_BY_COLS, preferred_element_type=f32).astype(bf16)
    for part in range(2):
        here = pl.ds(pl.multiple_of(jnp.bitwise_xor(x_place, part) * BLOCK, 16), BLOCK)
        for r in range(count):
            store(acc.at[here, places[r]], downs[r // 4].at[part, r % 4])
    loads[1].wait()
    for r, target in ((1, res_other), (0, res_mine)):
        res[r] = lax.dot_general(
            hid[r * rows : (r + 1) * rows], wd[...], COLS_BY_COLS, preferred_element_type=f32
        ).astype(bf16)
        store(res.at[r], target)
    for copy in stores:
        copy.wait()


def down_call(count, idx, hidden, wd, c0, c1):
    rows = c0.shape[0]
    split = 2 if count > 1 else 1
    return pl.pallas_call(
        partial(down_kernel, count),
        in_specs=[SMEM] + [ANY] * 4,
        out_specs=[ANY] * (2 + split),
        out_shape=[sds((rows, WIDTH))] * 2
        + [sds((2, count // split, BLOCK, WIDTH // count))] * split,
        scratch_shapes=[
            pltpu.VMEM((2 * rows, PADDED), bf16),
            pltpu.VMEM((WIDTH, PADDED), bf16),
            pltpu.VMEM((2 * rows, WIDTH), bf16),
            pltpu.VMEM((PADDED, WIDTH), bf16),
            pltpu.VMEM((2, rows, WIDTH), bf16),
            pltpu.SemaphoreType.DMA((4,)),
            pltpu.SemaphoreType.DMA((2 * count + 2,)),
        ],
        compiler_params=params(),
        cost_estimate=cost(15),
        name="down_project",
    )(idx, hidden, wd, c0, c1)


def norm_two_kernel(x0, x1, po, pr, so, sr, c0, c1, g_ref, wsel, res_o, low_o, mine_o, other_o, gain_o):
    step = pl.program_id(0)
    half = pl.num_programs(0) // 2
    first = step < half
    gain = g_ref[1:2]
    x = jnp.where(first, x0[...], x1[...])
    c = jnp.where(first, c0[...], c1[...])
    after = x.astype(f32) + po[...].astype(f32) + pr[...].astype(f32)
    xhat, inv_scale = normalize(after)
    second = so[...].astype(f32) + sr[...].astype(f32)
    res = c.astype(f32) + norm_back(second * gain, xhat, inv_scale)

    @pl.when(step == 0)
    def _():
        gain_o[...] = jnp.zeros_like(gain_o)

    @pl.when(first)
    def _():
        res_o[...] = res
        gain_o[...] += jnp.sum(second * xhat, axis=0, keepdims=True)

    low = res.astype(bf16)
    low_o[...] = low
    value = lax.dot_general(low, wsel[...], COLS_BY_COLS, preferred_element_type=f32).astype(bf16)
    mine_o[...] = value[:, :COLS]
    other_o[...] = value[:, COLS:]


def norm_two_call(x0, x1, po, pr, so, sr, c0, c1, gains, wsel, half=2):
    rows = x0.shape[0]
    size = rows // half
    spec = lambda width, at: pl.BlockSpec((size, width), lambda s: (at(s), 0))
    lower = lambda s: jnp.minimum(s, half - 1)
    upper = lambda s: jnp.maximum(s - half, 0)
    same = lambda s: s
    other = lambda s: lax.rem(s + half, 2 * half)
    whole = lambda shape: pl.BlockSpec(shape, lambda s: (0, 0))
    return pl.pallas_call(
        norm_two_kernel,
        grid=(2 * half,),
        in_specs=[
            spec(WIDTH, lower),
            spec(WIDTH, upper),
            spec(WIDTH, same),
            spec(WIDTH, other),
            spec(WIDTH, same),
            spec(WIDTH, other),
            spec(WIDTH, lower),
            spec(WIDTH, upper),
            whole((8, WIDTH)),
            whole((2 * COLS, WIDTH)),
        ],
        out_specs=[
            spec(WIDTH, lower),
            spec(WIDTH, same),
            spec(COLS, same),
            spec(COLS, same),
            whole((8, WIDTH)),
        ],
        out_shape=[
            sds((rows, WIDTH), f32),
            sds((2 * rows, WIDTH)),
            sds((2 * rows, COLS)),
            sds((2 * rows, COLS)),
            sds((8, WIDTH), f32),
        ],
        compiler_params=params(),
        cost_estimate=cost(8),
        name="norm_two_back",
    )(x0, x1, po, pr, so, sr, c0, c1, gains, wsel)


def out_grad_kernel(count, idx, ma, mb, oa, ob, low, keep_o, send_o, acc):
    shard = idx[0]
    width = WIDTH // count
    for (first, second), target in (((oa, ob), send_o), ((ma, mb), keep_o)):
        context = jnp.concatenate([first[...], second[...]], axis=0)
        acc[...] = lax.dot_general(context, low[...], ROWS_BY_COLS, preferred_element_type=f32)
        for k, r in enumerate(CHUNKS[:count]):
            place = aligned(jnp.bitwise_xor(shard, r), width) if count > 1 else pl.ds(0, width)
            target[k] = acc[:, place].astype(bf16)


def out_grad_call(count, idx, mine, other, low):
    vmem = pl.BlockSpec(memory_space=pltpu.VMEM)
    return pl.pallas_call(
        partial(out_grad_kernel, count),
        in_specs=[SMEM] + [vmem] * 5,
        out_specs=[vmem] * 2,
        out_shape=[sds((count, COLS, WIDTH // count))] * 2,
        scratch_shapes=[pltpu.VMEM((COLS, WIDTH), f32)],
        compiler_params=params(),
        cost_estimate=cost(4),
        name="out_grad",
    )(idx, *mine, *other, low)


def back_project_kernel(q0, q1, f0, f1, k0n, k1n, k0f, k1f, v0n, v1n, v0f, v1f, w_ref, both_o):
    for half, parts in (
        (1, (f0, f1, k0f, k1f, v0f, v1f)),
        (0, (q0, q1, k0n, k1n, v0n, v1n)),
    ):
        raw = jnp.concatenate([part[...] for part in parts], axis=1)
        both_o[half] = lax.dot_general(
            raw, w_ref[...], COLS_BY_COLS, preferred_element_type=f32
        ).astype(bf16)


def back_project(raw_pairs, w, chunk):
    rows = raw_pairs[0][0].shape[0] // 2
    at = lambda where: pl.BlockSpec((rows, 128), lambda i: (where, 0))
    q0, f0, k0, v0 = raw_pairs[0]
    q1, f1, k1, v1 = raw_pairs[1]
    return pl.pallas_call(
        back_project_kernel,
        grid=(1,),
        in_specs=[at(chunk)] * 6
        + [at(chunk + 2)] * 2
        + [at(chunk)] * 2
        + [at(chunk + 2)] * 2
        + [pl.BlockSpec((WIDTH, 3 * COLS), lambda i: (0, 0))],
        out_specs=pl.BlockSpec((2, rows, WIDTH), lambda i: (0, 0, 0)),
        out_shape=sds((2, rows, WIDTH)),
        compiler_params=params(),
        cost_estimate=cost(5),
        name="back_project",
    )(q0, q1, f0, f1, k0, k1, k0, k1, v0, v1, v0, v1, w)


def qkv_grad_kernel(count, idx, fn_ref, qn, qf, k_ref, v_ref, wq, wk, wv, g_ref, keep_o, *refs):
    if count > 1:
        send_o, gain_o, acc = refs
    else:
        gain_o, acc = refs
    rows = qn.shape[0]
    q = jnp.concatenate([qn[...], qf[...]], axis=0)
    raw = jnp.concatenate([q, k_ref[...], v_ref[...]], axis=1)
    acc[...] = lax.dot_general(fn_ref[...], raw, ROWS_BY_COLS, preferred_element_type=f32)
    shard = idx[0]
    size = WIDTH // count
    for k, r in enumerate(CHUNKS[:count]):
        place = aligned(jnp.bitwise_xor(shard, r), size) if count > 1 else pl.ds(0, size)
        target = (keep_o, send_o)[k // 4] if count > 1 else keep_o
        for part in range(3):
            value = acc[place, part * 128 : (part + 1) * 128]
            target[k % 4, part * size : (part + 1) * size] = value.astype(bf16)
    w = jnp.concatenate([wq[...], wk[...], wv[...]], axis=1)
    both = acc[...] * w.astype(f32)
    high = both.astype(bf16)
    rest = (both - high.astype(f32)).astype(bf16)
    ones = jnp.ones((8, w.shape[1]), bf16)
    total = lax.dot_general(ones, high, COLS_BY_COLS, preferred_element_type=f32)
    total += lax.dot_general(ones, rest, COLS_BY_COLS, preferred_element_type=f32)
    gain_o[...] = total / g_ref[0:1]


def qkv_grad_call(count, idx, first_low, raw, w, gains, pair):
    vmem = pl.BlockSpec(memory_space=pltpu.VMEM)
    split = 2 if count > 1 else 1
    size = WIDTH // count
    width = 3 * 128
    whole = lambda shape: pl.BlockSpec(shape, lambda i: (0,) * len(shape))
    weight = lambda part: pl.BlockSpec((WIDTH, 128), lambda i: (0, 2 * part + pair))
    grads = [(count // split, 3 * size, 128)] * split + [(8, WIDTH)]
    return pl.pallas_call(
        partial(qkv_grad_kernel, count),
        grid=(1,),
        in_specs=[SMEM, whole(first_low.shape)]
        + [whole(value.shape) for value in raw]
        + [weight(0), weight(1), weight(2), whole(gains.shape)],
        out_specs=[whole(shape) for shape in grads],
        out_shape=[sds(shape) for shape in grads[:-1]] + [sds(grads[-1], f32)],
        scratch_shapes=[pltpu.VMEM((WIDTH, width), f32)],
        compiler_params=params(),
        cost_estimate=cost(6),
        name="project_grad",
    )(idx, first_low, *raw, w, w, w, gains)


def norm_one_kernel(x_ref, res_ref, own, core, far, g_ref, o_ref):
    xhat, inv_scale = normalize(x_ref[...].astype(f32))
    first = own[0].astype(f32) + core[0].astype(f32) + far[...].astype(f32)
    o_ref[...] = res_ref[...] + norm_back(first * g_ref[0:1], xhat, inv_scale)


def norm_one_call(x, res, own, core, far, gains, steps=2):
    rows = x.shape[0]
    block = pl.BlockSpec((rows // steps, WIDTH), lambda i: (i, 0))
    return pl.pallas_call(
        norm_one_kernel,
        grid=(steps,),
        in_specs=[
            block,
            block,
            pl.BlockSpec((1, rows // steps, WIDTH), lambda i: (0, i, 0)),
            pl.BlockSpec((1, rows // steps, WIDTH), lambda i: (0, i, 0)),
            block,
            pl.BlockSpec((8, WIDTH), lambda i: (0, 0)),
        ],
        out_specs=block,
        out_shape=sds(res.shape, f32),
        compiler_params=params(),
        cost_estimate=cost(3),
        name="norm_one_back",
    )(x, res, own, core, far, gains)


def swap(value, axis, bits):
    size = lax.axis_size(axis)
    return lax.ppermute(value, axis, [(place, place ^ bits) for place in range(size)])


def plus(left, right):
    return (left.astype(f32) + right.astype(f32)).astype(bf16)


def together(*values):
    return lax.optimization_barrier(values)


def per_device(inputs, attn_gain, qkv_weight, out_weight, mlp_gain, in_weight, mlp_out, cotangent):
    _, rows, width = inputs.shape
    shards = lax.axis_size("shard")
    eight = shards == 8
    count = 8 if eight else 1
    piece = width // shards
    seq, shard = lax.axis_index("seq"), lax.axis_index("shard")
    x_place, core = seq // 2, seq % 2
    owners = [jnp.bitwise_xor(lax.rem(shard + 8 - 2 * (r % 4), 8), r // 4) for r in range(8)]
    idx = jnp.stack([shard, seq, x_place, core, *owners]).astype(jnp.int32)

    order = jnp.bitwise_xor(seq, jnp.arange(4))
    places = (order[:, None] * rows + jnp.arange(rows)[None, :]).reshape(-1)
    frequency = 1.0 / rope_base ** (jnp.arange(0, HD, 2, dtype=f32) / HD)
    angles = places.astype(f32)[:, None] * jnp.tile(frequency, 4)[None, :]
    sign = jnp.where(jnp.arange(128) % HD < HD // 2, -1.0, 1.0)
    cosine, sine = jnp.cos(angles), jnp.sin(angles) * sign

    x0 = inputs[0]
    c0 = cotangent[0]
    w_qkv = lax.dynamic_slice_in_dim(qkv_weight, seq * COLS, COLS, 2)
    w_qkv = jnp.transpose(w_qkv, (1, 0, 2)).reshape(piece, 3 * COLS)
    w_in = in_weight.reshape(piece, 2, 2, HALF)
    w_in = lax.dynamic_index_in_dim(w_in, core, 2, keepdims=False)
    w_in = jnp.pad(w_in, ((0, 0), (0, 0), (0, PADDED - HALF)))
    w_mine = lax.dynamic_index_in_dim(w_in, x_place, 1, keepdims=False)
    w_other = lax.dynamic_index_in_dim(w_in, 1 - x_place, 1, keepdims=False)
    w_down = lax.dynamic_slice_in_dim(mlp_out, core * HALF, HALF, 0).T
    w_down = jnp.pad(w_down, ((0, 0), (0, PADDED - HALF)))

    x2 = swap(x0, "seq", 2)
    by_y = lambda value: swap(value, "shard", 1)
    by_z = lambda value: swap(value, "shard", 2)
    by_zz = lambda value: swap(value, "shard", 4)
    by_x = lambda value: swap(value, "seq", 2)
    by_core = lambda value: swap(value, "seq", 1)
    if eight:
        gain_rows = jnp.concatenate([attn_gain, mlp_gain, jnp.zeros(3 * COLS - 2 * piece, bf16)])[None]
        a0 = jnp.concatenate([w_qkv, jnp.pad(gain_rows, ((0, EXTRA - 1), (0, 0)))], axis=0)
        f0 = jnp.concatenate([w_mine, out_weight, w_down], axis=1)
        narrow = lambda value: value[..., :PADDED]
        ring = lambda value: lax.ppermute(
            value, "shard", [(place, (place + 2) % 8) for place in range(8)]
        )
        a4, a2, a1 = by_zz(a0), by_z(a0), by_y(a0)
        a4, a2, a1, x0, cosine, sine, idx, f0, w_other = together(
            a4, a2, a1, x0, cosine, sine, idx, f0, w_other
        )
        a6, a35 = by_z(a4), by_y(jnp.stack([a2, a4]))
        x1 = by_core(x0)
        a6, a35, x2 = together(a6, a35, x2)
        a7 = by_y(a6)
        x3 = by_core(x2)
        x3, x1, a7, f0 = together(x3, x1, a7, f0)
        f1, f4 = ring(f0), by_y(f0)
        c1 = by_core(c0)
        first_low, q, k, v, w_full, gains = qkv_call(
            count,
            idx,
            (x0, x1, x2, x3),
            (
                (a0, a1, a2, a4, a35, a6, a7),
                tuple((array, lead, 0) for array, lead in
                    ((0, None), (1, None), (2, None), (4, 0), (3, None), (4, 1), (5, None), (6, None))),
            ),
            None,
            cosine,
            sine,
        )
        q, f1, f4, c1 = together(q, f1, f4, c1)
        f2, f5 = ring(f1), by_y(f1)
        e14 = by_x(jnp.stack([narrow(f1), narrow(f4)]))
        ctx_fa, lse_fa = attend(q, k, v, 2)
        ctx_fa, q = together(ctx_fa, q)
        oth_a = by_x(ctx_fa)
        ctx_fb, lse_fb = attend(q, k, v, 3)
        ctx_fb, q, f2, f5, e14, oth_a = together(ctx_fb, q, f2, f5, e14, oth_a)
        oth_b = by_x(ctx_fb)
        f3, f6 = ring(f2), by_y(f2)
        e25 = by_x(jnp.stack([narrow(f2), narrow(f5)]))
        ctx_na, lse_na = attend(q, k, v, 0)
        ctx_na, q = together(ctx_na, q)
        ctx_nb, lse_nb = attend(q, k, v, 1)
        ctx_nb, f3, f6, e25, oth_b = together(ctx_nb, f3, f6, e25, oth_b)
        f7 = by_y(f3)
        e36 = by_x(jnp.stack([narrow(f3), narrow(f6)]))
        ctx_nb, f7 = together(ctx_nb, f7)
        e7 = by_x(narrow(f7))
        arrays = (f0, f1, f2, f3, f4, f5, f6, f7, w_other, e14, e25, e36, e7)
        mine_at = tuple((array, None, 0) for array in range(8))
        out_pieces = (arrays[:8], tuple((array, None, PADDED) for array in range(8)))
        down_at = tuple((array, None, PADDED + WIDTH) for array in range(8))
        other_at = tuple(
            (array, lead, 0)
            for array, lead in ((8, None), (9, 0), (10, 0), (11, 0), (9, 1), (10, 1), (11, 1), (12, None))
        )
    else:
        x1, x3 = by_core(x0), by_core(x2)
        gather = lambda value: lax.all_gather(value, "shard", axis=0, tiled=True)
        alone = ((0, None, 0),)
        first_low, q, k, v, w_full, gains = qkv_call(
            count,
            idx,
            (x0, x1, x2, x3),
            ((gather(w_qkv),), alone),
            jnp.stack([gather(attn_gain), gather(mlp_gain)]),
            cosine,
            sine,
        )
        arrays = (gather(w_mine), gather(w_down))
        arrays += (by_x(arrays[0]),)
        out_pieces = ((gather(out_weight),), alone)
        mine_at, down_at, other_at = alone, ((1, None, 0),), ((2, None, 0),)
        (ctx_fa, lse_fa), (ctx_fb, lse_fb) = attend(q, k, v, 2), attend(q, k, v, 3)
        oth_a, oth_b = by_x(ctx_fa), by_x(ctx_fb)
        c1 = by_core(c0)
        (ctx_na, lse_na), (ctx_nb, lse_nb) = attend(q, k, v, 0), attend(q, k, v, 1)

    near, far, other = (ctx_na, ctx_nb), (ctx_fa, ctx_fb), (oth_a, oth_b)
    lse_near, lse_far = (lse_na, lse_nb), (lse_fa, lse_fb)
    out_own, w_sel = out_call(count, idx, near, other, out_pieces)
    if eight:
        out_own, *last = together(out_own, *arrays)
        arrays = tuple(last)
    out_core = by_core(out_own)
    hidden, second_own, w_down_full, *wide = mlp_call(
        count, idx, x0, x1, out_own, out_core, c0, c1, gains, arrays, mine_at, other_at, down_at
    )
    second_core = by_core(second_own)
    down_other, down_mine, *down = down_call(count, idx, hidden, w_down_full, c0, c1)
    down_mine, second_core = together(down_mine, second_core)
    res, res_low, grad_near, grad_other, gain_two = norm_two_call(
        x0, x1, out_own, out_core, second_own, second_core, c0, c1, gains, w_sel
    )
    grad_far = by_x(grad_other)
    out_keep, out_send = out_grad_call(count, idx, near, other, res_low)
    part = lambda half, pair, grads, earlier=None: attend_back(
        half, pair, q, grads, (near, far)[half], (lse_near, lse_far)[half], k, v, cosine, sine, earlier
    )
    if eight:
        a_keep, a_send, b_keep, b_send = wide
        a_got, b_got = by_y(a_send), by_x(b_send)
        down_got = by_y(down[1])
        out_send, grad_near = together(out_send, grad_near)
        out_got = by_x(out_send)
        down_core = by_core(down_other)
    else:
        down_core = by_core(down_other)
    q_n0, dk0, dv0 = part(0, 0, grad_near)
    if eight:
        q_n0, grad_near, grad_far, down_core, a_got, b_got = together(
            q_n0, grad_near, grad_far, down_core, a_got, b_got
        )
        a_keep, a_got = plus(a_keep[0], a_got[0]), by_x(plus(a_keep[1], a_got[1]))
        b_keep, b_got = plus(b_keep[:4], b_got[:4]), by_y(plus(b_keep[4:], b_got[4:]))
    q_n1, dk1, dv1 = part(0, 1, grad_near)
    q_n1, grad_far = together(q_n1, grad_far)
    q_f0, k0, v0 = part(1, 0, grad_far, (dk0, dv0))
    if eight:
        q_f0, out_got, down_got, a_got, b_got, grad_far = together(
            q_f0, out_got, down_got, a_got, b_got, grad_far
        )
        both = lambda lo, hi: jnp.concatenate(
            [plus(a_keep[lo:hi], a_got[lo:hi]), plus(b_keep[lo:hi], b_got[lo:hi])], axis=-1
        )
        wide_next, wide_keep = by_z(both(2, 4)), both(0, 2)
        down_keep, down_got = plus(down[0][0], down_got[0]), by_x(plus(down[0][1], down_got[1]))
    raw0 = (q_n0, q_f0, k0, v0)
    *terms0, gain_a = qkv_grad_call(count, idx, first_low, raw0, w_full, gains, 0)
    if eight:
        terms0[0], terms0[1], grad_far = together(terms0[0], terms0[1], grad_far)
        out_next = by_y(jnp.concatenate([plus(out_keep[4:], out_got[4:]), terms0[1]], axis=1))
        out_keep = plus(out_keep[:4], out_got[:4])
    q_f1, k1, v1 = part(1, 1, grad_far, (dk1, dv1))
    if eight:
        q_f1, wide_next, out_next = together(q_f1, wide_next, out_next)
        wide_last, wide_keep = by_zz(plus(wide_keep[1], wide_next[1])), plus(wide_keep[0], wide_next[0])
    raw1 = (q_n1, q_f1, k1, v1)
    first_core = back_project((raw0, raw1), w_full, 1)
    first_got = by_core(first_core)
    if eight:
        first_core, q_f1 = together(first_core, q_f1)
    raw1 = (q_n1, q_f1, k1, v1)
    *terms1, gain_b = qkv_grad_call(count, idx, first_low, raw1, w_full, gains, 1)
    if eight:
        terms1[0], terms1[1], first_got, q_f1 = together(terms1[0], terms1[1], first_got, q_f1)
        terms1_got = by_y(terms1[1])
    raw1 = (q_n1, q_f1, k1, v1)
    first_own = back_project((raw0, raw1), w_full, 0)
    if eight:
        first_own, first_got = together(first_own, first_got)
    far_sum = plus(first_own[1], first_got[1])
    first_far = by_x(far_sum)
    gain_terms = jnp.concatenate([gain_a[:1] + gain_b[:1], gain_two[:1]], axis=0)
    final = lambda mine, got: mine.astype(f32) + got.astype(f32)
    crossed = (seq == 1) | (seq == 2)
    cross = [(1, 2), (2, 1)]
    if eight:
        first_own, far_sum, down_got, gain_terms = together(first_own, far_sum, down_got, gain_terms)
        rest = lambda lo, hi: jnp.concatenate(
            [
                plus(down_keep[lo:hi], down_got[lo:hi]),
                plus(out_keep[lo:hi], out_next[lo:hi, :COLS]),
                plus(terms0[0][lo:hi], out_next[lo:hi, COLS:]),
            ],
            axis=1,
        )
        rest_next, rest_keep = by_z(rest(2, 4)), rest(0, 2)
        gain_got = by_core(gain_terms)
        terms1_got, gain_got, down_core = together(terms1_got, gain_got, down_core)
        terms1_next = by_z(plus(terms1[0][2:], terms1_got[2:]))
        terms1_keep = plus(terms1[0][:2], terms1_got[:2])
        gain_terms = gain_terms + gain_got
        gain_got = by_y(gain_terms)
        result = (
            x0.astype(f32)
            + out_own[:rows].astype(f32)
            + out_core[rows:].astype(f32)
            + down_mine.astype(f32)
            + down_core.astype(f32)
        ).astype(bf16)[None]
        rest_next, wide_last, gain_got, result = together(rest_next, wide_last, gain_got, result)
        rest_last, rest_keep = plus(rest_keep[1], rest_next[1]), plus(rest_keep[0], rest_next[0])
        down_last, down_keep = rest_last[:BLOCK], rest_keep[:BLOCK]
        down_last = lax.ppermute(
            down_last,
            ("seq", "shard"),
            [(8 * j + i, 8 * (0, 2, 1, 3)[j] + (i ^ 4)) for j in range(4) for i in range(8)],
        )
        down_moved = lax.ppermute(down_keep, "seq", cross)
        rest_last, rest_keep = by_zz(rest_last[BLOCK:]), rest_keep[BLOCK:]
        gain_terms = gain_terms + gain_got
        gain_got = by_z(gain_terms)
        input_grad = norm_one_call(x0, res, first_own, first_got, first_far, gains)[None]
        terms1_next, gain_got, input_grad = together(terms1_next, gain_got, input_grad)
        terms1_last = by_zz(plus(terms1_keep[1], terms1_next[1]))
        terms1_keep = plus(terms1_keep[0], terms1_next[0])
        gain_terms = gain_terms + gain_got
        gain_terms = gain_terms + by_zz(gain_terms)
        gain_terms = gain_terms + by_x(gain_terms)
        wide_total = final(wide_keep, wide_last)
        rest_total = final(rest_keep, rest_last)
        down_total = final(jnp.where(crossed, down_moved, down_keep), down_last)
        out_total = rest_total[:COLS]
        totals = [rest_total[COLS:], final(terms1_keep, terms1_last)]
    else:
        input_grad = norm_one_call(x0, res, first_own, first_got, first_far, gains)[None]
        wide_sum = plus(wide[0][0, 0], by_x(wide[0][1, 0]))
        scatter = lambda value, dim: lax.psum_scatter(
            value, "shard", scatter_dimension=dim, tiled=True
        ).astype(f32)
        wide_total = scatter(wide_sum, 0)
        down_total = scatter(plus(down[0][0, 0], by_x(down[0][1, 0])), 1)
        moved = lax.ppermute(down_total.astype(bf16), "seq", cross).astype(f32)
        down_total = jnp.where(crossed, moved, down_total)
        out_total = scatter(plus(out_keep, by_x(out_send))[0], 1)
        totals = [scatter(terms[0].reshape(3, width, 128), 1) for terms in (terms0, terms1)]
        gain_terms = lax.psum(gain_terms, ("seq", "shard"))
        result = (
            x0.astype(f32)
            + out_own[:rows].astype(f32)
            + out_core[rows:].astype(f32)
            + down_mine.astype(f32)
            + down_core.astype(f32)
        ).astype(bf16)[None]
    take = width // (4 * shards)
    gain_out = lax.dynamic_slice_in_dim(gain_terms, (seq * shards + shard) * take, take, 1)
    qkv_out = jnp.concatenate([total.reshape(3, piece, 128) for total in totals], axis=2)
    return (
        result,
        input_grad,
        gain_out[0],
        qkv_out,
        out_total,
        gain_out[1],
        wide_total[:, :HALF],
        down_total,
    )


def solution(mesh):
    placed = (
        P("shard", "seq", None),
        P("shard"),
        P(None, "shard", None),
        P("shard", None),
        P("shard"),
        P("shard", None),
        P(None, "shard"),
        P("shard", "seq", None),
    )
    return jax.shard_map(
        per_device,
        mesh=mesh,
        in_specs=placed,
        out_specs=(
            P("shard", "seq", None),
            P("shard", "seq", None),
            P(("seq", "shard")),
            P(None, "shard", "seq"),
            P("seq", "shard"),
            P(("seq", "shard")),
            P("shard", "seq"),
            P("seq", "shard"),
        ),
        check_vma=False,
    )
```
